128 devices in a mesh: gy: 16 (over z, y_hi, core), gz: 8 (over y_lo, x).
Axes of the slice: x: 4, y: 4 (y_hi: 2, y_lo: 2; y = y_hi * 2 + y_lo), z: 4, core: 2. Of those that a mesh axis runs over, the one named last changes fastest.
Arguments:
- volume: bfloat16 [4, 128, 64, 256], P(None, 'gy', 'gz'), may hold values from -6 to 6
- block_weight: bfloat16 [3, 3, 3, 256, 256], replicated, may hold values from -0.078125 to 0.078125
- aspp_weight: bfloat16 [3, 3, 3, 3, 256, 128], replicated, may hold values from -0.078125 to 0.078125
- proj_weight: bfloat16 [384, 128], replicated, may hold values from -0.3125 to 0.3125
- cotangent: bfloat16 [4, 128, 64, 128], P(None, 'gy', 'gz'), may hold values from -6 to 6
Outputs:
- pyramid_out: bfloat16 [4, 128, 64, 128], P(None, 'gy', 'gz')
- grad_volume: bfloat16 [4, 128, 64, 256], P(None, 'gy', 'gz')
- grad_block: float32 [1769472], P(('gy', 'gz'))
- grad_aspp: float32 [2654208], P(('gy', 'gz'))
- grad_proj: float32 [49152], P(('gy', 'gz'))
The draws below stay inside these ranges and needn't reach their ends.
All inputs are finite; a program needn't handle non-finite values.
Results may differ from the reference program's by a relative error of at most 0.01.
Values may be sent and summed in bfloat16 or wider, within the bound.
No kernel may reach another device: no remote copies, remote signals or barrier semaphores. Data moves between devices by JAX's collectives and lax.ppermute only.
A program may use at most 192 MiB of HBM per device.

```python
import jax
import jax.numpy as jnp

C = 256
A = 128
X = 4
NY = 128
NZ = 64


def block_scale(key, dims, shards, least, high):
    gain, own = 1.0, jax.random.fold_in(key, 6)
    for axis_at, parts in shards:
        steps = jnp.exp(jax.random.uniform(jax.random.fold_in(own, axis_at), (parts,), jnp.float32, least / len(shards), high / len(shards)))
        gain = gain * jnp.repeat(steps, dims[axis_at] // parts).reshape([-1 if axis == axis_at else 1 for axis in range(len(dims))])
    return gain


def bell_draw(rng, extent, scale, bound, shards=(), kind=jnp.bfloat16):
    result = scale * jax.random.normal(rng, extent, jnp.float32)
    if shards:
        result = result * block_scale(rng, extent, shards, -0.22, 0.18)
    return jnp.clip(result, -bound, bound).astype(kind)


def setup_inputs(seed: int = 0) -> dict:
    key_of = jax.random.split(jax.random.key(seed), 6)
    return {
        "volume": bell_draw(key_of[0], (X, NY, NZ, C), 1.0, 6.0, ((1, 16), (2, 8))),
        "block_weight": bell_draw(key_of[1], (3, 3, 3, C, C), (27 * C) ** -0.5, 0.078125),
        "aspp_weight": bell_draw(key_of[2], (3, 3, 3, 3, C, A), (27 * C) ** -0.5, 0.078125),
        "proj_weight": bell_draw(key_of[3], (3 * A, A), (3 * A) ** -0.5, 0.3125),
        "cotangent": bell_draw(key_of[4], (X, NY, NZ, A), 1.0, 6.0, ((1, 16), (2, 8))),
    }


dilation_rates = (2, 4, 8)

def silu_slope(value):
    sigma = jax.nn.sigmoid(value)
    return sigma * (1.0 + value * (1.0 - sigma))

def tap_conv(padded, kernel, dilation):
    depth = padded.shape[0] - 2 * dilation
    rows = padded.shape[1] - 2 * dilation
    cols = padded.shape[2] - 2 * dilation
    in_width = padded.shape[3]
    out_width = kernel.shape[-1]
    total = jnp.zeros((depth * rows * cols, out_width), jnp.float32)
    for first in range(3):
        for second in range(3):
            for third in range(3):
                piece = padded[first * dilation:first * dilation + depth, second * dilation:second * dilation + rows, third * dilation:third * dilation + cols]
                total = total + jnp.dot(piece.reshape(-1, in_width), kernel[first, second, third], preferred_element_type=jnp.float32)
    return total.reshape(depth, rows, cols, out_width)

def weight_grad(padded, grad_out, dilation):
    depth, rows, cols, out_width = grad_out.shape
    in_width = padded.shape[3]
    grad_rows = grad_out.reshape(-1, out_width)
    taps = []
    for first in range(3):
        for second in range(3):
            for third in range(3):
                piece = padded[first * dilation:first * dilation + depth, second * dilation:second * dilation + rows, third * dilation:third * dilation + cols]
                taps.append(jnp.dot(piece.reshape(-1, in_width).T, grad_rows, preferred_element_type=jnp.float32))
    return jnp.stack(taps).reshape(3, 3, 3, in_width, out_width)

def flipped(kernel):
    return jnp.swapaxes(kernel[::-1, ::-1, ::-1], 3, 4)

def pad_all(source, dilation):
    return jnp.pad(source, ((dilation, dilation), (dilation, dilation), (dilation, dilation), (0, 0)))

def reference(volume, block_weight, aspp_weight, proj_weight, cotangent):
    volume_padded = pad_all(volume, 1)
    pre_block = tap_conv(volume_padded, block_weight, 1)
    hidden = jax.nn.silu(pre_block).astype(jnp.bfloat16)
    branch_list = []
    for branch, dilation in enumerate(dilation_rates):
        branch_list.append(tap_conv(pad_all(hidden, dilation), aspp_weight[branch], dilation))
    branch_pre = jnp.concatenate(branch_list, -1).reshape(-1, 3 * A)
    joined_rows = jax.nn.silu(branch_pre).astype(jnp.bfloat16)
    pyramid_out = jnp.dot(joined_rows, proj_weight, preferred_element_type=jnp.float32).reshape(X, NY, NZ, A).astype(jnp.bfloat16)
    grad_rows = cotangent.reshape(-1, A)
    grad_proj = jnp.dot(joined_rows.T, grad_rows, preferred_element_type=jnp.float32)
    proj_back = jnp.dot(grad_rows, proj_weight.T, preferred_element_type=jnp.float32)
    grad_joined = (proj_back * silu_slope(branch_pre)).astype(jnp.bfloat16).reshape(X, NY, NZ, 3 * A)
    grad_hidden = jnp.zeros((X, NY, NZ, C), jnp.float32)
    aspp_list = []
    for branch, dilation in enumerate(dilation_rates):
        grad_piece = grad_joined[..., branch * A:(branch + 1) * A]
        grad_hidden = grad_hidden + tap_conv(pad_all(grad_piece, dilation), flipped(aspp_weight[branch]), dilation)
        aspp_list.append(weight_grad(pad_all(hidden, dilation), grad_piece, dilation))
    grad_pre = (grad_hidden * silu_slope(pre_block)).astype(jnp.bfloat16)
    grad_volume = tap_conv(pad_all(grad_pre, 1), flipped(block_weight), 1).astype(jnp.bfloat16)
    grad_block = weight_grad(volume_padded, grad_pre, 1)
    return (pyramid_out, grad_volume, grad_block.reshape(-1), jnp.stack(aspp_list).reshape(-1), grad_proj.reshape(-1))
```

```python
import jax
import jax.numpy as jnp
from jax import lax
from jax.experimental import pallas as pl
from jax.experimental.pallas import tpu as pltpu
from jax.sharding import Mesh
from jax.sharding import PartitionSpec as P

ALL = ("z", "yh", "c", "yl", "x")
F32 = jnp.float32
BF16 = jnp.bfloat16
VLIM = 60 * 1024 * 1024
WHOLE = pl.BlockSpec(memory_space=pltpu.VMEM)
SCALAR = pl.BlockSpec(memory_space=pltpu.SMEM)


def z_pairs(odd):
    pairs = []
    for gy in range(16):
        for gz in range(8):
            other = ((gz - odd) ^ 1) + odd
            if 0 <= other < 8:
                pairs.append((gy * 8 + gz, gy * 8 + other))
    return pairs


def y_pairs(odd):
    pairs = []
    for gy in range(16):
        for gz in range(8):
            other = ((gy - odd) ^ 1) + odd
            if 0 <= other < 16:
                pairs.append((gy * 8 + gz, other * 8 + gz))
    return pairs


def swap(value, pairs):
    return lax.ppermute(value, ALL, pairs)


def sigmoid(v):
    return 1.0 / (1.0 + jnp.exp(-v))


def slope(v):
    s = sigmoid(v)
    return s * (1.0 + v * (1.0 - s))


def call(body, outs, specs, scratch=(), flops=10**9, nbytes=10**7):
    return pl.pallas_call(
        body,
        out_shape=outs,
        in_specs=specs,
        out_specs=jax.tree.map(lambda _: WHOLE, outs),
        scratch_shapes=list(scratch),
        compiler_params=pltpu.CompilerParams(vmem_limit_bytes=VLIM),
        cost_estimate=pl.CostEstimate(flops=flops, bytes_accessed=nbytes, transcendentals=0),
    )


def shape(dims, kind):
    return jax.ShapeDtypeStruct(dims, kind)


def fill_thin(ext, block, left, right, up, down):
    width = block.shape[-1]
    ext[:, 1:9, 8:16, :] = block[...].astype(F32).reshape(4, 8, 8, width)
    left_f = left[...].astype(F32)
    right_f = right[...].astype(F32)
    for x in range(4):
        for y in range(8):
            ext[x, 1 + y, 7:8, :] = left_f[8 * x + y : 8 * x + y + 1]
            ext[x, 1 + y, 16:17, :] = right_f[8 * x + y : 8 * x + y + 1]
    for row, strip in ((0, up), (9, down)):
        s = strip[...].astype(F32)
        for x in range(4):
            ext[x, row, 8:16, :] = s[16 * x : 16 * x + 8]
            ext[x, row, 7:8, :] = s[16 * x + 8 : 16 * x + 9]
            ext[x, row, 16:17, :] = s[16 * x + 9 : 16 * x + 10]


def conv_rows(step):
    spans = []
    for tap in range(3):
        move = step * (tap - 1)
        start = max(0, -move)
        count = 4 - abs(move)
        if count > 0:
            spans.append((tap, 64 * start, 64 * (start + move), 64 * count))
    return spans


def dot_nn(a, b):
    return lax.dot_general(a, b, (((1,), (0,)), ((), ())), preferred_element_type=F32)


def dot_nt(a, b):
    return lax.dot_general(a, b, (((1,), (1,)), ((), ())), preferred_element_type=F32)


def dot_tn(a, b):
    return lax.dot_general(a, b, (((0,), (0,)), ((), ())), preferred_element_type=F32)


def block_kernel(v, left, right, up, down, w, hidden, pre, cols, ext):
    fill_thin(ext, v, left, right, up, down)
    for b in range(3):
        for c in range(3):
            k = 3 * b + c
            cols[:, 256 * k : 256 * k + 256] = (
                ext[:, b : b + 8, 7 + c : 15 + c, :].reshape(256, 256).astype(BF16)
            )
    pre[...] = dot_nn(cols[...], w[1])
    for tap, out_row, in_row, rows in conv_rows(1):
        if tap != 1:
            pre[out_row : out_row + rows] += dot_nn(cols[in_row : in_row + rows], w[tap])
    value = pre[...]
    hidden[...] = (value * sigmoid(value)).astype(BF16)


def place(parity, own, z1, z2, y1, y2, grid):
    z_even, y_even = parity[0], parity[1]
    z_first = 2 * z_even
    z_second = 2 - z_first
    y_first = 2 * y_even
    y_second = 2 - y_first
    grid[1, 1] = own[...]
    grid[1, z_first] = z1[...]
    grid[1, z_second] = z2[...]
    for y_at, rows in ((y_first, y1), (y_second, y2)):
        grid[y_at, z_first] = rows[0]
        grid[y_at, 1] = rows[1]
        grid[y_at, z_second] = rows[2]


def fill_wide(ext, grid, lanes):
    width = ext.shape[-1]
    for yi, (src, dst, rows) in enumerate(((4, 0, 4), (0, 4, 8), (0, 12, 4))):
        for zi in range(3):
            part = grid[yi, zi, :, lanes : lanes + width].astype(F32).reshape(4, 8, 8, width)
            ext[:, dst : dst + rows, 8 * zi : 8 * zi + 8, :] = part[:, src : src + rows]


def branch_kernel(
    parity, own, z1, z2, y1, y2, w2, w4, w8, proj, cot,
    out, joint, gproj, cols2, cols4, cols8, grid, ext, pre,
):
    place(parity, own, z1, z2, y1, y2, grid)
    fill_wide(ext, grid, 0)
    for b in range(3):
        for c in range(3):
            k = 256 * (3 * b + c)
            cols8[:, k : k + 256] = grid[b, c]
            for rate, cols in ((2, cols2), (4, cols4)):
                y0 = 4 + rate * (b - 1)
                z0 = 8 + rate * (c - 1)
                cols[:, k : k + 256] = (
                    ext[:, y0 : y0 + 8, z0 : z0 + 8, :].reshape(256, 256).astype(BF16)
                )
    pre[:, 0:128] = dot_nn(cols2[...], w2[1])
    for tap, out_row, in_row, rows in conv_rows(2):
        if tap != 1:
            pre[out_row : out_row + rows, 0:128] += dot_nn(cols2[in_row : in_row + rows], w2[tap])
    pre[:, 128:256] = dot_nn(cols4[...], w4[...])
    pre[:, 256:384] = dot_nn(cols8[...], w8[...])
    value = pre[...]
    joined = (value * sigmoid(value)).astype(BF16)
    out[...] = dot_nn(joined, proj[...]).astype(BF16)
    gproj[...] = dot_tn(joined, cot[...])
    back = dot_nt(cot[...], proj[...])
    joint[...] = (back * slope(value)).astype(BF16)


def rows_at(ref, base, offset, rows):
    phase = offset % 8
    start = pl.multiple_of(base + (offset - phase), 8)
    length = rows + (8 if phase else 0)
    return ref[pl.ds(start, length), :][phase : phase + rows].astype(BF16)


def aspp_grad_kernel(core, cols2, cols4, cols8, joint, gproj, mine, theirs, sums, proj_rows):
    zeros = jnp.zeros((2304, 128), F32)
    for branch, cols in ((0, cols2), (1, cols4), (2, cols8)):
        grad = joint[:, 128 * branch : 128 * branch + 128]
        spans = conv_rows(2) if branch == 0 else conv_rows(4)
        done = set()
        for tap, out_row, in_row, rows in spans:
            at = (27 * branch + 9 * tap) * 256
            sums[at : at + 2304] = dot_tn(
                cols[in_row : in_row + rows, :], grad[out_row : out_row + rows]
            )
            done.add(tap)
        for tap in range(3):
            if tap not in done:
                at = (27 * branch + 9 * tap) * 256
                sums[at : at + 2304] = zeros
    sums[20736:20752] = jnp.zeros((16, 128), F32)
    proj_rows[0:384] = gproj[...]
    proj_rows[384:400] = jnp.zeros((16, 128), F32)
    me = core[0]

    def step(g, carry):
        for half in range(2):
            for e in range(8):
                u = 8 * half + e
                chunk = rows_at(sums, g * (16 * 162), 162 * u, 168)
                tail = rows_at(proj_rows, g * 48, 3 * u, 8)

                @pl.when(me == half)
                def _():
                    mine[g, e, 0:168] = chunk
                    mine[g, e, 168:176] = tail

                @pl.when(me != half)
                def _():
                    theirs[g, e, 0:168] = chunk
                    theirs[g, e, 168:176] = tail

        return carry

    lax.fori_loop(0, 8, step, 0)


def hidden_grad_kernel(parity, own, z1, z2, y1, y2, w2, w4, w8, pre, grad_pre, grid, ext, acc):
    place(parity, own, z1, z2, y1, y2, grid)
    acc[...] = jnp.zeros_like(acc)
    for branch, rate, w in ((0, 2, w2), (1, 4, w4), (2, 8, w8)):
        if rate < 8:
            fill_wide(ext, grid, 128 * branch)
        for b in range(3):
            for c in range(3):
                k = 256 * (3 * b + c)
                if rate < 8:
                    y0 = 4 - rate * (b - 1)
                    z0 = 8 - rate * (c - 1)
                    piece = ext[:, y0 : y0 + 8, z0 : z0 + 8, :].reshape(256, 128).astype(BF16)
                else:
                    piece = grid[2 - b, 2 - c, :, 256:384]
                if rate == 2:
                    for tap, in_row, out_row, rows in conv_rows(2):
                        acc[out_row : out_row + rows] += dot_nt(
                            piece[in_row : in_row + rows], w[tap, k : k + 256, :]
                        )
                else:
                    acc[...] += dot_nt(piece, w[k : k + 256, :])
    grad_pre[...] = (acc[...] * slope(pre[...])).astype(BF16)


def block_grad_kernel(core, cols, grad, mine, theirs, sums):
    for tap, out_row, in_row, rows in conv_rows(1):
        sums[2304 * tap : 2304 * tap + 2304] = dot_tn(
            cols[in_row : in_row + rows, :], grad[out_row : out_row + rows, :]
        )
    sums[6912:6928] = jnp.zeros((16, 256), F32)
    me = core[0]

    def step(g, carry):
        for half in range(2):
            for e in range(8):
                chunk = rows_at(sums, g * 864, 54 * (8 * half + e), 56)

                @pl.when(me == half)
                def _():
                    mine[g, e, 0:56] = chunk[:, 0:128]
                    mine[g, e, 56:112] = chunk[:, 128:256]

                @pl.when(me != half)
                def _():
                    theirs[g, e, 0:56] = chunk[:, 0:128]
                    theirs[g, e, 56:112] = chunk[:, 128:256]

        return carry

    lax.fori_loop(0, 8, step, 0)


def volume_grad_kernel(gp, left, right, up, down, w, grad, ext, acc):
    fill_thin(ext, gp, left, right, up, down)
    acc[...] = jnp.zeros_like(acc)
    for b in range(3):
        for c in range(3):
            k = 256 * (3 * b + c)
            piece = ext[:, 2 - b : 10 - b, 9 - c : 17 - c, :].reshape(256, 256).astype(BF16)
            for tap, in_row, out_row, rows in conv_rows(1):
                acc[out_row : out_row + rows] += dot_nt(
                    piece[in_row : in_row + rows], w[tap, k : k + 256, :]
                )
    grad[...] = acc[...].astype(BF16)


def thin_halo(block, z_even, y_even):
    width = block.shape[-1]
    cells = block.reshape(4, 8, 8, width)
    first, last = cells[:, :, 0], cells[:, :, 7]
    z1 = swap(jnp.where(z_even, last, first), z_pairs(0))
    z2 = swap(jnp.where(z_even, first, last), z_pairs(1))
    left = jnp.where(z_even, z2, z1)
    right = jnp.where(z_even, z1, z2)

    def strip(y):
        return jnp.concatenate(
            [
                cells[:, y],
                left[:, y : y + 1],
                right[:, y : y + 1],
                jnp.zeros((4, 6, width), block.dtype),
            ],
            axis=1,
        )

    top, bottom = strip(0), strip(7)
    y1 = swap(jnp.where(y_even, bottom, top), y_pairs(0))
    y2 = swap(jnp.where(y_even, top, bottom), y_pairs(1))
    up = jnp.where(y_even, y2, y1)
    down = jnp.where(y_even, y1, y2)
    return (
        left.reshape(32, width),
        right.reshape(32, width),
        up.reshape(64, width),
        down.reshape(64, width),
    )


def block_halo(block):
    z1 = swap(block, z_pairs(0))
    z2 = swap(block, z_pairs(1))
    row = jnp.stack([z1, block, z2])
    y1 = swap(row, y_pairs(0))
    y2 = swap(row, y_pairs(1))
    return z1, z2, y1, y2


def local(volume, block_weight, aspp_weight, proj_weight, cotangent):
    core = lax.axis_index("c")
    z_even = lax.axis_index("x") % 2 == 0
    y_even = core == 0
    parity = jnp.stack([z_even.astype(jnp.int32), y_even.astype(jnp.int32)])
    core = core.astype(jnp.int32).reshape(1)
    core_pairs = y_pairs(0)

    v = volume.reshape(256, 256)
    w = block_weight.reshape(3, 2304, 256)
    wa = aspp_weight.reshape(3, 3, 2304, 128)
    w2, w4, w8 = wa[0], wa[1, 1], wa[2, 1]
    cot = cotangent.reshape(256, 128)

    thin = thin_halo(v, z_even, y_even)
    hidden, pre, cols = call(
        block_kernel,
        (shape((256, 256), BF16), shape((256, 256), F32), shape((256, 2304), BF16)),
        [WHOLE] * 6,
        [pltpu.VMEM((4, 10, 24, 256), F32)],
    )(v, *thin, w)

    around = block_halo(hidden)
    wide = shape((256, 2304), BF16)
    out, joint, gproj, cols2, cols4, cols8 = call(
        branch_kernel,
        (shape((256, 128), BF16), shape((256, 384), BF16), shape((384, 128), F32), wide, wide, wide),
        [SCALAR] + [WHOLE] * 10,
        [
            pltpu.VMEM((3, 3, 256, 256), BF16),
            pltpu.VMEM((4, 16, 24, 256), F32),
            pltpu.VMEM((256, 384), F32),
        ],
    )(parity, hidden, *around, w2, w4, w8, proj_weight, cot)

    around = block_halo(joint)
    unit = shape((8, 8, 176, 128), BF16)
    aspp_mine, aspp_theirs = call(
        aspp_grad_kernel,
        (unit, unit),
        [SCALAR] + [WHOLE] * 5,
        [pltpu.VMEM((20752, 128), F32), pltpu.VMEM((400, 128), F32)],
    )(core, cols2, cols4, cols8, joint, gproj)
    aspp_other = swap(aspp_theirs, core_pairs)

    (grad_pre,) = call(
        hidden_grad_kernel,
        (shape((256, 256), BF16),),
        [SCALAR] + [WHOLE] * 9,
        [
            pltpu.VMEM((3, 3, 256, 384), BF16),
            pltpu.VMEM((4, 16, 24, 128), F32),
            pltpu.VMEM((256, 256), F32),
        ],
    )(parity, joint, *around, w2, w4, w8, pre)

    unit = shape((8, 8, 112, 128), BF16)
    block_mine, block_theirs = call(
        block_grad_kernel,
        (unit, unit),
        [SCALAR] + [WHOLE] * 2,
        [pltpu.VMEM((6928, 256), F32)],
    )(core, cols, grad_pre)
    block_other = swap(block_theirs, core_pairs)

    aspp_part = (aspp_mine.astype(F32) + aspp_other.astype(F32)).astype(BF16)
    block_part = (block_mine.astype(F32) + block_other.astype(F32)).astype(BF16)
    send = jnp.concatenate([aspp_part.reshape(64, 176, 128), block_part.reshape(64, 112, 128)], axis=1)
    got = lax.all_to_all(send, ("z", "yh", "yl", "x"), 0, 0, tiled=True)
    share = jnp.sum(got.astype(F32), axis=0)

    thin = thin_halo(grad_pre, z_even, y_even)
    (grad_volume,) = call(
        volume_grad_kernel,
        (shape((256, 256), BF16),),
        [WHOLE] * 6,
        [pltpu.VMEM((4, 10, 24, 256), F32), pltpu.VMEM((256, 256), F32)],
    )(grad_pre, *thin, w)

    aspp_share = share[0:162].reshape(20736)
    proj_share = share[168:171].reshape(384)
    block_share = jnp.concatenate([share[176:230], share[232:286]], axis=1).reshape(13824)
    return (
        out.reshape(4, 8, 8, 128),
        grad_volume.reshape(4, 8, 8, 256),
        block_share,
        aspp_share,
        proj_share,
    )


def solution(mesh):
    fine = Mesh(mesh.devices.reshape(4, 2, 2, 2, 4), ALL)
    cells = P(None, ("z", "yh", "c"), ("yl", "x"), None)
    flat = P(ALL)
    return jax.shard_map(
        local,
        mesh=fine,
        in_specs=(cells, P(), P(), P(), cells),
        out_specs=(cells, cells, flat, flat, flat),
        check_vma=False,
    )
```

```python
import jax
import jax.numpy as jnp
from jax import lax
from jax.experimental import pallas as pl
from jax.experimental.pallas import tpu as pltpu
from jax.sharding import Mesh
from jax.sharding import PartitionSpec as P

ALL = ("z", "yh", "c", "yl", "x")
F32 = jnp.float32
BF16 = jnp.bfloat16
VLIM = 60 * 1024 * 1024
WHOLE = pl.BlockSpec(memory_space=pltpu.VMEM)
SCALAR = pl.BlockSpec(memory_space=pltpu.SMEM)


def z_pairs(odd):
    pairs = []
    for gy in range(16):
        for gz in range(8):
            other = ((gz - odd) ^ 1) + odd
            if 0 <= other < 8:
                pairs.append((gy * 8 + gz, gy * 8 + other))
    return pairs


def y_pairs(odd):
    pairs = []
    for gy in range(16):
        for gz in range(8):
            other = ((gy - odd) ^ 1) + odd
            if 0 <= other < 16:
                pairs.append((gy * 8 + gz, other * 8 + gz))
    return pairs


def swap(value, pairs):
    return lax.ppermute(value, ALL, pairs)


def sigmoid(v):
    return 1.0 / (1.0 + jnp.exp(-v))


def slope(v):
    s = sigmoid(v)
    return s * (1.0 + v * (1.0 - s))


def call(body, outs, specs, scratch=(), flops=10**9, nbytes=10**7):
    return pl.pallas_call(
        body,
        out_shape=outs,
        in_specs=specs,
        out_specs=jax.tree.map(lambda _: WHOLE, outs),
        scratch_shapes=list(scratch),
        compiler_params=pltpu.CompilerParams(vmem_limit_bytes=VLIM),
        cost_estimate=pl.CostEstimate(flops=flops, bytes_accessed=nbytes, transcendentals=0),
    )


def shape(dims, kind):
    return jax.ShapeDtypeStruct(dims, kind)


def fill_thin(ext, block, left, right, up, down):
    width = block.shape[-1]
    ext[:, 1:9, 8:16, :] = block[...].astype(F32).reshape(4, 8, 8, width)
    left_f = left[...].astype(F32)
    right_f = right[...].astype(F32)
    for x in range(4):
        for y in range(8):
            ext[x, 1 + y, 7:8, :] = left_f[8 * x + y : 8 * x + y + 1]
            ext[x, 1 + y, 16:17, :] = right_f[8 * x + y : 8 * x + y + 1]
    for row, strip in ((0, up), (9, down)):
        s = strip[...].astype(F32)
        for x in range(4):
            ext[x, row, 8:16, :] = s[16 * x : 16 * x + 8]
            ext[x, row, 7:8, :] = s[16 * x + 8 : 16 * x + 9]
            ext[x, row, 16:17, :] = s[16 * x + 9 : 16 * x + 10]


def conv_rows(step):
    spans = []
    for tap in range(3):
        move = step * (tap - 1)
        start = max(0, -move)
        count = 4 - abs(move)
        if count > 0:
            spans.append((tap, 64 * start, 64 * (start + move), 64 * count))
    return spans


def dot_nn(a, b):
    return lax.dot_general(a, b, (((1,), (0,)), ((), ())), preferred_element_type=F32)


def dot_nt(a, b):
    return lax.dot_general(a, b, (((1,), (1,)), ((), ())), preferred_element_type=F32)


def dot_tn(a, b):
    return lax.dot_general(a, b, (((0,), (0,)), ((), ())), preferred_element_type=F32)


def block_kernel(v, left, right, up, down, w, hidden, pre, cols, ext):
    fill_thin(ext, v, left, right, up, down)
    for b in range(3):
        for c in range(3):
            k = 3 * b + c
            cols[:, 256 * k : 256 * k + 256] = (
                ext[:, b : b + 8, 7 + c : 15 + c, :].reshape(256, 256).astype(BF16)
            )
    pre[...] = dot_nn(cols[...], w[1])
    for tap, out_row, in_row, rows in conv_rows(1):
        if tap != 1:
            pre[out_row : out_row + rows] += dot_nn(cols[in_row : in_row + rows], w[tap])
    value = pre[...]
    hidden[...] = (value * sigmoid(value)).astype(BF16)


def place(parity, own, z1, z2, y1, y2, grid):
    z_even, y_even = parity[0], parity[1]
    z_first = 2 * z_even
    z_second = 2 - z_first
    y_first = 2 * y_even
    y_second = 2 - y_first
    grid[1, 1] = own[...]
    grid[1, z_first] = z1[...]
    grid[1, z_second] = z2[...]
    for y_at, rows in ((y_first, y1), (y_second, y2)):
        grid[y_at, z_first] = rows[0]
        grid[y_at, 1] = rows[1]
        grid[y_at, z_second] = rows[2]


def fill_wide(ext, grid, lanes):
    width = ext.shape[-1]
    for yi, (src, dst, rows) in enumerate(((4, 0, 4), (0, 4, 8), (0, 12, 4))):
        for zi in range(3):
            part = grid[yi, zi, :, lanes : lanes + width].astype(F32).reshape(4, 8, 8, width)
            ext[:, dst : dst + rows, 8 * zi : 8 * zi + 8, :] = part[:, src : src + rows]


def branch_kernel(
    parity, own, z1, z2, y1, y2, w2, w4, w8, proj, cot,
    out, joint, gproj, cols2, cols4, cols8, grid, ext, pre,
):
    place(parity, own, z1, z2, y1, y2, grid)
    fill_wide(ext, grid, 0)
    for b in range(3):
        for c in range(3):
            k = 256 * (3 * b + c)
            cols8[:, k : k + 256] = grid[b, c]
            for rate, cols in ((2, cols2), (4, cols4)):
                y0 = 4 + rate * (b - 1)
                z0 = 8 + rate * (c - 1)
                cols[:, k : k + 256] = (
                    ext[:, y0 : y0 + 8, z0 : z0 + 8, :].reshape(256, 256).astype(BF16)
                )
    pre[:, 0:128] = dot_nn(cols2[...], w2[1])
    for tap, out_row, in_row, rows in conv_rows(2):
        if tap != 1:
            pre[out_row : out_row + rows, 0:128] += dot_nn(cols2[in_row : in_row + rows], w2[tap])
    pre[:, 128:256] = dot_nn(cols4[...], w4[...])
    pre[:, 256:384] = dot_nn(cols8[...], w8[...])
    value = pre[...]
    joined = (value * sigmoid(value)).astype(BF16)
    out[...] = dot_nn(joined, proj[...]).astype(BF16)
    gproj[...] = dot_tn(joined, cot[...])
    back = dot_nt(cot[...], proj[...])
    joint[...] = (back * slope(value)).astype(BF16)


def rows_at(ref, base, offset, rows):
    phase = offset % 8
    start = pl.multiple_of(base + (offset - phase), 8)
    length = rows + (8 if phase else 0)
    return ref[pl.ds(start, length), :][phase : phase + rows].astype(BF16)


def aspp_grad_kernel(core, cols2, cols4, cols8, joint, gproj, mine, theirs, sums, proj_rows):
    zeros = jnp.zeros((2304, 128), F32)
    for branch, cols in ((0, cols2), (1, cols4), (2, cols8)):
        grad = joint[:, 128 * branch : 128 * branch + 128]
        spans = conv_rows(2) if branch == 0 else conv_rows(4)
        done = set()
        for tap, out_row, in_row, rows in spans:
            at = (27 * branch + 9 * tap) * 256
            sums[at : at + 2304] = dot_tn(
                cols[in_row : in_row + rows, :], grad[out_row : out_row + rows]
            )
            done.add(tap)
        for tap in range(3):
            if tap not in done:
                at = (27 * branch + 9 * tap) * 256
                sums[at : at + 2304] = zeros
    sums[20736:20752] = jnp.zeros((16, 128), F32)
    proj_rows[0:384] = gproj[...]
    proj_rows[384:400] = jnp.zeros((16, 128), F32)
    me = core[0]

    def step(g, carry):
        for half in range(2):
            for e in range(8):
                u = 8 * half + e
                chunk = rows_at(sums, g * (16 * 162), 162 * u, 168)
                tail = rows_at(proj_rows, g * 48, 3 * u, 8)

                @pl.when(me == half)
                def _():
                    mine[g, e, 0:168] = chunk
                    mine[g, e, 168:176] = tail

                @pl.when(me != half)
                def _():
                    theirs[g, e, 0:168] = chunk
                    theirs[g, e, 168:176] = tail

        return carry

    lax.fori_loop(0, 8, step, 0)


def hidden_grad_kernel(parity, own, z1, z2, y1, y2, w2, w4, w8, pre, grad_pre, grid, ext, acc):
    place(parity, own, z1, z2, y1, y2, grid)
    acc[...] = jnp.zeros_like(acc)
    for branch, rate, w in ((0, 2, w2), (1, 4, w4), (2, 8, w8)):
        if rate < 8:
            fill_wide(ext, grid, 128 * branch)
        for b in range(3):
            for c in range(3):
                k = 256 * (3 * b + c)
                if rate < 8:
                    y0 = 4 - rate * (b - 1)
                    z0 = 8 - rate * (c - 1)
                    piece = ext[:, y0 : y0 + 8, z0 : z0 + 8, :].reshape(256, 128).astype(BF16)
                else:
                    piece = grid[2 - b, 2 - c, :, 256:384]
                if rate == 2:
                    for tap, in_row, out_row, rows in conv_rows(2):
                        acc[out_row : out_row + rows] += dot_nt(
                            piece[in_row : in_row + rows], w[tap, k : k + 256, :]
                        )
                else:
                    acc[...] += dot_nt(piece, w[k : k + 256, :])
    grad_pre[...] = (acc[...] * slope(pre[...])).astype(BF16)


def block_grad_kernel(core, cols, grad, mine, theirs, sums):
    for tap, out_row, in_row, rows in conv_rows(1):
        sums[2304 * tap : 2304 * tap + 2304] = dot_tn(
            cols[in_row : in_row + rows, :], grad[out_row : out_row + rows, :]
        )
    sums[6912:6928] = jnp.zeros((16, 256), F32)
    me = core[0]

    def step(g, carry):
        for half in range(2):
            for e in range(8):
                chunk = rows_at(sums, g * 864, 54 * (8 * half + e), 56)

                @pl.when(me == half)
                def _():
                    mine[g, e, 0:56] = chunk[:, 0:128]
                    mine[g, e, 56:112] = chunk[:, 128:256]

                @pl.when(me != half)
                def _():
                    theirs[g, e, 0:56] = chunk[:, 0:128]
                    theirs[g, e, 56:112] = chunk[:, 128:256]

        return carry

    lax.fori_loop(0, 8, step, 0)


def volume_grad_kernel(gp, left, right, up, down, w, grad, ext, acc):
    fill_thin(ext, gp, left, right, up, down)
    acc[...] = jnp.zeros_like(acc)
    for b in range(3):
        for c in range(3):
            k = 256 * (3 * b + c)
            piece = ext[:, 2 - b : 10 - b, 9 - c : 17 - c, :].reshape(256, 256).astype(BF16)
            for tap, in_row, out_row, rows in conv_rows(1):
                acc[out_row : out_row + rows] += dot_nt(
                    piece[in_row : in_row + rows], w[tap, k : k + 256, :]
                )
    grad[...] = acc[...].astype(BF16)


def thin_halo(block, z_even, y_even):
    width = block.shape[-1]
    cells = block.reshape(4, 8, 8, width)
    first, last = cells[:, :, 0], cells[:, :, 7]
    z1 = swap(jnp.where(z_even, last, first), z_pairs(0))
    z2 = swap(jnp.where(z_even, first, last), z_pairs(1))
    left = jnp.where(z_even, z2, z1)
    right = jnp.where(z_even, z1, z2)

    def strip(y):
        return jnp.concatenate(
            [
                cells[:, y],
                left[:, y : y + 1],
                right[:, y : y + 1],
                jnp.zeros((4, 6, width), block.dtype),
            ],
            axis=1,
        )

    top, bottom = strip(0), strip(7)
    y1 = swap(jnp.where(y_even, bottom, top), y_pairs(0))
    y2 = swap(jnp.where(y_even, top, bottom), y_pairs(1))
    up = jnp.where(y_even, y2, y1)
    down = jnp.where(y_even, y1, y2)
    return (
        left.reshape(32, width),
        right.reshape(32, width),
        up.reshape(64, width),
        down.reshape(64, width),
    )


def block_halo(block):
    z1 = swap(block, z_pairs(0))
    z2 = swap(block, z_pairs(1))
    row = jnp.stack([z1, block, z2])
    y1 = swap(row, y_pairs(0))
    y2 = swap(row, y_pairs(1))
    return z1, z2, y1, y2


def to_owners(chunks):
    return lax.all_to_all(chunks, ("z", "yh", "yl", "x"), 0, 0, tiled=True)


def step(volume, block_weight, aspp_weight, proj_weight, cotangent):
    core = lax.axis_index("c")
    z_even = lax.axis_index("x") % 2 == 0
    y_even = core == 0
    parity = jnp.stack([z_even.astype(jnp.int32), y_even.astype(jnp.int32)])
    core = core.astype(jnp.int32).reshape(1)
    core_pairs = y_pairs(0)

    v = volume.reshape(256, 256)
    w = block_weight.reshape(3, 2304, 256)
    wa = aspp_weight.reshape(3, 3, 2304, 128)
    w2, w4, w8 = wa[0], wa[1, 1], wa[2, 1]
    cot = cotangent.reshape(256, 128)

    thin = thin_halo(v, z_even, y_even)
    hidden, pre, cols = call(
        block_kernel,
        (shape((256, 256), BF16), shape((256, 256), F32), shape((256, 2304), BF16)),
        [WHOLE] * 6,
        [pltpu.VMEM((4, 10, 24, 256), F32)],
    )(v, *thin, w)

    around = block_halo(hidden)
    wide = shape((256, 2304), BF16)
    out, joint, gproj, cols2, cols4, cols8 = call(
        branch_kernel,
        (shape((256, 128), BF16), shape((256, 384), BF16), shape((384, 128), F32), wide, wide, wide),
        [SCALAR] + [WHOLE] * 10,
        [
            pltpu.VMEM((3, 3, 256, 256), BF16),
            pltpu.VMEM((4, 16, 24, 256), F32),
            pltpu.VMEM((256, 384), F32),
        ],
    )(parity, hidden, *around, w2, w4, w8, proj_weight, cot)

    around = block_halo(joint)
    unit = shape((8, 8, 176, 128), BF16)
    aspp_mine, aspp_theirs = call(
        aspp_grad_kernel,
        (unit, unit),
        [SCALAR] + [WHOLE] * 5,
        [pltpu.VMEM((20752, 128), F32), pltpu.VMEM((400, 128), F32)],
    )(core, cols2, cols4, cols8, joint, gproj)
    aspp_other = swap(aspp_theirs, core_pairs)
    aspp_part = (aspp_mine.astype(F32) + aspp_other.astype(F32)).astype(BF16)
    aspp_got = to_owners(aspp_part.reshape(64, 176, 128))

    (grad_pre,) = call(
        hidden_grad_kernel,
        (shape((256, 256), BF16),),
        [SCALAR] + [WHOLE] * 9,
        [
            pltpu.VMEM((3, 3, 256, 384), BF16),
            pltpu.VMEM((4, 16, 24, 128), F32),
            pltpu.VMEM((256, 256), F32),
        ],
    )(parity, joint, *around, w2, w4, w8, pre)

    unit = shape((8, 8, 112, 128), BF16)
    block_mine, block_theirs = call(
        block_grad_kernel,
        (unit, unit),
        [SCALAR] + [WHOLE] * 2,
        [pltpu.VMEM((6928, 256), F32)],
    )(core, cols, grad_pre)
    block_other = swap(block_theirs, core_pairs)

    block_part = (block_mine.astype(F32) + block_other.astype(F32)).astype(BF16)
    block_got = to_owners(block_part.reshape(64, 112, 128))

    thin = thin_halo(grad_pre, z_even, y_even)
    (grad_volume,) = call(
        volume_grad_kernel,
        (shape((256, 256), BF16),),
        [WHOLE] * 6,
        [pltpu.VMEM((4, 10, 24, 256), F32), pltpu.VMEM((256, 256), F32)],
    )(grad_pre, *thin, w)

    share = jnp.sum(aspp_got.astype(F32), axis=0)
    aspp_share = share[0:162].reshape(20736)
    proj_share = share[168:171].reshape(384)
    share = jnp.sum(block_got.astype(F32), axis=0)
    block_share = jnp.concatenate([share[0:54], share[56:110]], axis=1).reshape(13824)
    return (
        out.reshape(4, 8, 8, 128),
        grad_volume.reshape(4, 8, 8, 256),
        block_share,
        aspp_share,
        proj_share,
    )


def solution(mesh):
    fine = Mesh(mesh.devices.reshape(4, 2, 2, 2, 4), ALL)
    cells = P(None, ("z", "yh", "c"), ("yl", "x"), None)
    flat = P(ALL)
    return jax.shard_map(
        step,
        mesh=fine,
        in_specs=(cells, P(), P(), P(), cells),
        out_specs=(cells, cells, flat, flat, flat),
        check_vma=False,
    )
```

```python
import jax
import jax.numpy as jnp
from jax import lax
from jax.experimental import pallas as pl
from jax.experimental.pallas import tpu as pltpu
from jax.sharding import Mesh
from jax.sharding import PartitionSpec as P

ALL = ("z", "yh", "c", "yl", "x")
F32 = jnp.float32
BF16 = jnp.bfloat16
VLIM = 60 * 1024 * 1024
WHOLE = pl.BlockSpec(memory_space=pltpu.VMEM)
SCALAR = pl.BlockSpec(memory_space=pltpu.SMEM)


def z_pairs(odd):
    pairs = []
    for gy in range(16):
        for gz in range(8):
            other = ((gz - odd) ^ 1) + odd
            if 0 <= other < 8:
                pairs.append((gy * 8 + gz, gy * 8 + other))
    return pairs


def y_pairs(odd):
    pairs = []
    for gy in range(16):
        for gz in range(8):
            other = ((gy - odd) ^ 1) + odd
            if 0 <= other < 16:
                pairs.append((gy * 8 + gz, other * 8 + gz))
    return pairs


def swap(value, pairs):
    return lax.ppermute(value, ALL, pairs)


def sigmoid(v):
    return 1.0 / (1.0 + jnp.exp(-v))


def slope(v):
    s = sigmoid(v)
    return s * (1.0 + v * (1.0 - s))


def call(body, outs, specs, scratch=(), flops=10**9, nbytes=10**7):
    return pl.pallas_call(
        body,
        out_shape=outs,
        in_specs=specs,
        out_specs=jax.tree.map(lambda _: WHOLE, outs),
        scratch_shapes=list(scratch),
        compiler_params=pltpu.CompilerParams(vmem_limit_bytes=VLIM),
        cost_estimate=pl.CostEstimate(flops=flops, bytes_accessed=nbytes, transcendentals=0),
    )


def shape(dims, kind):
    return jax.ShapeDtypeStruct(dims, kind)


def fill_thin(ext, block, left, right, up, down):
    width = block.shape[-1]
    ext[:, 1:9, 8:16, :] = block[...].astype(F32).reshape(4, 8, 8, width)
    left_f = left[...].astype(F32)
    right_f = right[...].astype(F32)
    for x in range(4):
        for y in range(8):
            ext[x, 1 + y, 7:8, :] = left_f[8 * x + y : 8 * x + y + 1]
            ext[x, 1 + y, 16:17, :] = right_f[8 * x + y : 8 * x + y + 1]
    for row, strip in ((0, up), (9, down)):
        s = strip[...].astype(F32)
        for x in range(4):
            ext[x, row, 8:16, :] = s[16 * x : 16 * x + 8]
            ext[x, row, 7:8, :] = s[16 * x + 8 : 16 * x + 9]
            ext[x, row, 16:17, :] = s[16 * x + 9 : 16 * x + 10]


def conv_rows(step):
    spans = []
    for tap in range(3):
        move = step * (tap - 1)
        start = max(0, -move)
        count = 4 - abs(move)
        if count > 0:
            spans.append((tap, 64 * start, 64 * (start + move), 64 * count))
    return spans


def dot_nn(a, b):
    return lax.dot_general(a, b, (((1,), (0,)), ((), ())), preferred_element_type=F32)


def dot_nt(a, b):
    return lax.dot_general(a, b, (((1,), (1,)), ((), ())), preferred_element_type=F32)


def dot_tn(a, b):
    return lax.dot_general(a, b, (((0,), (0,)), ((), ())), preferred_element_type=F32)


def block_kernel(v, left, right, up, down, w, hidden, pre, cols, ext):
    fill_thin(ext, v, left, right, up, down)
    for b in range(3):
        for c in range(3):
            k = 3 * b + c
            cols[:, 256 * k : 256 * k + 256] = (
                ext[:, b : b + 8, 7 + c : 15 + c, :].reshape(256, 256).astype(BF16)
            )
    pre[...] = dot_nn(cols[...], w[1])
    for tap, out_row, in_row, rows in conv_rows(1):
        if tap != 1:
            pre[out_row : out_row + rows] += dot_nn(cols[in_row : in_row + rows], w[tap])
    value = pre[...]
    hidden[...] = (value * sigmoid(value)).astype(BF16)


def place(parity, own, z1, z2, y1, y2, grid):
    z_even, y_even = parity[0], parity[1]
    z_first = 2 * z_even
    z_second = 2 - z_first
    y_first = 2 * y_even
    y_second = 2 - y_first
    grid[1, 1] = own[...]
    grid[1, z_first] = z1[...]
    grid[1, z_second] = z2[...]
    for y_at, rows in ((y_first, y1), (y_second, y2)):
        grid[y_at, z_first] = rows[0]
        grid[y_at, 1] = rows[1]
        grid[y_at, z_second] = rows[2]


def fill_wide(ext, grid, lanes):
    width = ext.shape[-1]
    for yi, (src, dst, rows) in enumerate(((4, 0, 4), (0, 4, 8), (0, 12, 4))):
        for zi in range(3):
            part = grid[yi, zi, :, lanes : lanes + width].astype(F32).reshape(4, 8, 8, width)
            ext[:, dst : dst + rows, 8 * zi : 8 * zi + 8, :] = part[:, src : src + rows]


def branch_kernel(
    parity, own, z1, z2, y1, y2, w2, w4, w8, proj, cot,
    out, joint, gproj, cols2, cols4, cols8, grid, ext, pre,
):
    place(parity, own, z1, z2, y1, y2, grid)
    fill_wide(ext, grid, 0)
    for b in range(3):
        for c in range(3):
            k = 256 * (3 * b + c)
            cols8[:, k : k + 256] = grid[b, c]
            for rate, cols in ((2, cols2), (4, cols4)):
                y0 = 4 + rate * (b - 1)
                z0 = 8 + rate * (c - 1)
                cols[:, k : k + 256] = (
                    ext[:, y0 : y0 + 8, z0 : z0 + 8, :].reshape(256, 256).astype(BF16)
                )
    pre[:, 0:128] = dot_nn(cols2[...], w2[1])
    for tap, out_row, in_row, rows in conv_rows(2):
        if tap != 1:
            pre[out_row : out_row + rows, 0:128] += dot_nn(cols2[in_row : in_row + rows], w2[tap])
    pre[:, 128:256] = dot_nn(cols4[...], w4[...])
    pre[:, 256:384] = dot_nn(cols8[...], w8[...])
    value = pre[...]
    joined = (value * sigmoid(value)).astype(BF16)
    out[...] = dot_nn(joined, proj[...]).astype(BF16)
    gproj[...] = dot_tn(joined, cot[...])
    back = dot_nt(cot[...], proj[...])
    joint[...] = (back * slope(value)).astype(BF16)


def vanishing(row):
    tap = row // 256
    return tap >= 27 and (tap % 27) // 9 != 1


def share_plan():
    starts, forwards = [], ([], [])
    owners = []
    for c in range(2):
        device = [16 * (h // 8) + 8 * c + h % 8 for h in range(64)]
        full = [h for h in range(64) if not all(vanishing(162 * device[h] + r) for r in range(162))]
        spare = [h for h in range(64) if h not in full]
        slots = [[None, None] for _ in range(64)]
        for h in full:
            slots[h] = [162 * device[h], 162 * device[h] + 54]
            owners.append(device[h])
        for i, h in enumerate(full):
            slot, helper = divmod(i, len(spare))
            slots[spare[helper]][slot] = 162 * device[h] + 108
            forwards[slot].append((device[spare[helper]], device[h]))
        starts.append(slots)
    return starts, forwards, owners


SLOTS, FORWARDS, OWNERS = share_plan()


def aspp_grad_kernel(core, cols2, cols4, cols8, joint, gproj, mine, theirs, sums, proj_rows):
    for branch, cols in ((0, cols2), (1, cols4), (2, cols8)):
        grad = joint[:, 128 * branch : 128 * branch + 128]
        for tap, out_row, in_row, rows in conv_rows(2 if branch == 0 else 4):
            at = (27 * branch + 9 * tap) * 256
            sums[at : at + 2304] = dot_tn(
                cols[in_row : in_row + rows, :], grad[out_row : out_row + rows]
            )
    for unit in OWNERS:
        for row in range(162 * unit // 8 * 8, 162 * unit + 168, 8):
            if vanishing(row):
                sums[row : row + 8] = jnp.zeros((8, 128), F32)
    proj_rows[0:384] = gproj[...]
    proj_rows[384:400] = jnp.zeros((16, 128), F32)

    def pack(target, c):
        for h in range(64):
            for slot in range(2):
                start = SLOTS[c][h][slot]
                if start is None:
                    piece = jnp.zeros((56, 128), BF16)
                else:
                    piece = sums[start : start + 56].astype(BF16)
                target[h, 56 * slot : 56 * slot + 56] = piece
            at = 3 * (16 * (h // 8) + 8 * c + h % 8)
            target[h, 112:120] = proj_rows[at : at + 8].astype(BF16)

    for me in range(2):

        @pl.when(core[0] == me)
        def _():
            pack(mine, me)
            pack(theirs, 1 - me)


def rows_at(ref, base, offset, rows):
    phase = offset % 8
    start = pl.multiple_of(base + (offset - phase), 8)
    length = rows + (8 if phase else 0)
    return ref[pl.ds(start, length), :][phase : phase + rows].astype(BF16)


def hidden_grad_kernel(parity, own, z1, z2, y1, y2, w2, w4, w8, pre, grad_pre, grid, ext, acc):
    place(parity, own, z1, z2, y1, y2, grid)
    acc[...] = jnp.zeros_like(acc)
    for branch, rate, w in ((0, 2, w2), (1, 4, w4), (2, 8, w8)):
        if rate < 8:
            fill_wide(ext, grid, 128 * branch)
        for b in range(3):
            for c in range(3):
                k = 256 * (3 * b + c)
                if rate < 8:
                    y0 = 4 - rate * (b - 1)
                    z0 = 8 - rate * (c - 1)
                    piece = ext[:, y0 : y0 + 8, z0 : z0 + 8, :].reshape(256, 128).astype(BF16)
                else:
                    piece = grid[2 - b, 2 - c, :, 256:384]
                if rate == 2:
                    for tap, in_row, out_row, rows in conv_rows(2):
                        acc[out_row : out_row + rows] += dot_nt(
                            piece[in_row : in_row + rows], w[tap, k : k + 256, :]
                        )
                else:
                    acc[...] += dot_nt(piece, w[k : k + 256, :])
    grad_pre[...] = (acc[...] * slope(pre[...])).astype(BF16)


def block_grad_kernel(core, cols, grad, mine, theirs, sums):
    for tap, out_row, in_row, rows in conv_rows(1):
        sums[2304 * tap : 2304 * tap + 2304] = dot_tn(
            cols[in_row : in_row + rows, :], grad[out_row : out_row + rows, :]
        )
    sums[6912:6928] = jnp.zeros((16, 256), F32)
    me = core[0]

    def step(g, carry):
        for half in range(2):
            for e in range(8):
                chunk = rows_at(sums, g * 864, 54 * (8 * half + e), 56)

                @pl.when(me == half)
                def _():
                    mine[g, e, 0:56] = chunk[:, 0:128]
                    mine[g, e, 56:112] = chunk[:, 128:256]

                @pl.when(me != half)
                def _():
                    theirs[g, e, 0:56] = chunk[:, 0:128]
                    theirs[g, e, 56:112] = chunk[:, 128:256]

        return carry

    lax.fori_loop(0, 8, step, 0)


def volume_grad_kernel(gp, left, right, up, down, w, grad, ext, acc):
    fill_thin(ext, gp, left, right, up, down)
    acc[...] = jnp.zeros_like(acc)
    for b in range(3):
        for c in range(3):
            k = 256 * (3 * b + c)
            piece = ext[:, 2 - b : 10 - b, 9 - c : 17 - c, :].reshape(256, 256).astype(BF16)
            for tap, in_row, out_row, rows in conv_rows(1):
                acc[out_row : out_row + rows] += dot_nt(
                    piece[in_row : in_row + rows], w[tap, k : k + 256, :]
                )
    grad[...] = acc[...].astype(BF16)


def thin_halo(block, z_even, y_even):
    width = block.shape[-1]
    cells = block.reshape(4, 8, 8, width)
    first, last = cells[:, :, 0], cells[:, :, 7]
    z1 = jnp.where(z_even, last, first)
    z2 = jnp.where(z_even, first, last)
    z1 = swap(z1, z_pairs(0))
    z2 = swap(z2, z_pairs(1))
    left = jnp.where(z_even, z2, z1)
    right = jnp.where(z_even, z1, z2)

    def strip(y):
        return jnp.concatenate(
            [
                cells[:, y],
                left[:, y : y + 1],
                right[:, y : y + 1],
                jnp.zeros((4, 6, width), block.dtype),
            ],
            axis=1,
        )

    top, bottom = strip(0), strip(7)
    y1 = jnp.where(y_even, bottom, top)
    y2 = jnp.where(y_even, top, bottom)
    y1 = swap(y1, y_pairs(0))
    y2 = swap(y2, y_pairs(1))
    up = jnp.where(y_even, y2, y1)
    down = jnp.where(y_even, y1, y2)
    return (
        left.reshape(32, width),
        right.reshape(32, width),
        up.reshape(64, width),
        down.reshape(64, width),
    )


def block_halo(block):
    z1 = swap(block, z_pairs(0))
    z2 = swap(block, z_pairs(1))
    row = jnp.stack([z1, block, z2])
    y1 = swap(row, y_pairs(0))
    y2 = swap(row, y_pairs(1))
    return z1, z2, y1, y2


def to_owners(chunks):
    return lax.all_to_all(chunks, ("z", "yh", "yl", "x"), 0, 0, tiled=True)


def step(volume, block_weight, aspp_weight, proj_weight, cotangent):
    core = lax.axis_index("c")
    z_even = lax.axis_index("x") % 2 == 0
    y_even = core == 0
    parity = jnp.stack([z_even.astype(jnp.int32), y_even.astype(jnp.int32)])
    core = core.astype(jnp.int32).reshape(1)
    core_pairs = y_pairs(0)

    v = volume.reshape(256, 256)
    w = block_weight.reshape(3, 2304, 256)
    wa = aspp_weight.reshape(3, 3, 2304, 128)
    w2, w4, w8 = wa[0], wa[1, 1], wa[2, 1]
    cot = cotangent.reshape(256, 128)

    thin = thin_halo(v, z_even, y_even)
    hidden, pre, cols = call(
        block_kernel,
        (shape((256, 256), BF16), shape((256, 256), F32), shape((256, 2304), BF16)),
        [WHOLE] * 6,
        [pltpu.VMEM((4, 10, 24, 256), F32)],
    )(v, *thin, w)

    around = block_halo(hidden)
    wide = shape((256, 2304), BF16)
    out, joint, gproj, cols2, cols4, cols8 = call(
        branch_kernel,
        (shape((256, 128), BF16), shape((256, 384), BF16), shape((384, 128), F32), wide, wide, wide),
        [SCALAR] + [WHOLE] * 10,
        [
            pltpu.VMEM((3, 3, 256, 256), BF16),
            pltpu.VMEM((4, 16, 24, 256), F32),
            pltpu.VMEM((256, 384), F32),
        ],
    )(parity, hidden, *around, w2, w4, w8, proj_weight, cot)

    around = block_halo(joint)
    unit = shape((64, 120, 128), BF16)
    aspp_mine, aspp_theirs = call(
        aspp_grad_kernel,
        (unit, unit),
        [SCALAR] + [WHOLE] * 5,
        [pltpu.VMEM((20752, 128), F32), pltpu.VMEM((400, 128), F32)],
    )(core, cols2, cols4, cols8, joint, gproj)
    aspp_other = swap(aspp_theirs, core_pairs)
    aspp_part = (aspp_mine.astype(F32) + aspp_other.astype(F32)).astype(BF16)
    aspp_got = to_owners(aspp_part)

    (grad_pre,) = call(
        hidden_grad_kernel,
        (shape((256, 256), BF16),),
        [SCALAR] + [WHOLE] * 9,
        [
            pltpu.VMEM((3, 3, 256, 384), BF16),
            pltpu.VMEM((4, 16, 24, 128), F32),
            pltpu.VMEM((256, 256), F32),
        ],
    )(parity, joint, *around, w2, w4, w8, pre)

    unit = shape((8, 8, 112, 128), BF16)
    block_mine, block_theirs = call(
        block_grad_kernel,
        (unit, unit),
        [SCALAR] + [WHOLE] * 2,
        [pltpu.VMEM((6928, 256), F32)],
    )(core, cols, grad_pre)
    block_other = swap(block_theirs, core_pairs)

    block_part = (block_mine.astype(F32) + block_other.astype(F32)).astype(BF16)
    block_got = to_owners(block_part.reshape(64, 112, 128))

    thin = thin_halo(grad_pre, z_even, y_even)
    (grad_volume,) = call(
        volume_grad_kernel,
        (shape((256, 256), BF16),),
        [WHOLE] * 6,
        [pltpu.VMEM((4, 10, 24, 256), F32), pltpu.VMEM((256, 256), F32)],
    )(grad_pre, *thin, w)

    share = jnp.sum(aspp_got.astype(F32), axis=0)
    third = swap(share[0:54], FORWARDS[0]) + swap(share[56:110], FORWARDS[1])
    place_of = lax.axis_index(ALL)
    owner = jnp.any(place_of == jnp.array(OWNERS, jnp.int32))
    aspp_share = jnp.concatenate([share[0:54], share[56:110], third])
    aspp_share = jnp.where(owner, aspp_share, 0.0).reshape(20736)
    proj_share = share[112:115].reshape(384)
    share = jnp.sum(block_got.astype(F32), axis=0)
    block_share = jnp.concatenate([share[0:54], share[56:110]], axis=1).reshape(13824)
    return (
        out.reshape(4, 8, 8, 128),
        grad_volume.reshape(4, 8, 8, 256),
        block_share,
        aspp_share,
        proj_share,
    )


def solution(mesh):
    fine = Mesh(mesh.devices.reshape(4, 2, 2, 2, 4), ALL)
    cells = P(None, ("z", "yh", "c"), ("yl", "x"), None)
    flat = P(ALL)
    return jax.shard_map(
        step,
        mesh=fine,
        in_specs=(cells, P(), P(), P(), cells),
        out_specs=(cells, cells, flat, flat, flat),
        check_vma=False,
    )
```

```python
import jax
import jax.numpy as jnp
from jax import lax
from jax.experimental import pallas as pl
from jax.experimental.pallas import tpu as pltpu
from jax.sharding import Mesh
from jax.sharding import PartitionSpec as P

ALL = ("z", "yh", "c", "yl", "x")
F32 = jnp.float32
BF16 = jnp.bfloat16
VLIM = 60 * 1024 * 1024
WHOLE = pl.BlockSpec(memory_space=pltpu.VMEM)
SCALAR = pl.BlockSpec(memory_space=pltpu.SMEM)


def z_pairs(odd):
    pairs = []
    for gy in range(16):
        for gz in range(8):
            other = ((gz - odd) ^ 1) + odd
            if 0 <= other < 8:
                pairs.append((gy * 8 + gz, gy * 8 + other))
    return pairs


def y_pairs(odd):
    pairs = []
    for gy in range(16):
        for gz in range(8):
            other = ((gy - odd) ^ 1) + odd
            if 0 <= other < 16:
                pairs.append((gy * 8 + gz, other * 8 + gz))
    return pairs


def swap(value, pairs):
    return lax.ppermute(value, ALL, pairs)


def sigmoid(v):
    return 1.0 / (1.0 + jnp.exp(-v))


def slope(v):
    s = sigmoid(v)
    return s * (1.0 + v * (1.0 - s))


def call(body, outs, specs, scratch=(), flops=10**9, nbytes=10**7):
    return pl.pallas_call(
        body,
        out_shape=outs,
        in_specs=specs,
        out_specs=jax.tree.map(lambda _: WHOLE, outs),
        scratch_shapes=list(scratch),
        compiler_params=pltpu.CompilerParams(vmem_limit_bytes=VLIM),
        cost_estimate=pl.CostEstimate(flops=flops, bytes_accessed=nbytes, transcendentals=0),
    )


def shape(dims, kind):
    return jax.ShapeDtypeStruct(dims, kind)


def fill_thin(ext, block, left, right, up, down):
    width = block.shape[-1]
    ext[:, 1:9, 8:16, :] = block[...].astype(F32).reshape(4, 8, 8, width)
    left_f = left[...].astype(F32)
    right_f = right[...].astype(F32)
    for x in range(4):
        for y in range(8):
            ext[x, 1 + y, 7:8, :] = left_f[8 * x + y : 8 * x + y + 1]
            ext[x, 1 + y, 16:17, :] = right_f[8 * x + y : 8 * x + y + 1]
    for row, strip in ((0, up), (9, down)):
        s = strip[...].astype(F32)
        for x in range(4):
            ext[x, row, 8:16, :] = s[16 * x : 16 * x + 8]
            ext[x, row, 7:8, :] = s[16 * x + 8 : 16 * x + 9]
            ext[x, row, 16:17, :] = s[16 * x + 9 : 16 * x + 10]


def conv_rows(step):
    spans = []
    for tap in range(3):
        move = step * (tap - 1)
        start = max(0, -move)
        count = 4 - abs(move)
        if count > 0:
            spans.append((tap, 64 * start, 64 * (start + move), 64 * count))
    return spans


def dot_nn(a, b):
    return lax.dot_general(a, b, (((1,), (0,)), ((), ())), preferred_element_type=F32)


def dot_nt(a, b):
    return lax.dot_general(a, b, (((1,), (1,)), ((), ())), preferred_element_type=F32)


def dot_tn(a, b):
    return lax.dot_general(a, b, (((0,), (0,)), ((), ())), preferred_element_type=F32)


def block_kernel(v, left, right, up, down, w, hidden, pre, cols, ext):
    fill_thin(ext, v, left, right, up, down)
    for b in range(3):
        for c in range(3):
            k = 3 * b + c
            cols[:, 256 * k : 256 * k + 256] = (
                ext[:, b : b + 8, 7 + c : 15 + c, :].reshape(256, 256).astype(BF16)
            )
    pre[...] = dot_nn(cols[...], w[1])
    for tap, out_row, in_row, rows in conv_rows(1):
        if tap != 1:
            pre[out_row : out_row + rows] += dot_nn(cols[in_row : in_row + rows], w[tap])
    value = pre[...]
    hidden[...] = (value * sigmoid(value)).astype(BF16)


def start_weights(source, target, sems):
    copies = [
        pltpu.make_async_copy(source.at[pl.ds(0, 3)], target.at[pl.ds(0, 3)], sems.at[0]),
        pltpu.make_async_copy(source.at[pl.ds(4, 1)], target.at[pl.ds(3, 1)], sems.at[1]),
        pltpu.make_async_copy(source.at[pl.ds(7, 1)], target.at[pl.ds(4, 1)], sems.at[2]),
    ]
    for copy in copies:
        copy.start()
    return copies


def line_up(even, own, first, second, line):
    after = 2 * even
    line[1] = own[...]
    line[after] = first[...]
    line[2 - after] = second[...]


def widen(line, lanes, ext):
    width = ext.shape[-1]
    for zi in range(3):
        part = line[zi, :, lanes : lanes + width].astype(F32)
        ext[:, :, 8 * zi : 8 * zi + 8, :] = part.reshape(4, 8, 8, width)


def window(line, ext, lanes, move):
    width = ext.shape[-1]
    if move % 8 == 0:
        return line[1 + move // 8, :, lanes : lanes + width]
    return ext[:, :, 8 + move : 16 + move, :].reshape(256, width).astype(BF16)


RATES = (2, 4, 8)
ROWS_SENT = ((384, 448), (256, 384), (0, 256))


def row_kernel(parity, hidden, z1, z2, weights, pre, sent1, sent2, line, ext, cols, w, part, sems):
    copies = start_weights(weights, w, sems)
    line_up(parity[0], hidden, z1, z2, line)
    widen(line, 0, ext)
    for i, rate in enumerate(RATES):
        for c in range(3):
            cols[i, :, 256 * c : 256 * c + 256] = window(line, ext, 0, rate * (c - 1))
    for copy in copies:
        copy.wait()
    y_even = parity[1] == 1
    for i, rate in enumerate(RATES):
        out = slice(128 * i, 128 * i + 128)
        for b in (1, 0, 2):
            taps = slice(768 * b, 768 * b + 768)
            if rate == 2:
                part[...] = dot_nn(cols[i], w[1, taps]).reshape(4, 8, 8, 128)
                for a, out_row, in_row, rows in conv_rows(2):
                    if a != 1:
                        layers = slice(out_row // 64, (out_row + rows) // 64)
                        part[layers] += dot_nn(cols[i, in_row : in_row + rows], w[a, taps]).reshape(
                            rows // 64, 8, 8, 128
                        )
            else:
                part[...] = dot_nn(cols[i], w[2 + i, taps]).reshape(4, 8, 8, 128)
            lo, hi = ROWS_SENT[i]
            if b == 1:
                pre[:, :, :, out] = part[...]
            elif b == 0:
                if rate < 8:
                    pre[:, rate:8, :, out] += part[:, 0 : 8 - rate]
                message = part[:, 8 - rate : 8].reshape(32 * rate, 128).astype(BF16)

                @pl.when(y_even)
                def _():
                    sent1[lo:hi] = message

                @pl.when(jnp.logical_not(y_even))
                def _():
                    sent2[lo:hi] = message
            else:
                if rate < 8:
                    pre[:, 0 : 8 - rate, :, out] += part[:, rate:8]
                message = part[:, 0:rate].reshape(32 * rate, 128).astype(BF16)

                @pl.when(y_even)
                def _():
                    sent2[lo:hi] = message

                @pl.when(jnp.logical_not(y_even))
                def _():
                    sent1[lo:hi] = message


def branch_kernel(parity, own, y1, y2, proj, cot, out, joint, gproj, pre):
    pre[...] = own[...]

    def add(before, after):
        for i, rate in enumerate(RATES):
            lo, hi = ROWS_SENT[i]
            lanes = slice(128 * i, 128 * i + 128)
            pre[:, 0:rate, :, lanes] += before[lo:hi].astype(F32).reshape(4, rate, 8, 128)
            pre[:, 8 - rate : 8, :, lanes] += after[lo:hi].astype(F32).reshape(4, rate, 8, 128)

    @pl.when(parity[1] == 1)
    def _():
        add(y2, y1)

    @pl.when(parity[1] == 0)
    def _():
        add(y1, y2)

    value = pre[...].reshape(256, 384)
    joined = (value * sigmoid(value)).astype(BF16)
    out[...] = dot_nn(joined, proj[...]).astype(BF16)
    gproj[...] = dot_tn(joined, cot[...])
    back = dot_nt(cot[...], proj[...])
    joint[...] = (back * slope(value)).astype(BF16)


def spread_kernel(
    parity, joint, z1, z2, weights, own, sent1, sent2, cols, line, ext, w, part, up, down, sems
):
    copies = start_weights(weights, w, sems)
    line_up(parity[0], joint, z1, z2, line)
    for i, rate in enumerate(RATES):
        if rate < 8:
            widen(line, 128 * i, ext)
        for c in range(3):
            at = 384 * i + 128 * c
            cols[:, at : at + 128] = window(line, ext, 128 * i, -rate * (c - 1))
    for copy in copies:
        copy.wait()
    for b in range(3):
        for i, rate in reversed(list(enumerate(RATES))):
            for c in range(3):
                at = 384 * i + 128 * c
                tap = slice(768 * b + 256 * c, 768 * b + 256 * c + 256)
                if rate == 2:
                    term = dot_nt(cols[:, at : at + 128], w[1, tap])
                else:
                    term = dot_nt(cols[:, at : at + 128], w[2 + i, tap])
                term = term.reshape(4, 8, 8, 256)
                if c == 0:
                    part[...] = term
                else:
                    part[...] += term
                if rate == 2:
                    for a, in_row, out_row, rows in conv_rows(2):
                        if a != 1:
                            layers = slice(out_row // 64, (out_row + rows) // 64)
                            part[layers] += dot_nt(
                                cols[in_row : in_row + rows, at : at + 128], w[a, tap]
                            ).reshape(rows // 64, 8, 8, 256)
            if b == 1:
                own[...] += part[...]
            elif b == 0:
                if rate == 8:
                    up[...] = part[...]
                    own[...] = jnp.zeros_like(own)
                else:
                    own[:, 0 : 8 - rate] += part[:, rate:8]
                    up[:, 8 - rate : 8] += part[:, 0:rate]
            else:
                if rate == 8:
                    down[...] = part[...]
                else:
                    own[:, rate:8] += part[:, 0 : 8 - rate]
                    down[:, 0:rate] += part[:, 8 - rate : 8]
    y_even = parity[1] == 1
    up_message = up[...].reshape(256, 256).astype(BF16)
    down_message = down[...].reshape(256, 256).astype(BF16)

    @pl.when(y_even)
    def _():
        sent1[...] = down_message
        sent2[...] = up_message

    @pl.when(jnp.logical_not(y_even))
    def _():
        sent1[...] = up_message
        sent2[...] = down_message


def vanishing(row):
    tap = row // 256
    return tap >= 27 and (tap % 27) // 9 != 1


def share_plan():
    starts, forwards = [], ([], [])
    owners = []
    for c in range(2):
        device = [16 * (h // 8) + 8 * c + h % 8 for h in range(64)]
        full = [h for h in range(64) if not all(vanishing(162 * device[h] + r) for r in range(162))]
        spare = [h for h in range(64) if h not in full]
        slots = [[None, None] for _ in range(64)]
        for h in full:
            slots[h] = [162 * device[h], 162 * device[h] + 54]
            owners.append(device[h])
        for i, h in enumerate(full):
            slot, helper = divmod(i, len(spare))
            slots[spare[helper]][slot] = 162 * device[h] + 108
            forwards[slot].append((device[spare[helper]], device[h]))
        starts.append(slots)
    return starts, forwards, owners


SLOTS, FORWARDS, OWNERS = share_plan()


def aspp_grad_kernel(
    core, parity, hidden, h1, h2, cols, gproj, mine, theirs, line, left, block, sums, proj_rows
):
    line_up(parity[1], hidden, h1, h2, line)
    for i, rate in enumerate(RATES):
        cut = 8 * rate
        for b in range(3):
            lanes = slice(256 * b, 256 * b + 256)
            if b == 1 or rate == 8:
                left[:, lanes] = line[b]
                continue
            for x in range(0, 256, 64):
                if b == 0:
                    left[x : x + cut, lanes] = line[0, x + 64 - cut : x + 64]
                    left[x + cut : x + 64, lanes] = line[1, x : x + 64 - cut]
                else:
                    left[x : x + 64 - cut, lanes] = line[1, x + cut : x + 64]
                    left[x + 64 - cut : x + 64, lanes] = line[2, x : x + cut]
        for a, out_row, in_row, rows in conv_rows(2 if i == 0 else 4):
            block[...] = dot_tn(
                left[in_row : in_row + rows, :],
                cols[out_row : out_row + rows, 384 * i : 384 * i + 384],
            )
            for b in range(3):
                for c in range(3):
                    at = 256 * (27 * i + 9 * a + 3 * b + c)
                    sums[at : at + 256] = block[256 * b : 256 * b + 256, 128 * c : 128 * c + 128]
    for unit in OWNERS:
        for row in range(162 * unit // 8 * 8, 162 * unit + 168, 8):
            if vanishing(row):
                sums[row : row + 8] = jnp.zeros((8, 128), F32)
    proj_rows[0:384] = gproj[...]
    proj_rows[384:400] = jnp.zeros((16, 128), F32)

    def pack(target, c):
        for h in range(64):
            for slot in range(2):
                start = SLOTS[c][h][slot]
                if start is None:
                    piece = jnp.zeros((56, 128), BF16)
                else:
                    piece = sums[start : start + 56].astype(BF16)
                target[h, 56 * slot : 56 * slot + 56] = piece
            at = 3 * (16 * (h // 8) + 8 * c + h % 8)
            target[h, 112:120] = proj_rows[at : at + 8].astype(BF16)

    for me in range(2):

        @pl.when(core[0] == me)
        def _():
            pack(mine, me)
            pack(theirs, 1 - me)


def rows_at(ref, base, offset, rows):
    phase = offset % 8
    start = pl.multiple_of(base + (offset - phase), 8)
    length = rows + (8 if phase else 0)
    return ref[pl.ds(start, length), :][phase : phase + rows].astype(BF16)


def block_grad_kernel(core, cols, grad, mine, theirs, sums):
    for tap, out_row, in_row, rows in conv_rows(1):
        sums[2304 * tap : 2304 * tap + 2304] = dot_tn(
            cols[in_row : in_row + rows, :], grad[out_row : out_row + rows, :]
        )
    sums[6912:6928] = jnp.zeros((16, 256), F32)
    me = core[0]

    def step(g, carry):
        for half in range(2):
            for e in range(8):
                chunk = rows_at(sums, g * 864, 54 * (8 * half + e), 56)

                @pl.when(me == half)
                def _():
                    mine[g, e, 0:56] = chunk[:, 0:128]
                    mine[g, e, 56:112] = chunk[:, 128:256]

                @pl.when(me != half)
                def _():
                    theirs[g, e, 0:56] = chunk[:, 0:128]
                    theirs[g, e, 56:112] = chunk[:, 128:256]

        return carry

    lax.fori_loop(0, 8, step, 0)


def volume_grad_kernel(gp, left, right, up, down, w, grad, ext, acc):
    fill_thin(ext, gp, left, right, up, down)
    acc[...] = jnp.zeros_like(acc)
    for b in range(3):
        for c in range(3):
            k = 256 * (3 * b + c)
            piece = ext[:, 2 - b : 10 - b, 9 - c : 17 - c, :].reshape(256, 256).astype(BF16)
            for tap, in_row, out_row, rows in conv_rows(1):
                acc[out_row : out_row + rows] += dot_nt(
                    piece[in_row : in_row + rows], w[tap, k : k + 256, :]
                )
    grad[...] = acc[...].astype(BF16)


def thin_halo(block, z_even, y_even):
    width = block.shape[-1]
    cells = block.reshape(4, 8, 8, width)
    first, last = cells[:, :, 0], cells[:, :, 7]
    z1 = jnp.where(z_even, last, first)
    z2 = jnp.where(z_even, first, last)
    z1 = swap(z1, z_pairs(0))
    z2 = swap(z2, z_pairs(1))
    left = jnp.where(z_even, z2, z1)
    right = jnp.where(z_even, z1, z2)

    def strip(y):
        return jnp.concatenate(
            [
                cells[:, y],
                left[:, y : y + 1],
                right[:, y : y + 1],
                jnp.zeros((4, 6, width), block.dtype),
            ],
            axis=1,
        )

    top, bottom = strip(0), strip(7)
    y1 = jnp.where(y_even, bottom, top)
    y2 = jnp.where(y_even, top, bottom)
    y1 = swap(y1, y_pairs(0))
    y2 = swap(y2, y_pairs(1))
    up = jnp.where(y_even, y2, y1)
    down = jnp.where(y_even, y1, y2)
    return (
        left.reshape(32, width),
        right.reshape(32, width),
        up.reshape(64, width),
        down.reshape(64, width),
    )


def both_ways(first, second, pairs):
    return swap(first, pairs(0)), swap(second, pairs(1))


def to_owners(chunks):
    return lax.all_to_all(chunks, ("z", "yh", "yl", "x"), 0, 0, tiled=True)


def step(volume, block_weight, aspp_weight, proj_weight, cotangent):
    core = lax.axis_index("c")
    z_even = lax.axis_index("x") % 2 == 0
    y_even = core == 0
    parity = jnp.stack([z_even.astype(jnp.int32), y_even.astype(jnp.int32)])
    core = core.astype(jnp.int32).reshape(1)
    core_pairs = y_pairs(0)

    v = volume.reshape(256, 256)
    w = block_weight.reshape(3, 2304, 256)
    wa = aspp_weight.reshape(9, 2304, 128)
    cot = cotangent.reshape(256, 128)

    thin = thin_halo(v, z_even, y_even)
    hidden, pre, cols = call(
        block_kernel,
        (shape((256, 256), BF16), shape((256, 256), F32), shape((256, 2304), BF16)),
        [WHOLE] * 6,
        [pltpu.VMEM((4, 10, 24, 256), F32)],
    )(v, *thin, w)

    cells = shape((4, 8, 8, 384), F32)
    message = shape((448, 128), BF16)
    weights = [pltpu.VMEM((5, 2304, 128), BF16)]
    dma = [pltpu.SemaphoreType.DMA((3,))]
    z1, z2 = both_ways(hidden, hidden, z_pairs)
    own, sent1, sent2 = call(
        row_kernel,
        (cells, message, message),
        [SCALAR] + [WHOLE] * 3 + [pl.BlockSpec(memory_space=pl.ANY)],
        [
            pltpu.VMEM((3, 256, 256), BF16),
            pltpu.VMEM((4, 8, 24, 256), F32),
            pltpu.VMEM((3, 256, 768), BF16),
            *weights,
            pltpu.VMEM((4, 8, 8, 128), F32),
            *dma,
        ],
    )(parity, hidden, z1, z2, wa)
    y1, y2 = both_ways(sent1, sent2, y_pairs)
    h1, h2 = both_ways(hidden, hidden, y_pairs)
    out, joint, gproj = call(
        branch_kernel,
        (shape((256, 128), BF16), shape((256, 384), BF16), shape((384, 128), F32)),
        [SCALAR] + [WHOLE] * 5,
        [pltpu.VMEM((4, 8, 8, 384), F32)],
    )(parity, own, y1, y2, proj_weight, cot)

    z1, z2 = both_ways(joint, joint, z_pairs)
    own, sent1, sent2, grads = call(
        spread_kernel,
        (
            shape((4, 8, 8, 256), F32),
            shape((256, 256), BF16),
            shape((256, 256), BF16),
            shape((256, 1152), BF16),
        ),
        [SCALAR] + [WHOLE] * 3 + [pl.BlockSpec(memory_space=pl.ANY)],
        [
            pltpu.VMEM((3, 256, 384), BF16),
            pltpu.VMEM((4, 8, 24, 128), F32),
            *weights,
            pltpu.VMEM((4, 8, 8, 256), F32),
            pltpu.VMEM((4, 8, 8, 256), F32),
            pltpu.VMEM((4, 8, 8, 256), F32),
            *dma,
        ],
    )(parity, joint, z1, z2, wa)
    y1, y2 = both_ways(sent1, sent2, y_pairs)
    unit = shape((64, 120, 128), BF16)
    aspp_mine, aspp_theirs = call(
        aspp_grad_kernel,
        (unit, unit),
        [SCALAR] * 2 + [WHOLE] * 5,
        [
            pltpu.VMEM((3, 256, 256), BF16),
            pltpu.VMEM((256, 768), BF16),
            pltpu.VMEM((768, 384), F32),
            pltpu.VMEM((20752, 128), F32),
            pltpu.VMEM((400, 128), F32),
        ],
    )(core, parity, hidden, h1, h2, grads, gproj)
    aspp_other = swap(aspp_theirs, core_pairs)
    aspp_part = (aspp_mine.astype(F32) + aspp_other.astype(F32)).astype(BF16)
    aspp_got = to_owners(aspp_part)

    grad_hidden = own.reshape(256, 256) + (y1.astype(F32) + y2.astype(F32))
    grad_pre = (grad_hidden * slope(pre)).astype(BF16)

    unit = shape((8, 8, 112, 128), BF16)
    block_mine, block_theirs = call(
        block_grad_kernel,
        (unit, unit),
        [SCALAR] + [WHOLE] * 2,
        [pltpu.VMEM((6928, 256), F32)],
    )(core, cols, grad_pre)
    block_other = swap(block_theirs, core_pairs)

    block_part = (block_mine.astype(F32) + block_other.astype(F32)).astype(BF16)
    block_got = to_owners(block_part.reshape(64, 112, 128))

    thin = thin_halo(grad_pre, z_even, y_even)
    (grad_volume,) = call(
        volume_grad_kernel,
        (shape((256, 256), BF16),),
        [WHOLE] * 6,
        [pltpu.VMEM((4, 10, 24, 256), F32), pltpu.VMEM((256, 256), F32)],
    )(grad_pre, *thin, w)

    share = jnp.sum(aspp_got.astype(F32), axis=0)
    third = swap(share[0:54], FORWARDS[0]) + swap(share[56:110], FORWARDS[1])
    place_of = lax.axis_index(ALL)
    owner = jnp.any(place_of == jnp.array(OWNERS, jnp.int32))
    aspp_share = jnp.concatenate([share[0:54], share[56:110], third])
    aspp_share = jnp.where(owner, aspp_share, 0.0).reshape(20736)
    proj_share = share[112:115].reshape(384)
    share = jnp.sum(block_got.astype(F32), axis=0)
    block_share = jnp.concatenate([share[0:54], share[56:110]], axis=1).reshape(13824)
    return (
        out.reshape(4, 8, 8, 128),
        grad_volume.reshape(4, 8, 8, 256),
        block_share,
        aspp_share,
        proj_share,
    )


def solution(mesh):
    fine = Mesh(mesh.devices.reshape(4, 2, 2, 2, 4), ALL)
    cells = P(None, ("z", "yh", "c"), ("yl", "x"), None)
    flat = P(ALL)
    return jax.shard_map(
        step,
        mesh=fine,
        in_specs=(cells, P(), P(), P(), cells),
        out_specs=(cells, cells, flat, flat, flat),
        check_vma=False,
    )
```

```python
import jax
import jax.numpy as jnp
from jax import lax
from jax.experimental import pallas as pl
from jax.experimental.pallas import tpu as pltpu
from jax.sharding import Mesh
from jax.sharding import PartitionSpec as P

ALL = ("z", "yh", "c", "yl", "x")
F32 = jnp.float32
BF16 = jnp.bfloat16
VLIM = 24 * 1024 * 1024
WHOLE = pl.BlockSpec(memory_space=pltpu.VMEM)
STORED = pl.BlockSpec(memory_space=pltpu.HBM)
SCALAR = pl.BlockSpec(memory_space=pltpu.SMEM)


def z_pairs(odd):
    pairs = []
    for gy in range(16):
        for gz in range(8):
            other = ((gz - odd) ^ 1) + odd
            if 0 <= other < 8:
                pairs.append((gy * 8 + gz, gy * 8 + other))
    return pairs


def y_pairs(odd):
    pairs = []
    for gy in range(16):
        for gz in range(8):
            other = ((gy - odd) ^ 1) + odd
            if 0 <= other < 16:
                pairs.append((gy * 8 + gz, other * 8 + gz))
    return pairs


def swap(value, pairs):
    return lax.ppermute(value, ALL, pairs)


def sigmoid(v):
    return 1.0 / (1.0 + jnp.exp(-v))


def slope(v):
    s = sigmoid(v)
    return s * (1.0 + v * (1.0 - s))


def call(body, outs, specs, scratch=(), leaves=()):
    kernel = pl.pallas_call(
        body,
        out_shape=tuple(
            o if i in leaves else pltpu.VMEM(o.shape, o.dtype) for i, o in enumerate(outs)
        ),
        in_specs=specs,
        out_specs=jax.tree.map(lambda _: WHOLE, outs),
        scratch_shapes=list(scratch),
        compiler_params=pltpu.CompilerParams(vmem_limit_bytes=VLIM),
        cost_estimate=pl.CostEstimate(flops=10**9, bytes_accessed=10**7, transcendentals=0),
    )

    def run(*args):
        args = [
            arg if spec is SCALAR else pltpu.with_memory_space_constraint(arg, spec.memory_space)
            for arg, spec in zip(args, specs)
        ]
        return kernel(*args)

    return run


def shape(dims, kind):
    return jax.ShapeDtypeStruct(dims, kind)


def fill_thin(ext, block, left, right, up, down):
    width = block.shape[-1]
    ext[:, 1:9, 8:16, :] = block[...].astype(F32).reshape(4, 8, 8, width)
    left_f = left[...].astype(F32)
    right_f = right[...].astype(F32)
    for x in range(4):
        for y in range(8):
            ext[x, 1 + y, 7:8, :] = left_f[8 * x + y : 8 * x + y + 1]
            ext[x, 1 + y, 16:17, :] = right_f[8 * x + y : 8 * x + y + 1]
    for row, strip in ((0, up), (9, down)):
        s = strip[...].astype(F32)
        for x in range(4):
            ext[x, row, 8:16, :] = s[16 * x : 16 * x + 8]
            ext[x, row, 7:8, :] = s[16 * x + 8 : 16 * x + 9]
            ext[x, row, 16:17, :] = s[16 * x + 9 : 16 * x + 10]


def conv_rows(step):
    spans = []
    for tap in range(3):
        move = step * (tap - 1)
        start = max(0, -move)
        count = 4 - abs(move)
        if count > 0:
            spans.append((tap, 64 * start, 64 * (start + move), 64 * count))
    return spans


def dot_nn(a, b):
    return lax.dot_general(a, b, (((1,), (0,)), ((), ())), preferred_element_type=F32)


def dot_nt(a, b):
    return lax.dot_general(a, b, (((1,), (1,)), ((), ())), preferred_element_type=F32)


def dot_tn(a, b):
    return lax.dot_general(a, b, (((0,), (0,)), ((), ())), preferred_element_type=F32)


def block_kernel(v, left, right, up, down, weights, hidden, pre, cols, ext, w, sems):
    copies = [pltpu.make_async_copy(weights.at[a], w.at[a], sems.at[a]) for a in range(3)]
    for a in (1, 0, 2):
        copies[a].start()
    fill_thin(ext, v, left, right, up, down)
    for b in range(3):
        for c in range(3):
            k = 3 * b + c
            cols[:, 256 * k : 256 * k + 256] = (
                ext[:, b : b + 8, 7 + c : 15 + c, :].reshape(256, 256).astype(BF16)
            )
    copies[1].wait()
    pre[...] = dot_nn(cols[...], w[1])
    for tap, out_row, in_row, rows in conv_rows(1):
        if tap != 1:
            copies[tap].wait()
            pre[out_row : out_row + rows] += dot_nn(cols[in_row : in_row + rows], w[tap])
    value = pre[...]
    hidden[...] = (value * sigmoid(value)).astype(BF16)


def start_weights(source, target, sems):
    copies = [
        pltpu.make_async_copy(source.at[pl.ds(0, 3)], target.at[pl.ds(0, 3)], sems.at[0]),
        pltpu.make_async_copy(source.at[pl.ds(4, 1)], target.at[pl.ds(3, 1)], sems.at[1]),
        pltpu.make_async_copy(source.at[pl.ds(7, 1)], target.at[pl.ds(4, 1)], sems.at[2]),
    ]
    for copy in reversed(copies):
        copy.start()
    return copies


def line_up(even, own, first, second, line):
    after = 2 * even
    line[1] = own[...]
    line[after] = first[...]
    line[2 - after] = second[...]


def widen(line, lanes, ext):
    width = ext.shape[-1]
    for zi in range(3):
        part = line[zi, :, lanes : lanes + width].astype(F32)
        ext[:, :, 8 * zi : 8 * zi + 8, :] = part.reshape(4, 8, 8, width)


def window(line, ext, lanes, move):
    width = ext.shape[-1]
    if move % 8 == 0:
        return line[1 + move // 8, :, lanes : lanes + width]
    return ext[:, :, 8 + move : 16 + move, :].reshape(256, width).astype(BF16)


RATES = (2, 4, 8)
ROWS_SENT = ((384, 448), (256, 384), (0, 256))


def row_kernel(parity, hidden, z1, z2, weights, pre, sent1, sent2, line, ext, cols, w, part, sems):
    copies = start_weights(weights, w, sems)
    line_up(parity[0], hidden, z1, z2, line)
    widen(line, 0, ext)
    for i, rate in enumerate(RATES):
        for c in range(3):
            cols[i, :, 256 * c : 256 * c + 256] = window(line, ext, 0, rate * (c - 1))
    for lo in (0, 128):
        for sent in (sent1, sent2):
            sent[448 + 2 * lo : 704 + 2 * lo] = hidden[:, lo : lo + 128]
    y_even = parity[1] == 1
    for i, rate in reversed(list(enumerate(RATES))):
        copies[i].wait()
        out = slice(128 * i, 128 * i + 128)
        for b in (1, 0, 2):
            taps = slice(768 * b, 768 * b + 768)
            if rate == 2:
                part[...] = dot_nn(cols[i], w[1, taps]).reshape(4, 8, 8, 128)
                for a, out_row, in_row, rows in conv_rows(2):
                    if a != 1:
                        layers = slice(out_row // 64, (out_row + rows) // 64)
                        part[layers] += dot_nn(cols[i, in_row : in_row + rows], w[a, taps]).reshape(
                            rows // 64, 8, 8, 128
                        )
            else:
                part[...] = dot_nn(cols[i], w[2 + i, taps]).reshape(4, 8, 8, 128)
            lo, hi = ROWS_SENT[i]
            if b == 1:
                pre[:, :, :, out] = part[...]
            elif b == 0:
                if rate < 8:
                    pre[:, rate:8, :, out] += part[:, 0 : 8 - rate]
                message = part[:, 8 - rate : 8].reshape(32 * rate, 128).astype(BF16)

                @pl.when(y_even)
                def _():
                    sent1[lo:hi] = message

                @pl.when(jnp.logical_not(y_even))
                def _():
                    sent2[lo:hi] = message
            else:
                if rate < 8:
                    pre[:, 0 : 8 - rate, :, out] += part[:, rate:8]
                message = part[:, 0:rate].reshape(32 * rate, 128).astype(BF16)

                @pl.when(y_even)
                def _():
                    sent2[lo:hi] = message

                @pl.when(jnp.logical_not(y_even))
                def _():
                    sent1[lo:hi] = message


def branch_kernel(parity, own, y1, y2, proj, cot, out, joint, gproj, pre):
    pre[...] = own[...]

    def add(before, after):
        for i, rate in enumerate(RATES):
            lo, hi = ROWS_SENT[i]
            lanes = slice(128 * i, 128 * i + 128)
            pre[:, 0:rate, :, lanes] += before[lo:hi].astype(F32).reshape(4, rate, 8, 128)
            pre[:, 8 - rate : 8, :, lanes] += after[lo:hi].astype(F32).reshape(4, rate, 8, 128)

    @pl.when(parity[1] == 1)
    def _():
        add(y2, y1)

    @pl.when(parity[1] == 0)
    def _():
        add(y1, y2)

    value = pre[...].reshape(256, 384)
    joined = (value * sigmoid(value)).astype(BF16)
    out[...] = dot_nn(joined, proj[...]).astype(BF16)
    gproj[...] = dot_tn(joined, cot[...])
    back = dot_nt(cot[...], proj[...])
    joint[...] = (back * slope(value)).astype(BF16)


def spread_kernel(parity, cols, weights, own, sent1, sent2, w, part, up, down, sems):
    copies = start_weights(weights, w, sems)
    for b in range(3):
        for i, rate in reversed(list(enumerate(RATES))):
            if b == 0:
                copies[i].wait()
            for c in range(3):
                at = 384 * i + 128 * c
                tap = slice(768 * b + 256 * c, 768 * b + 256 * c + 256)
                if rate == 2:
                    term = dot_nt(cols[:, at : at + 128], w[1, tap])
                else:
                    term = dot_nt(cols[:, at : at + 128], w[2 + i, tap])
                term = term.reshape(4, 8, 8, 256)
                if c == 0:
                    part[...] = term
                else:
                    part[...] += term
                if rate == 2:
                    for a, in_row, out_row, rows in conv_rows(2):
                        if a != 1:
                            layers = slice(out_row // 64, (out_row + rows) // 64)
                            part[layers] += dot_nt(
                                cols[in_row : in_row + rows, at : at + 128], w[a, tap]
                            ).reshape(rows // 64, 8, 8, 256)
            if b == 1:
                own[...] += part[...]
            elif b == 0:
                if rate == 8:
                    up[...] = part[...]
                    own[...] = jnp.zeros_like(own)
                else:
                    own[:, 0 : 8 - rate] += part[:, rate:8]
                    up[:, 8 - rate : 8] += part[:, 0:rate]
            else:
                if rate == 8:
                    down[...] = part[...]
                else:
                    own[:, rate:8] += part[:, 0 : 8 - rate]
                    down[:, 0:rate] += part[:, 8 - rate : 8]
    y_even = parity[1] == 1
    up_message = up[...].reshape(256, 256).astype(BF16)
    down_message = down[...].reshape(256, 256).astype(BF16)

    @pl.when(y_even)
    def _():
        sent1[...] = down_message
        sent2[...] = up_message

    @pl.when(jnp.logical_not(y_even))
    def _():
        sent1[...] = up_message
        sent2[...] = down_message


def vanishing(row):
    tap = row // 256
    return tap >= 27 and (tap % 27) // 9 != 1


def share_plan():
    starts, forwards = [], ([], [])
    owners = []
    for c in range(2):
        device = [16 * (h // 8) + 8 * c + h % 8 for h in range(64)]
        full = [h for h in range(64) if not all(vanishing(162 * device[h] + r) for r in range(162))]
        spare = [h for h in range(64) if h not in full]
        slots = [[None, None] for _ in range(64)]
        for h in full:
            slots[h] = [162 * device[h], 162 * device[h] + 54]
            owners.append(device[h])
        for i, h in enumerate(full):
            slot, helper = divmod(i, len(spare))
            slots[spare[helper]][slot] = 162 * device[h] + 108
            forwards[slot].append((device[spare[helper]], device[h]))
        starts.append(slots)
    return starts, forwards, owners


SLOTS, FORWARDS, OWNERS = share_plan()


def aspp_grad_kernel(
    core, parity, hidden, y1, y2, joint, z1, z2, gproj,
    mine, theirs, cols, line, near, ext, left, block, sums, proj_rows,
):
    line_up(parity[0], joint, z1, z2, near)
    for i, rate in enumerate(RATES):
        if rate < 8:
            widen(near, 128 * i, ext)
        for c in range(3):
            at = 384 * i + 128 * c
            cols[:, at : at + 128] = window(near, ext, 128 * i, -rate * (c - 1))
    after = 2 * parity[1]
    line[1] = hidden[...]
    for lo in (0, 128):
        line[after, :, lo : lo + 128] = y1[448 + 2 * lo : 704 + 2 * lo]
        line[2 - after, :, lo : lo + 128] = y2[448 + 2 * lo : 704 + 2 * lo]
    for i, rate in enumerate(RATES):
        cut = 8 * rate
        for b in range(3):
            lanes = slice(256 * b, 256 * b + 256)
            if b == 1 or rate == 8:
                left[:, lanes] = line[b]
                continue
            for x in range(0, 256, 64):
                if b == 0:
                    left[x : x + cut, lanes] = line[0, x + 64 - cut : x + 64]
                    left[x + cut : x + 64, lanes] = line[1, x : x + 64 - cut]
                else:
                    left[x : x + 64 - cut, lanes] = line[1, x + cut : x + 64]
                    left[x + 64 - cut : x + 64, lanes] = line[2, x : x + cut]
        for a, out_row, in_row, rows in conv_rows(2 if i == 0 else 4):
            block[...] = dot_tn(
                left[in_row : in_row + rows, :],
                cols[out_row : out_row + rows, 384 * i : 384 * i + 384],
            )
            for b in range(3):
                for c in range(3):
                    at = 256 * (27 * i + 9 * a + 3 * b + c)
                    sums[at : at + 256] = block[256 * b : 256 * b + 256, 128 * c : 128 * c + 128]
    for unit in OWNERS:
        for row in range(162 * unit // 8 * 8, 162 * unit + 168, 8):
            if vanishing(row):
                sums[row : row + 8] = jnp.zeros((8, 128), F32)
    proj_rows[0:8] = jnp.zeros((8, 128), F32)
    proj_rows[8:392] = gproj[...]
    proj_rows[392:400] = jnp.zeros((8, 128), F32)
    spare = lax.broadcasted_iota(jnp.int32, (8, 128), 0) >= 6

    def pack(target, c):
        for h in range(64):
            for slot in range(2):
                start = SLOTS[c][h][slot]
                row = 2 + 3 * (16 * (h // 8) + 8 * c + h % 8) + 2 * slot
                last = proj_rows[row : row + 8]
                if start is None:
                    target[h, 56 * slot : 56 * slot + 48] = jnp.zeros((48, 128), BF16)
                else:
                    target[h, 56 * slot : 56 * slot + 48] = sums[start : start + 48].astype(BF16)
                    last = jnp.where(spare, last, sums[start + 48 : start + 56])
                target[h, 56 * slot + 48 : 56 * slot + 56] = last.astype(BF16)

    for me in range(2):

        @pl.when(core[0] == me)
        def _():
            pack(mine, me)
            pack(theirs, 1 - me)


def rows_at(ref, base, offset, rows):
    phase = offset % 8
    start = pl.multiple_of(base + (offset - phase), 8)
    length = rows + (8 if phase else 0)
    return ref[pl.ds(start, length), :][phase : phase + rows].astype(BF16)


def block_grad_kernel(core, cols, grad, mine, theirs, sums):
    for tap, out_row, in_row, rows in conv_rows(1):
        sums[2304 * tap : 2304 * tap + 2304] = dot_tn(
            cols[in_row : in_row + rows, :], grad[out_row : out_row + rows, :]
        )
    sums[6912:6928] = jnp.zeros((16, 256), F32)
    me = core[0]

    def step(g, carry):
        for half in range(2):
            for e in range(8):
                chunk = rows_at(sums, g * 864, 54 * (8 * half + e), 56)

                @pl.when(me == half)
                def _():
                    mine[g, e, 0:56] = chunk[:, 0:128]
                    mine[g, e, 56:112] = chunk[:, 128:256]

                @pl.when(me != half)
                def _():
                    theirs[g, e, 0:56] = chunk[:, 0:128]
                    theirs[g, e, 56:112] = chunk[:, 128:256]

        return carry

    lax.fori_loop(0, 8, step, 0)


def volume_grad_kernel(gp, left, right, up, down, w, grad, ext, acc):
    fill_thin(ext, gp, left, right, up, down)
    acc[...] = jnp.zeros_like(acc)
    for b in range(3):
        for c in range(3):
            k = 256 * (3 * b + c)
            piece = ext[:, 2 - b : 10 - b, 9 - c : 17 - c, :].reshape(256, 256).astype(BF16)
            for tap, in_row, out_row, rows in conv_rows(1):
                acc[out_row : out_row + rows] += dot_nt(
                    piece[in_row : in_row + rows], w[tap, k : k + 256, :]
                )
    grad[...] = acc[...].astype(BF16)


def thin_halo(block, z_even, y_even):
    width = block.shape[-1]
    cells = block.reshape(4, 8, 8, width)
    first, last = cells[:, :, 0], cells[:, :, 7]
    z1 = jnp.where(z_even, last, first)
    z2 = jnp.where(z_even, first, last)
    z1 = swap(z1, z_pairs(0))
    z2 = swap(z2, z_pairs(1))
    left = jnp.where(z_even, z2, z1)
    right = jnp.where(z_even, z1, z2)

    def strip(y):
        return jnp.concatenate(
            [
                cells[:, y],
                left[:, y : y + 1],
                right[:, y : y + 1],
                jnp.zeros((4, 6, width), block.dtype),
            ],
            axis=1,
        )

    top, bottom = strip(0), strip(7)
    y1 = jnp.where(y_even, bottom, top)
    y2 = jnp.where(y_even, top, bottom)
    y1 = swap(y1, y_pairs(0))
    y2 = swap(y2, y_pairs(1))
    up = jnp.where(y_even, y2, y1)
    down = jnp.where(y_even, y1, y2)
    return (
        left.reshape(32, width),
        right.reshape(32, width),
        up.reshape(64, width),
        down.reshape(64, width),
    )


def both_ways(first, second, pairs):
    return swap(first, pairs(0)), swap(second, pairs(1))


def to_owners(chunks):
    return lax.all_to_all(chunks, ("z", "yh", "yl", "x"), 0, 0, tiled=True)


def step(volume, block_weight, aspp_weight, proj_weight, cotangent):
    core = lax.axis_index("c")
    z_even = lax.axis_index("x") % 2 == 0
    y_even = core == 0
    parity = jnp.stack([z_even.astype(jnp.int32), y_even.astype(jnp.int32)])
    core = core.astype(jnp.int32).reshape(1)
    core_pairs = y_pairs(0)

    v = volume.reshape(256, 256)
    w = block_weight.reshape(3, 2304, 256)
    wa = aspp_weight.reshape(9, 2304, 128)
    cot = cotangent.reshape(256, 128)

    thin = thin_halo(v, z_even, y_even)
    hidden, pre, cols = call(
        block_kernel,
        (shape((256, 256), BF16), shape((256, 256), F32), shape((256, 2304), BF16)),
        [WHOLE] * 5 + [STORED],
        [
            pltpu.VMEM((4, 10, 24, 256), F32),
            pltpu.VMEM((3, 2304, 256), BF16),
            pltpu.SemaphoreType.DMA((3,)),
        ],
    )(v, *thin, w)

    cells = shape((4, 8, 8, 384), F32)
    message = shape((960, 128), BF16)
    weights = [pltpu.VMEM((5, 2304, 128), BF16)]
    dma = [pltpu.SemaphoreType.DMA((3,))]
    z1, z2 = both_ways(hidden, hidden, z_pairs)
    own, sent1, sent2 = call(
        row_kernel,
        (cells, message, message),
        [SCALAR] + [WHOLE] * 3 + [STORED],
        [
            pltpu.VMEM((3, 256, 256), BF16),
            pltpu.VMEM((4, 8, 24, 256), F32),
            pltpu.VMEM((3, 256, 768), BF16),
            *weights,
            pltpu.VMEM((4, 8, 8, 128), F32),
            *dma,
        ],
    )(parity, hidden, z1, z2, wa)
    y1, y2 = both_ways(sent1, sent2, y_pairs)
    out, joint, gproj = call(
        branch_kernel,
        (shape((256, 128), BF16), shape((256, 384), BF16), shape((384, 128), F32)),
        [SCALAR] + [WHOLE] * 5,
        [pltpu.VMEM((4, 8, 8, 384), F32)],
        leaves=(0,),
    )(parity, own, y1, y2, proj_weight, cot)

    z1, z2 = both_ways(joint, joint, z_pairs)
    unit = shape((64, 112, 128), BF16)
    aspp_mine, aspp_theirs, grads = call(
        aspp_grad_kernel,
        (unit, unit, shape((256, 1152), BF16)),
        [SCALAR] * 2 + [WHOLE] * 7,
        [
            pltpu.VMEM((3, 256, 256), BF16),
            pltpu.VMEM((3, 256, 384), BF16),
            pltpu.VMEM((4, 8, 24, 128), F32),
            pltpu.VMEM((256, 768), BF16),
            pltpu.VMEM((768, 384), F32),
            pltpu.VMEM((20752, 128), F32),
            pltpu.VMEM((400, 128), F32),
        ],
    )(core, parity, hidden, y1, y2, joint, z1, z2, gproj)
    aspp_other = swap(aspp_theirs, core_pairs)
    own, sent1, sent2 = call(
        spread_kernel,
        (shape((4, 8, 8, 256), F32), shape((256, 256), BF16), shape((256, 256), BF16)),
        [SCALAR, WHOLE, STORED],
        [
            *weights,
            pltpu.VMEM((4, 8, 8, 256), F32),
            pltpu.VMEM((4, 8, 8, 256), F32),
            pltpu.VMEM((4, 8, 8, 256), F32),
            *dma,
        ],
    )(parity, grads, wa)
    y1, y2 = both_ways(sent1, sent2, y_pairs)
    aspp_part = (aspp_mine.astype(F32) + aspp_other.astype(F32)).astype(BF16)
    aspp_got = to_owners(aspp_part)

    grad_hidden = own.reshape(256, 256) + (y1.astype(F32) + y2.astype(F32))
    grad_pre = (grad_hidden * slope(pre)).astype(BF16)

    unit = shape((8, 8, 112, 128), BF16)
    block_mine, block_theirs = call(
        block_grad_kernel,
        (unit, unit),
        [SCALAR] + [WHOLE] * 2,
        [pltpu.VMEM((6928, 256), F32)],
    )(core, cols, grad_pre)
    block_other = swap(block_theirs, core_pairs)

    block_part = (block_mine.astype(F32) + block_other.astype(F32)).astype(BF16)
    block_got = to_owners(block_part.reshape(64, 112, 128))

    thin = thin_halo(grad_pre, z_even, y_even)
    (grad_volume,) = call(
        volume_grad_kernel,
        (shape((256, 256), BF16),),
        [WHOLE] * 6,
        [pltpu.VMEM((4, 10, 24, 256), F32), pltpu.VMEM((256, 256), F32)],
        leaves=(0,),
    )(grad_pre, *thin, w)

    share = jnp.sum(aspp_got.astype(F32), axis=0)
    third = swap(share[0:54], FORWARDS[0]) + swap(share[56:110], FORWARDS[1])
    place_of = lax.axis_index(ALL)
    owner = jnp.any(place_of == jnp.array(OWNERS, jnp.int32))
    aspp_share = jnp.concatenate([share[0:54], share[56:110], third])
    aspp_share = jnp.where(owner, aspp_share, 0.0).reshape(20736)
    proj_share = jnp.concatenate([share[54:56], share[110:111]]).reshape(384)
    share = jnp.sum(block_got.astype(F32), axis=0)
    block_share = jnp.concatenate([share[0:54], share[56:110]], axis=1).reshape(13824)
    return (
        out.reshape(4, 8, 8, 128),
        grad_volume.reshape(4, 8, 8, 256),
        block_share,
        aspp_share,
        proj_share,
    )


def solution(mesh):
    fine = Mesh(mesh.devices.reshape(4, 2, 2, 2, 4), ALL)
    cells = P(None, ("z", "yh", "c"), ("yl", "x"), None)
    flat = P(ALL)
    return jax.shard_map(
        step,
        mesh=fine,
        in_specs=(cells, P(), P(), P(), cells),
        out_specs=(cells, cells, flat, flat, flat),
        check_vma=False,
    )
```

```python
import jax
import jax.numpy as jnp
from jax import lax
from jax.experimental import pallas as pl
from jax.experimental.pallas import tpu as pltpu
from jax.sharding import Mesh
from jax.sharding import PartitionSpec as P

ALL = ("z", "yh", "c", "yl", "x")
F32 = jnp.float32
BF16 = jnp.bfloat16
VLIM = 24 * 1024 * 1024
WHOLE = pl.BlockSpec(memory_space=pltpu.VMEM)
STORED = pl.BlockSpec(memory_space=pltpu.HBM)
SCALAR = pl.BlockSpec(memory_space=pltpu.SMEM)


def z_pairs(odd):
    pairs = []
    for gy in range(16):
        for gz in range(8):
            other = ((gz - odd) ^ 1) + odd
            if 0 <= other < 8:
                pairs.append((gy * 8 + gz, gy * 8 + other))
    return pairs


def y_pairs(odd):
    pairs = []
    for gy in range(16):
        for gz in range(8):
            other = ((gy - odd) ^ 1) + odd
            if 0 <= other < 16:
                pairs.append((gy * 8 + gz, other * 8 + gz))
    return pairs


def swap(value, pairs):
    return lax.ppermute(value, ALL, pairs)


def sigmoid(v):
    return 1.0 / (1.0 + jnp.exp(-v))


def slope(v):
    s = sigmoid(v)
    return s * (1.0 + v * (1.0 - s))


def call(body, outs, specs, scratch=(), leaves=()):
    kernel = pl.pallas_call(
        body,
        out_shape=tuple(
            o if i in leaves else pltpu.VMEM(o.shape, o.dtype) for i, o in enumerate(outs)
        ),
        in_specs=specs,
        out_specs=jax.tree.map(lambda _: WHOLE, outs),
        scratch_shapes=list(scratch),
        compiler_params=pltpu.CompilerParams(vmem_limit_bytes=VLIM),
        cost_estimate=pl.CostEstimate(flops=10**9, bytes_accessed=10**7, transcendentals=0),
    )

    def run(*args):
        args = [
            arg if spec is SCALAR else pltpu.with_memory_space_constraint(arg, spec.memory_space)
            for arg, spec in zip(args, specs)
        ]
        return kernel(*args)

    return run


def shape(dims, kind):
    return jax.ShapeDtypeStruct(dims, kind)


def fill_thin(ext, block, left, right, up, down):
    width = block.shape[-1]
    ext[:, 1:9, 8:16, :] = block[...].astype(F32).reshape(4, 8, 8, width)
    left_f = left[...].astype(F32)
    right_f = right[...].astype(F32)
    for x in range(4):
        for y in range(8):
            ext[x, 1 + y, 7:8, :] = left_f[8 * x + y : 8 * x + y + 1]
            ext[x, 1 + y, 16:17, :] = right_f[8 * x + y : 8 * x + y + 1]
    for row, strip in ((0, up), (9, down)):
        s = strip[...].astype(F32)
        for x in range(4):
            ext[x, row, 8:16, :] = s[16 * x : 16 * x + 8]
            ext[x, row, 7:8, :] = s[16 * x + 8 : 16 * x + 9]
            ext[x, row, 16:17, :] = s[16 * x + 9 : 16 * x + 10]


def conv_rows(step):
    spans = []
    for tap in range(3):
        move = step * (tap - 1)
        start = max(0, -move)
        count = 4 - abs(move)
        if count > 0:
            spans.append((tap, 64 * start, 64 * (start + move), 64 * count))
    return spans


def dot_nn(a, b):
    return lax.dot_general(a, b, (((1,), (0,)), ((), ())), preferred_element_type=F32)


def dot_nt(a, b):
    return lax.dot_general(a, b, (((1,), (1,)), ((), ())), preferred_element_type=F32)


def dot_tn(a, b):
    return lax.dot_general(a, b, (((0,), (0,)), ((), ())), preferred_element_type=F32)


def block_kernel(v, left, right, up, down, weights, hidden, pre, cols, ext, w, sems):
    copies = [pltpu.make_async_copy(weights.at[a], w.at[a], sems.at[a]) for a in range(3)]
    for a in (1, 0, 2):
        copies[a].start()
    fill_thin(ext, v, left, right, up, down)
    for b in range(3):
        for c in range(3):
            k = 3 * b + c
            cols[:, 256 * k : 256 * k + 256] = (
                ext[:, b : b + 8, 7 + c : 15 + c, :].reshape(256, 256).astype(BF16)
            )
    copies[1].wait()
    pre[...] = dot_nn(cols[...], w[1])
    for tap, out_row, in_row, rows in conv_rows(1):
        if tap != 1:
            copies[tap].wait()
            pre[out_row : out_row + rows] += dot_nn(cols[in_row : in_row + rows], w[tap])
    value = pre[...]
    hidden[...] = (value * sigmoid(value)).astype(BF16)


def start_weights(source, target, sems):
    copies = [
        pltpu.make_async_copy(source.at[pl.ds(0, 3)], target.at[pl.ds(0, 3)], sems.at[0]),
        pltpu.make_async_copy(source.at[pl.ds(4, 1)], target.at[pl.ds(3, 1)], sems.at[1]),
        pltpu.make_async_copy(source.at[pl.ds(7, 1)], target.at[pl.ds(4, 1)], sems.at[2]),
    ]
    for copy in reversed(copies):
        copy.start()
    return copies


def line_up(even, own, first, second, line):
    after = 2 * even
    line[1] = own[...]
    line[after] = first[...]
    line[2 - after] = second[...]


def widen(line, lanes, ext):
    width = ext.shape[-1]
    for zi in range(3):
        part = line[zi, :, lanes : lanes + width].astype(F32)
        ext[:, :, 8 * zi : 8 * zi + 8, :] = part.reshape(4, 8, 8, width)


def window(line, ext, lanes, move):
    width = ext.shape[-1]
    if move % 8 == 0:
        return line[1 + move // 8, :, lanes : lanes + width]
    return ext[:, :, 8 + move : 16 + move, :].reshape(256, width).astype(BF16)


RATES = (2, 4, 8)
ROWS_SENT = ((384, 448), (256, 384), (0, 256))


def row_kernel(parity, hidden, z1, z2, weights, pre, sent1, sent2, line, ext, cols, w, part, sems):
    copies = start_weights(weights, w, sems)
    line_up(parity[0], hidden, z1, z2, line)
    widen(line, 0, ext)
    for i, rate in enumerate(RATES):
        for c in range(3):
            cols[i, :, 256 * c : 256 * c + 256] = window(line, ext, 0, rate * (c - 1))
    y_even = parity[1] == 1
    for i, rate in reversed(list(enumerate(RATES))):
        copies[i].wait()
        out = slice(128 * i, 128 * i + 128)
        for b in (1, 0, 2):
            taps = slice(768 * b, 768 * b + 768)
            if rate == 2:
                part[...] = dot_nn(cols[i], w[1, taps]).reshape(4, 8, 8, 128)
                for a, out_row, in_row, rows in conv_rows(2):
                    if a != 1:
                        layers = slice(out_row // 64, (out_row + rows) // 64)
                        part[layers] += dot_nn(cols[i, in_row : in_row + rows], w[a, taps]).reshape(
                            rows // 64, 8, 8, 128
                        )
            else:
                part[...] = dot_nn(cols[i], w[2 + i, taps]).reshape(4, 8, 8, 128)
            lo, hi = ROWS_SENT[i]
            if b == 1:
                pre[:, :, :, out] = part[...]
            elif b == 0:
                if rate < 8:
                    pre[:, rate:8, :, out] += part[:, 0 : 8 - rate]
                message = part[:, 8 - rate : 8].reshape(32 * rate, 128).astype(BF16)

                @pl.when(y_even)
                def _():
                    sent1[lo:hi] = message

                @pl.when(jnp.logical_not(y_even))
                def _():
                    sent2[lo:hi] = message
            else:
                if rate < 8:
                    pre[:, 0 : 8 - rate, :, out] += part[:, rate:8]
                message = part[:, 0:rate].reshape(32 * rate, 128).astype(BF16)

                @pl.when(y_even)
                def _():
                    sent2[lo:hi] = message

                @pl.when(jnp.logical_not(y_even))
                def _():
                    sent1[lo:hi] = message


def branch_kernel(parity, own, y1, y2, proj, cot, out, joint, gproj, pre):
    pre[...] = own[...]

    def add(before, after):
        for i, rate in enumerate(RATES):
            lo, hi = ROWS_SENT[i]
            lanes = slice(128 * i, 128 * i + 128)
            pre[:, 0:rate, :, lanes] += before[lo:hi].astype(F32).reshape(4, rate, 8, 128)
            pre[:, 8 - rate : 8, :, lanes] += after[lo:hi].astype(F32).reshape(4, rate, 8, 128)

    @pl.when(parity[1] == 1)
    def _():
        add(y2, y1)

    @pl.when(parity[1] == 0)
    def _():
        add(y1, y2)

    value = pre[...].reshape(256, 384)
    joined = (value * sigmoid(value)).astype(BF16)
    out[...] = dot_nn(joined, proj[...]).astype(BF16)
    gproj[...] = dot_tn(joined, cot[...])
    back = dot_nt(cot[...], proj[...])
    joint[...] = (back * slope(value)).astype(BF16)


def spread_kernel(parity, cols, weights, own, sent1, sent2, w, part, up, down, sems):
    copies = start_weights(weights, w, sems)
    for b in range(3):
        for i, rate in reversed(list(enumerate(RATES))):
            if b == 0:
                copies[i].wait()
            for c in range(3):
                at = 384 * i + 128 * c
                tap = slice(768 * b + 256 * c, 768 * b + 256 * c + 256)
                if rate == 2:
                    term = dot_nt(cols[:, at : at + 128], w[1, tap])
                else:
                    term = dot_nt(cols[:, at : at + 128], w[2 + i, tap])
                term = term.reshape(4, 8, 8, 256)
                if c == 0:
                    part[...] = term
                else:
                    part[...] += term
                if rate == 2:
                    for a, in_row, out_row, rows in conv_rows(2):
                        if a != 1:
                            layers = slice(out_row // 64, (out_row + rows) // 64)
                            part[layers] += dot_nt(
                                cols[in_row : in_row + rows, at : at + 128], w[a, tap]
                            ).reshape(rows // 64, 8, 8, 256)
            if b == 1:
                own[...] += part[...]
            elif b == 0:
                if rate == 8:
                    up[...] = part[...]
                    own[...] = jnp.zeros_like(own)
                else:
                    own[:, 0 : 8 - rate] += part[:, rate:8]
                    up[:, 8 - rate : 8] += part[:, 0:rate]
            else:
                if rate == 8:
                    down[...] = part[...]
                else:
                    own[:, rate:8] += part[:, 0 : 8 - rate]
                    down[:, 0:rate] += part[:, 8 - rate : 8]
    y_even = parity[1] == 1
    up_message = up[...].reshape(256, 256).astype(BF16)
    down_message = down[...].reshape(256, 256).astype(BF16)

    @pl.when(y_even)
    def _():
        sent1[...] = down_message
        sent2[...] = up_message

    @pl.when(jnp.logical_not(y_even))
    def _():
        sent1[...] = up_message
        sent2[...] = down_message


def vanishing(row):
    tap = row // 256
    return tap >= 27 and (tap % 27) // 9 != 1


def share_plan():
    starts, forwards = [], ([], [])
    owners = []
    for c in range(2):
        device = [16 * (h // 8) + 8 * c + h % 8 for h in range(64)]
        full = [h for h in range(64) if not all(vanishing(162 * device[h] + r) for r in range(162))]
        spare = [h for h in range(64) if h not in full]
        slots = [[None, None] for _ in range(64)]
        for h in full:
            slots[h] = [162 * device[h], 162 * device[h] + 54]
            owners.append(device[h])
        for i, h in enumerate(full):
            slot, helper = divmod(i, len(spare))
            slots[spare[helper]][slot] = 162 * device[h] + 108
            forwards[slot].append((device[spare[helper]], device[h]))
        starts.append(slots)
    return starts, forwards, owners


SLOTS, FORWARDS, OWNERS = share_plan()


def aspp_grad_kernel(
    core, parity, hidden, y1, y2, joint, z1, z2, gproj,
    mine, theirs, cols, line, near, ext, left, block, sums, proj_rows,
):
    line_up(parity[0], joint, z1, z2, near)
    for i, rate in enumerate(RATES):
        if rate < 8:
            widen(near, 128 * i, ext)
        for c in range(3):
            at = 384 * i + 128 * c
            cols[:, at : at + 128] = window(near, ext, 128 * i, -rate * (c - 1))
    line_up(parity[1], hidden, y1, y2, line)
    for i, rate in enumerate(RATES):
        cut = 8 * rate
        for b in range(3):
            lanes = slice(256 * b, 256 * b + 256)
            if b == 1 or rate == 8:
                left[:, lanes] = line[b]
                continue
            for x in range(0, 256, 64):
                if b == 0:
                    left[x : x + cut, lanes] = line[0, x + 64 - cut : x + 64]
                    left[x + cut : x + 64, lanes] = line[1, x : x + 64 - cut]
                else:
                    left[x : x + 64 - cut, lanes] = line[1, x + cut : x + 64]
                    left[x + 64 - cut : x + 64, lanes] = line[2, x : x + cut]
        for a, out_row, in_row, rows in conv_rows(2 if i == 0 else 4):
            block[...] = dot_tn(
                left[in_row : in_row + rows, :],
                cols[out_row : out_row + rows, 384 * i : 384 * i + 384],
            )
            for b in range(3):
                for c in range(3):
                    at = 256 * (27 * i + 9 * a + 3 * b + c)
                    sums[at : at + 256] = block[256 * b : 256 * b + 256, 128 * c : 128 * c + 128]
    for unit in OWNERS:
        for row in range(162 * unit // 8 * 8, 162 * unit + 168, 8):
            if vanishing(row):
                sums[row : row + 8] = jnp.zeros((8, 128), F32)
    proj_rows[0:8] = jnp.zeros((8, 128), F32)
    proj_rows[8:392] = gproj[...]
    proj_rows[392:400] = jnp.zeros((8, 128), F32)
    spare = lax.broadcasted_iota(jnp.int32, (8, 128), 0) >= 6

    def pack(target, c):
        for h in range(64):
            for slot in range(2):
                start = SLOTS[c][h][slot]
                row = 2 + 3 * (16 * (h // 8) + 8 * c + h % 8) + 2 * slot
                last = proj_rows[row : row + 8]
                if start is None:
                    target[h, 56 * slot : 56 * slot + 48] = jnp.zeros((48, 128), BF16)
                else:
                    target[h, 56 * slot : 56 * slot + 48] = sums[start : start + 48].astype(BF16)
                    last = jnp.where(spare, last, sums[start + 48 : start + 56])
                target[h, 56 * slot + 48 : 56 * slot + 56] = last.astype(BF16)

    for me in range(2):

        @pl.when(core[0] == me)
        def _():
            pack(mine, me)
            pack(theirs, 1 - me)


def rows_at(ref, base, offset, rows):
    phase = offset % 8
    start = pl.multiple_of(base + (offset - phase), 8)
    length = rows + (8 if phase else 0)
    return ref[pl.ds(start, length), :][phase : phase + rows].astype(BF16)


def block_grad_kernel(core, cols, grad, mine, theirs, sums):
    for tap, out_row, in_row, rows in conv_rows(1):
        sums[2304 * tap : 2304 * tap + 2304] = dot_tn(
            cols[in_row : in_row + rows, :], grad[out_row : out_row + rows, :]
        )
    sums[6912:6928] = jnp.zeros((16, 256), F32)
    me = core[0]

    def step(g, carry):
        for half in range(2):
            for e in range(8):
                chunk = rows_at(sums, g * 864, 54 * (8 * half + e), 56)

                @pl.when(me == half)
                def _():
                    mine[g, e, 0:56] = chunk[:, 0:128]
                    mine[g, e, 56:112] = chunk[:, 128:256]

                @pl.when(me != half)
                def _():
                    theirs[g, e, 0:56] = chunk[:, 0:128]
                    theirs[g, e, 56:112] = chunk[:, 128:256]

        return carry

    lax.fori_loop(0, 8, step, 0)


def volume_grad_kernel(gp, left, right, up, down, w, grad, ext, acc):
    fill_thin(ext, gp, left, right, up, down)
    acc[...] = jnp.zeros_like(acc)
    for b in range(3):
        for c in range(3):
            k = 256 * (3 * b + c)
            piece = ext[:, 2 - b : 10 - b, 9 - c : 17 - c, :].reshape(256, 256).astype(BF16)
            for tap, in_row, out_row, rows in conv_rows(1):
                acc[out_row : out_row + rows] += dot_nt(
                    piece[in_row : in_row + rows], w[tap, k : k + 256, :]
                )
    grad[...] = acc[...].astype(BF16)


def thin_halo(block, z_even, y_even):
    width = block.shape[-1]
    cells = block.reshape(4, 8, 8, width)
    first, last = cells[:, :, 0], cells[:, :, 7]
    z1 = jnp.where(z_even, last, first)
    z2 = jnp.where(z_even, first, last)
    z1, z2 = both_ways(z1, z2, z_pairs)
    left = jnp.where(z_even, z2, z1)
    right = jnp.where(z_even, z1, z2)

    def strip(y):
        return jnp.concatenate(
            [
                cells[:, y],
                left[:, y : y + 1],
                right[:, y : y + 1],
                jnp.zeros((4, 6, width), block.dtype),
            ],
            axis=1,
        )

    top, bottom = strip(0), strip(7)
    y1 = jnp.where(y_even, bottom, top)
    y2 = jnp.where(y_even, top, bottom)
    y1, y2 = both_ways(y1, y2, y_pairs)
    up = jnp.where(y_even, y2, y1)
    down = jnp.where(y_even, y1, y2)
    return (
        left.reshape(32, width),
        right.reshape(32, width),
        up.reshape(64, width),
        down.reshape(64, width),
    )


def both_ways(first, second, pairs):
    first = swap(first, pairs(0))
    second = swap(second, pairs(1))
    return first, second


def to_owners(chunks):
    return lax.all_to_all(chunks, ("z", "yh", "yl", "x"), 0, 0, tiled=True)


def step(volume, block_weight, aspp_weight, proj_weight, cotangent):
    core = lax.axis_index("c")
    z_even = lax.axis_index("x") % 2 == 0
    y_even = core == 0
    parity = jnp.stack([z_even.astype(jnp.int32), y_even.astype(jnp.int32)])
    core = core.astype(jnp.int32).reshape(1)
    core_pairs = y_pairs(0)

    v = volume.reshape(256, 256)
    w = block_weight.reshape(3, 2304, 256)
    wa = aspp_weight.reshape(9, 2304, 128)
    cot = cotangent.reshape(256, 128)

    thin = thin_halo(v, z_even, y_even)
    hidden, pre, cols = call(
        block_kernel,
        (shape((256, 256), BF16), shape((256, 256), F32), shape((256, 2304), BF16)),
        [WHOLE] * 5 + [STORED],
        [
            pltpu.VMEM((4, 10, 24, 256), F32),
            pltpu.VMEM((3, 2304, 256), BF16),
            pltpu.SemaphoreType.DMA((3,)),
        ],
    )(v, *thin, w)

    cells = shape((4, 8, 8, 384), F32)
    message = shape((448, 128), BF16)
    weights = [pltpu.VMEM((5, 2304, 128), BF16)]
    dma = [pltpu.SemaphoreType.DMA((3,))]
    z1, z2 = both_ways(hidden, hidden, z_pairs)
    h1, h2 = both_ways(hidden, hidden, y_pairs)
    own, sent1, sent2 = call(
        row_kernel,
        (cells, message, message),
        [SCALAR] + [WHOLE] * 3 + [STORED],
        [
            pltpu.VMEM((3, 256, 256), BF16),
            pltpu.VMEM((4, 8, 24, 256), F32),
            pltpu.VMEM((3, 256, 768), BF16),
            *weights,
            pltpu.VMEM((4, 8, 8, 128), F32),
            *dma,
        ],
    )(parity, hidden, z1, z2, wa)
    y1, y2 = both_ways(sent1, sent2, y_pairs)
    out, joint, gproj = call(
        branch_kernel,
        (shape((256, 128), BF16), shape((256, 384), BF16), shape((384, 128), F32)),
        [SCALAR] + [WHOLE] * 5,
        [pltpu.VMEM((4, 8, 8, 384), F32)],
        leaves=(0,),
    )(parity, own, y1, y2, proj_weight, cot)

    z1, z2 = both_ways(joint, joint, z_pairs)
    unit = shape((64, 112, 128), BF16)
    aspp_mine, aspp_theirs, grads = call(
        aspp_grad_kernel,
        (unit, unit, shape((256, 1152), BF16)),
        [SCALAR] * 2 + [WHOLE] * 7,
        [
            pltpu.VMEM((3, 256, 256), BF16),
            pltpu.VMEM((3, 256, 384), BF16),
            pltpu.VMEM((4, 8, 24, 128), F32),
            pltpu.VMEM((256, 768), BF16),
            pltpu.VMEM((768, 384), F32),
            pltpu.VMEM((20752, 128), F32),
            pltpu.VMEM((400, 128), F32),
        ],
    )(core, parity, hidden, h1, h2, joint, z1, z2, gproj)
    aspp_other = swap(aspp_theirs, core_pairs)
    own, sent1, sent2 = call(
        spread_kernel,
        (shape((4, 8, 8, 256), F32), shape((256, 256), BF16), shape((256, 256), BF16)),
        [SCALAR, WHOLE, STORED],
        [
            *weights,
            pltpu.VMEM((4, 8, 8, 256), F32),
            pltpu.VMEM((4, 8, 8, 256), F32),
            pltpu.VMEM((4, 8, 8, 256), F32),
            *dma,
        ],
    )(parity, grads, wa)
    y1, y2 = both_ways(sent1, sent2, y_pairs)
    aspp_part = (aspp_mine.astype(F32) + aspp_other.astype(F32)).astype(BF16)
    aspp_got = to_owners(aspp_part)

    grad_hidden = own.reshape(256, 256) + (y1.astype(F32) + y2.astype(F32))
    grad_pre = (grad_hidden * slope(pre)).astype(BF16)

    unit = shape((8, 8, 112, 128), BF16)
    block_mine, block_theirs = call(
        block_grad_kernel,
        (unit, unit),
        [SCALAR] + [WHOLE] * 2,
        [pltpu.VMEM((6928, 256), F32)],
    )(core, cols, grad_pre)
    block_other = swap(block_theirs, core_pairs)

    block_part = (block_mine.astype(F32) + block_other.astype(F32)).astype(BF16)
    block_got = to_owners(block_part.reshape(64, 112, 128))

    thin = thin_halo(grad_pre, z_even, y_even)
    (grad_volume,) = call(
        volume_grad_kernel,
        (shape((256, 256), BF16),),
        [WHOLE] * 6,
        [pltpu.VMEM((4, 10, 24, 256), F32), pltpu.VMEM((256, 256), F32)],
        leaves=(0,),
    )(grad_pre, *thin, w)

    share = jnp.sum(aspp_got.astype(F32), axis=0)
    third = swap(share[0:54], FORWARDS[0]) + swap(share[56:110], FORWARDS[1])
    place_of = lax.axis_index(ALL)
    owner = jnp.any(place_of == jnp.array(OWNERS, jnp.int32))
    aspp_share = jnp.concatenate([share[0:54], share[56:110], third])
    aspp_share = jnp.where(owner, aspp_share, 0.0).reshape(20736)
    proj_share = jnp.concatenate([share[54:56], share[110:111]]).reshape(384)
    share = jnp.sum(block_got.astype(F32), axis=0)
    block_share = jnp.concatenate([share[0:54], share[56:110]], axis=1).reshape(13824)
    return (
        out.reshape(4, 8, 8, 128),
        grad_volume.reshape(4, 8, 8, 256),
        block_share,
        aspp_share,
        proj_share,
    )


def solution(mesh):
    fine = Mesh(mesh.devices.reshape(4, 2, 2, 2, 4), ALL)
    cells = P(None, ("z", "yh", "c"), ("yl", "x"), None)
    flat = P(ALL)
    return jax.shard_map(
        step,
        mesh=fine,
        in_specs=(cells, P(), P(), P(), cells),
        out_specs=(cells, cells, flat, flat, flat),
        check_vma=False,
    )
```

```python
import jax
import jax.numpy as jnp
from jax import lax
from jax.experimental import pallas as pl
from jax.experimental.pallas import tpu as pltpu
from jax.sharding import Mesh
from jax.sharding import PartitionSpec as P

ALL = ("z", "yh", "c", "yl", "x")
F32 = jnp.float32
BF16 = jnp.bfloat16
VLIM = 24 * 1024 * 1024
WHOLE = pl.BlockSpec(memory_space=pltpu.VMEM)
STORED = pl.BlockSpec(memory_space=pltpu.HBM)
SCALAR = pl.BlockSpec(memory_space=pltpu.SMEM)


def z_pairs(odd):
    pairs = []
    for gy in range(16):
        for gz in range(8):
            other = ((gz - odd) ^ 1) + odd
            if 0 <= other < 8:
                pairs.append((gy * 8 + gz, gy * 8 + other))
    return pairs


def y_pairs(odd):
    pairs = []
    for gy in range(16):
        for gz in range(8):
            other = ((gy - odd) ^ 1) + odd
            if 0 <= other < 16:
                pairs.append((gy * 8 + gz, other * 8 + gz))
    return pairs


def swap(value, pairs):
    return lax.ppermute(value, ALL, pairs)


def sigmoid(v):
    return 1.0 / (1.0 + jnp.exp(-v))


def slope(v):
    s = sigmoid(v)
    return s * (1.0 + v * (1.0 - s))


def call(body, outs, specs, scratch=(), leaves=()):
    kernel = pl.pallas_call(
        body,
        out_shape=tuple(
            o if i in leaves else pltpu.VMEM(o.shape, o.dtype) for i, o in enumerate(outs)
        ),
        in_specs=specs,
        out_specs=jax.tree.map(lambda _: WHOLE, outs),
        scratch_shapes=list(scratch),
        compiler_params=pltpu.CompilerParams(vmem_limit_bytes=VLIM),
        cost_estimate=pl.CostEstimate(flops=10**9, bytes_accessed=10**7, transcendentals=0),
    )

    def run(*args):
        args = [
            arg if spec is SCALAR else pltpu.with_memory_space_constraint(arg, spec.memory_space)
            for arg, spec in zip(args, specs)
        ]
        return kernel(*args)

    return run


def shape(dims, kind):
    return jax.ShapeDtypeStruct(dims, kind)


def fill_thin(ext, block, left, right, up, down, ready=None):
    left_f = left[...].astype(F32)
    right_f = right[...].astype(F32)
    for x in range(4):
        for y in range(8):
            ext[x, 1 + y, 7:8, :] = left_f[8 * x + y : 8 * x + y + 1]
            ext[x, 1 + y, 16:17, :] = right_f[8 * x + y : 8 * x + y + 1]
    for row, strip in ((0, up), (9, down)):
        s = strip[...].astype(F32)
        for x in range(4):
            ext[x, row, 8:16, :] = s[16 * x : 16 * x + 8]
            ext[x, row, 7:8, :] = s[16 * x + 8 : 16 * x + 9]
            ext[x, row, 16:17, :] = s[16 * x + 9 : 16 * x + 10]
    if ready is not None:
        ready.wait()
    width = block.shape[-1]
    ext[:, 1:9, 8:16, :] = block[...].astype(F32).reshape(4, 8, 8, width)


def conv_rows(step):
    spans = []
    for tap in range(3):
        move = step * (tap - 1)
        start = max(0, -move)
        count = 4 - abs(move)
        if count > 0:
            spans.append((tap, 64 * start, 64 * (start + move), 64 * count))
    return spans


def dot_nn(a, b):
    return lax.dot_general(a, b, (((1,), (0,)), ((), ())), preferred_element_type=F32)


def dot_nt(a, b):
    return lax.dot_general(a, b, (((1,), (1,)), ((), ())), preferred_element_type=F32)


def dot_tn(a, b):
    return lax.dot_general(a, b, (((0,), (0,)), ((), ())), preferred_element_type=F32)


def block_kernel(volume, left, right, up, down, weights, hidden, pre, cols, ext, v, w, sems):
    ready = pltpu.make_async_copy(volume, v, sems.at[3])
    ready.start()
    copies = [pltpu.make_async_copy(weights.at[a], w.at[a], sems.at[a]) for a in range(3)]
    for a in (1, 0, 2):
        copies[a].start()
    fill_thin(ext, v, left, right, up, down, ready)
    for b in range(3):
        for c in range(3):
            k = 3 * b + c
            cols[:, 256 * k : 256 * k + 256] = (
                ext[:, b : b + 8, 7 + c : 15 + c, :].reshape(256, 256).astype(BF16)
            )
    copies[1].wait()
    pre[...] = dot_nn(cols[...], w[1])
    for tap, out_row, in_row, rows in conv_rows(1):
        if tap != 1:
            copies[tap].wait()
            pre[out_row : out_row + rows] += dot_nn(cols[in_row : in_row + rows], w[tap])
    value = pre[...]
    hidden[...] = (value * sigmoid(value)).astype(BF16)


def start_weights(source, target, sems):
    copies = [
        pltpu.make_async_copy(source.at[pl.ds(0, 3)], target.at[pl.ds(0, 3)], sems.at[0]),
        pltpu.make_async_copy(source.at[pl.ds(4, 1)], target.at[pl.ds(3, 1)], sems.at[1]),
        pltpu.make_async_copy(source.at[pl.ds(7, 1)], target.at[pl.ds(4, 1)], sems.at[2]),
    ]
    for copy in reversed(copies):
        copy.start()
    return copies


def line_up(even, own, first, second, line):
    after = 2 * even
    line[1] = own[...]
    line[after] = first[...]
    line[2 - after] = second[...]


def widen(line, lanes, ext):
    width = ext.shape[-1]
    for zi in range(3):
        part = line[zi, :, lanes : lanes + width].astype(F32)
        ext[:, :, 8 * zi : 8 * zi + 8, :] = part.reshape(4, 8, 8, width)


def window(line, ext, lanes, move):
    width = ext.shape[-1]
    if move % 8 == 0:
        return line[1 + move // 8, :, lanes : lanes + width]
    return ext[:, :, 8 + move : 16 + move, :].reshape(256, width).astype(BF16)


RATES = (2, 4, 8)
ROWS_SENT = ((384, 448), (256, 384), (0, 256))


def row_kernel(parity, hidden, z1, z2, weights, pre, sent1, sent2, line, ext, cols, w, part, sems):
    copies = start_weights(weights, w, sems)
    line_up(parity[0], hidden, z1, z2, line)
    widen(line, 0, ext)
    for i, rate in enumerate(RATES):
        for c in range(3):
            cols[i, :, 256 * c : 256 * c + 256] = window(line, ext, 0, rate * (c - 1))
    y_even = parity[1] == 1
    for i, rate in reversed(list(enumerate(RATES))):
        copies[i].wait()
        out = slice(128 * i, 128 * i + 128)
        for b in (1, 0, 2):
            taps = slice(768 * b, 768 * b + 768)
            if rate == 2:
                part[...] = dot_nn(cols[i], w[1, taps]).reshape(4, 8, 8, 128)
                for a, out_row, in_row, rows in conv_rows(2):
                    if a != 1:
                        layers = slice(out_row // 64, (out_row + rows) // 64)
                        part[layers] += dot_nn(cols[i, in_row : in_row + rows], w[a, taps]).reshape(
                            rows // 64, 8, 8, 128
                        )
            else:
                part[...] = dot_nn(cols[i], w[2 + i, taps]).reshape(4, 8, 8, 128)
            lo, hi = ROWS_SENT[i]
            if b == 1:
                pre[:, :, :, out] = part[...]
            elif b == 0:
                if rate < 8:
                    pre[:, rate:8, :, out] += part[:, 0 : 8 - rate]
                message = part[:, 8 - rate : 8].reshape(32 * rate, 128).astype(BF16)

                @pl.when(y_even)
                def _():
                    sent1[lo:hi] = message

                @pl.when(jnp.logical_not(y_even))
                def _():
                    sent2[lo:hi] = message
            else:
                if rate < 8:
                    pre[:, 0 : 8 - rate, :, out] += part[:, rate:8]
                message = part[:, 0:rate].reshape(32 * rate, 128).astype(BF16)

                @pl.when(y_even)
                def _():
                    sent2[lo:hi] = message

                @pl.when(jnp.logical_not(y_even))
                def _():
                    sent1[lo:hi] = message


def branch_kernel(parity, own, y1, y2, proj, cot, out, joint, gproj, pre):
    pre[...] = own[...]

    def add(before, after):
        for i, rate in enumerate(RATES):
            lo, hi = ROWS_SENT[i]
            lanes = slice(128 * i, 128 * i + 128)
            pre[:, 0:rate, :, lanes] += before[lo:hi].astype(F32).reshape(4, rate, 8, 128)
            pre[:, 8 - rate : 8, :, lanes] += after[lo:hi].astype(F32).reshape(4, rate, 8, 128)

    @pl.when(parity[1] == 1)
    def _():
        add(y2, y1)

    @pl.when(parity[1] == 0)
    def _():
        add(y1, y2)

    value = pre[...].reshape(256, 384)
    joined = (value * sigmoid(value)).astype(BF16)
    out[...] = dot_nn(joined, proj[...]).astype(BF16)
    gproj[...] = dot_tn(joined, cot[...])
    back = dot_nt(cot[...], proj[...])
    joint[...] = (back * slope(value)).astype(BF16)


def spread_kernel(parity, cols, weights, own, sent1, sent2, w, part, up, down, sems):
    copies = start_weights(weights, w, sems)
    for b in range(3):
        for i, rate in reversed(list(enumerate(RATES))):
            if b == 0:
                copies[i].wait()
            for c in range(3):
                at = 384 * i + 128 * c
                tap = slice(768 * b + 256 * c, 768 * b + 256 * c + 256)
                if rate == 2:
                    term = dot_nt(cols[:, at : at + 128], w[1, tap])
                else:
                    term = dot_nt(cols[:, at : at + 128], w[2 + i, tap])
                term = term.reshape(4, 8, 8, 256)
                if c == 0:
                    part[...] = term
                else:
                    part[...] += term
                if rate == 2:
                    for a, in_row, out_row, rows in conv_rows(2):
                        if a != 1:
                            layers = slice(out_row // 64, (out_row + rows) // 64)
                            part[layers] += dot_nt(
                                cols[in_row : in_row + rows, at : at + 128], w[a, tap]
                            ).reshape(rows // 64, 8, 8, 256)
            if b == 1:
                own[...] += part[...]
            elif b == 0:
                if rate == 8:
                    up[...] = part[...]
                    own[...] = jnp.zeros_like(own)
                else:
                    own[:, 0 : 8 - rate] += part[:, rate:8]
                    up[:, 8 - rate : 8] += part[:, 0:rate]
            else:
                if rate == 8:
                    down[...] = part[...]
                else:
                    own[:, rate:8] += part[:, 0 : 8 - rate]
                    down[:, 0:rate] += part[:, 8 - rate : 8]
    y_even = parity[1] == 1
    up_message = up[...].reshape(256, 256).astype(BF16)
    down_message = down[...].reshape(256, 256).astype(BF16)

    @pl.when(y_even)
    def _():
        sent1[...] = down_message
        sent2[...] = up_message

    @pl.when(jnp.logical_not(y_even))
    def _():
        sent1[...] = up_message
        sent2[...] = down_message


def vanishing(row):
    tap = row // 256
    return tap >= 27 and (tap % 27) // 9 != 1


def share_plan():
    starts, forwards = [], ([], [])
    owners = []
    for c in range(2):
        device = [16 * (h // 8) + 8 * c + h % 8 for h in range(64)]
        full = [h for h in range(64) if not all(vanishing(162 * device[h] + r) for r in range(162))]
        spare = [h for h in range(64) if h not in full]
        slots = [[None, None] for _ in range(64)]
        for h in full:
            slots[h] = [162 * device[h], 162 * device[h] + 54]
            owners.append(device[h])
        for i, h in enumerate(full):
            slot, helper = divmod(i, len(spare))
            slots[spare[helper]][slot] = 162 * device[h] + 108
            forwards[slot].append((device[spare[helper]], device[h]))
        starts.append(slots)
    return starts, forwards, owners


SLOTS, FORWARDS, OWNERS = share_plan()


def aspp_grad_kernel(
    core, parity, hidden, y1, y2, joint, z1, z2, gproj,
    mine, theirs, cols, line, near, ext, left, block, sums, proj_rows,
):
    line_up(parity[0], joint, z1, z2, near)
    for i, rate in enumerate(RATES):
        if rate < 8:
            widen(near, 128 * i, ext)
        for c in range(3):
            at = 384 * i + 128 * c
            cols[:, at : at + 128] = window(near, ext, 128 * i, -rate * (c - 1))
    line_up(parity[1], hidden, y1, y2, line)
    for i, rate in enumerate(RATES):
        cut = 8 * rate
        for b in range(3):
            lanes = slice(256 * b, 256 * b + 256)
            if b == 1 or rate == 8:
                left[:, lanes] = line[b]
                continue
            for x in range(0, 256, 64):
                if b == 0:
                    left[x : x + cut, lanes] = line[0, x + 64 - cut : x + 64]
                    left[x + cut : x + 64, lanes] = line[1, x : x + 64 - cut]
                else:
                    left[x : x + 64 - cut, lanes] = line[1, x + cut : x + 64]
                    left[x + 64 - cut : x + 64, lanes] = line[2, x : x + cut]
        for a, out_row, in_row, rows in conv_rows(2 if i == 0 else 4):
            block[...] = dot_tn(
                left[in_row : in_row + rows, :],
                cols[out_row : out_row + rows, 384 * i : 384 * i + 384],
            )
            for b in range(3):
                for c in range(3):
                    at = 256 * (27 * i + 9 * a + 3 * b + c)
                    sums[at : at + 256] = block[256 * b : 256 * b + 256, 128 * c : 128 * c + 128]
    for unit in OWNERS:
        for row in range(162 * unit // 8 * 8, 162 * unit + 168, 8):
            if vanishing(row):
                sums[row : row + 8] = jnp.zeros((8, 128), F32)
    proj_rows[0:8] = jnp.zeros((8, 128), F32)
    proj_rows[8:392] = gproj[...]
    proj_rows[392:400] = jnp.zeros((8, 128), F32)
    spare = lax.broadcasted_iota(jnp.int32, (8, 128), 0) >= 6

    def pack(target, c):
        for h in range(64):
            for slot in range(2):
                start = SLOTS[c][h][slot]
                row = 2 + 3 * (16 * (h // 8) + 8 * c + h % 8) + 2 * slot
                last = proj_rows[row : row + 8]
                if start is None:
                    target[h, 56 * slot : 56 * slot + 48] = jnp.zeros((48, 128), BF16)
                else:
                    target[h, 56 * slot : 56 * slot + 48] = sums[start : start + 48].astype(BF16)
                    last = jnp.where(spare, last, sums[start + 48 : start + 56])
                target[h, 56 * slot + 48 : 56 * slot + 56] = last.astype(BF16)

    for me in range(2):

        @pl.when(core[0] == me)
        def _():
            pack(mine, me)
            pack(theirs, 1 - me)


def rows_at(ref, base, offset, rows):
    phase = offset % 8
    start = pl.multiple_of(base + (offset - phase), 8)
    length = rows + (8 if phase else 0)
    return ref[pl.ds(start, length), :][phase : phase + rows].astype(BF16)


def block_grad_kernel(core, cols, grad, mine, theirs, sums):
    for tap, out_row, in_row, rows in conv_rows(1):
        sums[2304 * tap : 2304 * tap + 2304] = dot_tn(
            cols[in_row : in_row + rows, :], grad[out_row : out_row + rows, :]
        )
    sums[6912:6928] = jnp.zeros((16, 256), F32)
    me = core[0]

    def step(g, carry):
        for half in range(2):
            for e in range(8):
                chunk = rows_at(sums, g * 864, 54 * (8 * half + e), 56)

                @pl.when(me == half)
                def _():
                    mine[g, e, 0:56] = chunk[:, 0:128]
                    mine[g, e, 56:112] = chunk[:, 128:256]

                @pl.when(me != half)
                def _():
                    theirs[g, e, 0:56] = chunk[:, 0:128]
                    theirs[g, e, 56:112] = chunk[:, 128:256]

        return carry

    lax.fori_loop(0, 8, step, 0)


def finish_kernel(
    owner, got, share, third1, third2, block_share, aspp_share, parts, own, add1, add2, sems
):
    moves = ((got, parts), (share, own), (third1, add1), (third2, add2))
    copies = [pltpu.make_async_copy(a, b, sems.at[i]) for i, (a, b) in enumerate(moves)]
    for copy in copies:
        copy.start()
    for copy in copies[1:]:
        copy.wait()
    keep = owner[0] == 1
    aspp_share[0:54] = jnp.where(keep, own[0:54], 0.0)
    aspp_share[54:108] = jnp.where(keep, own[56:110], 0.0)
    aspp_share[108:162] = jnp.where(keep, add1[...] + add2[...], 0.0)
    copies[0].wait()
    total = parts[0].astype(F32)
    for source in range(1, 64):
        total += parts[source].astype(F32)
    block_share[pl.ds(0, 54, stride=2), :] = total[0:54]
    block_share[pl.ds(1, 54, stride=2), :] = total[56:110]


def volume_grad_kernel(gp, left, right, up, down, w, grad, ext, acc):
    fill_thin(ext, gp, left, right, up, down)
    acc[...] = jnp.zeros_like(acc)
    for b in range(3):
        for c in range(3):
            k = 256 * (3 * b + c)
            piece = ext[:, 2 - b : 10 - b, 9 - c : 17 - c, :].reshape(256, 256).astype(BF16)
            for tap, in_row, out_row, rows in conv_rows(1):
                acc[out_row : out_row + rows] += dot_nt(
                    piece[in_row : in_row + rows], w[tap, k : k + 256, :]
                )
    grad[...] = acc[...].astype(BF16)


def thin_halo(block, z_even, y_even):
    width = block.shape[-1]
    cells = block.reshape(4, 8, 8, width)
    first, last = cells[:, :, 0], cells[:, :, 7]
    z1 = jnp.where(z_even, last, first)
    z2 = jnp.where(z_even, first, last)
    z1, z2 = both_ways(z1, z2, z_pairs)
    left = jnp.where(z_even, z2, z1)
    right = jnp.where(z_even, z1, z2)

    def strip(y):
        return jnp.concatenate(
            [
                cells[:, y],
                left[:, y : y + 1],
                right[:, y : y + 1],
                jnp.zeros((4, 6, width), block.dtype),
            ],
            axis=1,
        )

    top, bottom = strip(0), strip(7)
    y1 = jnp.where(y_even, bottom, top)
    y2 = jnp.where(y_even, top, bottom)
    y1, y2 = both_ways(y1, y2, y_pairs)
    up = jnp.where(y_even, y2, y1)
    down = jnp.where(y_even, y1, y2)
    return (
        left.reshape(32, width),
        right.reshape(32, width),
        up.reshape(64, width),
        down.reshape(64, width),
    )


def both_ways(first, second, pairs):
    first = swap(first, pairs(0))
    second = swap(second, pairs(1))
    return first, second


def to_owners(chunks):
    return lax.all_to_all(chunks, ("z", "yh", "yl", "x"), 0, 0, tiled=True)


def step(volume, block_weight, aspp_weight, proj_weight, cotangent):
    core = lax.axis_index("c")
    z_even = lax.axis_index("x") % 2 == 0
    y_even = core == 0
    parity = jnp.stack([z_even.astype(jnp.int32), y_even.astype(jnp.int32)])
    core = core.astype(jnp.int32).reshape(1)
    core_pairs = y_pairs(0)

    v = volume.reshape(256, 256)
    w = block_weight.reshape(3, 2304, 256)
    wa = aspp_weight.reshape(9, 2304, 128)
    cot = cotangent.reshape(256, 128)

    thin = thin_halo(v, z_even, y_even)
    hidden, pre, cols = call(
        block_kernel,
        (shape((256, 256), BF16), shape((256, 256), F32), shape((256, 2304), BF16)),
        [STORED] + [WHOLE] * 4 + [STORED],
        [
            pltpu.VMEM((4, 10, 24, 256), F32),
            pltpu.VMEM((256, 256), BF16),
            pltpu.VMEM((3, 2304, 256), BF16),
            pltpu.SemaphoreType.DMA((4,)),
        ],
    )(v, *thin, w)

    cells = shape((4, 8, 8, 384), F32)
    message = shape((448, 128), BF16)
    weights = [pltpu.VMEM((5, 2304, 128), BF16)]
    dma = [pltpu.SemaphoreType.DMA((3,))]
    z1, z2 = both_ways(hidden, hidden, z_pairs)
    h1, h2 = both_ways(hidden, hidden, y_pairs)
    own, sent1, sent2 = call(
        row_kernel,
        (cells, message, message),
        [SCALAR] + [WHOLE] * 3 + [STORED],
        [
            pltpu.VMEM((3, 256, 256), BF16),
            pltpu.VMEM((4, 8, 24, 256), F32),
            pltpu.VMEM((3, 256, 768), BF16),
            *weights,
            pltpu.VMEM((4, 8, 8, 128), F32),
            *dma,
        ],
    )(parity, hidden, z1, z2, wa)
    y1, y2 = both_ways(sent1, sent2, y_pairs)
    out, joint, gproj = call(
        branch_kernel,
        (shape((256, 128), BF16), shape((256, 384), BF16), shape((384, 128), F32)),
        [SCALAR] + [WHOLE] * 5,
        [pltpu.VMEM((4, 8, 8, 384), F32)],
        leaves=(0,),
    )(parity, own, y1, y2, proj_weight, cot)

    z1, z2 = both_ways(joint, joint, z_pairs)
    unit = shape((64, 112, 128), BF16)
    aspp_mine, aspp_theirs, grads = call(
        aspp_grad_kernel,
        (unit, unit, shape((256, 1152), BF16)),
        [SCALAR] * 2 + [WHOLE] * 7,
        [
            pltpu.VMEM((3, 256, 256), BF16),
            pltpu.VMEM((3, 256, 384), BF16),
            pltpu.VMEM((4, 8, 24, 128), F32),
            pltpu.VMEM((256, 768), BF16),
            pltpu.VMEM((768, 384), F32),
            pltpu.VMEM((20752, 128), F32),
            pltpu.VMEM((400, 128), F32),
        ],
    )(core, parity, hidden, h1, h2, joint, z1, z2, gproj)
    aspp_other = swap(aspp_theirs, core_pairs)
    own, sent1, sent2 = call(
        spread_kernel,
        (shape((4, 8, 8, 256), F32), shape((256, 256), BF16), shape((256, 256), BF16)),
        [SCALAR, WHOLE, STORED],
        [
            *weights,
            pltpu.VMEM((4, 8, 8, 256), F32),
            pltpu.VMEM((4, 8, 8, 256), F32),
            pltpu.VMEM((4, 8, 8, 256), F32),
            *dma,
        ],
    )(parity, grads, wa)
    y1, y2 = both_ways(sent1, sent2, y_pairs)
    aspp_part = (aspp_mine.astype(F32) + aspp_other.astype(F32)).astype(BF16)
    aspp_got = to_owners(aspp_part)

    grad_hidden = own.reshape(256, 256) + (y1.astype(F32) + y2.astype(F32))
    grad_pre = (grad_hidden * slope(pre)).astype(BF16)

    unit = shape((8, 8, 112, 128), BF16)
    block_mine, block_theirs = call(
        block_grad_kernel,
        (unit, unit),
        [SCALAR] + [WHOLE] * 2,
        [pltpu.VMEM((6928, 256), F32)],
    )(core, cols, grad_pre)
    block_other = swap(block_theirs, core_pairs)

    block_part = (block_mine.astype(F32) + block_other.astype(F32)).astype(BF16)
    block_got = to_owners(block_part.reshape(64, 112, 128))

    thin = thin_halo(grad_pre, z_even, y_even)
    share = jnp.sum(aspp_got.astype(F32), axis=0)
    third1 = swap(share[0:54], FORWARDS[0])
    third2 = swap(share[56:110], FORWARDS[1])
    place_of = lax.axis_index(ALL)
    owner = jnp.any(place_of == jnp.array(OWNERS, jnp.int32)).astype(jnp.int32).reshape(1)
    (grad_volume,) = call(
        volume_grad_kernel,
        (shape((256, 256), BF16),),
        [WHOLE] * 6,
        [pltpu.VMEM((4, 10, 24, 256), F32), pltpu.VMEM((256, 256), F32)],
        leaves=(0,),
    )(grad_pre, *thin, w)
    block_share, aspp_share = call(
        finish_kernel,
        (shape((108, 128), F32), shape((162, 128), F32)),
        [SCALAR] + [STORED] * 4,
        [
            pltpu.VMEM((64, 112, 128), BF16),
            pltpu.VMEM((112, 128), F32),
            pltpu.VMEM((54, 128), F32),
            pltpu.VMEM((54, 128), F32),
            pltpu.SemaphoreType.DMA((4,)),
        ],
        leaves=(0, 1),
    )(owner, block_got, share, third1, third2)
    proj_share = jnp.concatenate([share[54:56], share[110:111]]).reshape(384)
    return (
        out.reshape(4, 8, 8, 128),
        grad_volume.reshape(4, 8, 8, 256),
        block_share.reshape(13824),
        aspp_share.reshape(20736),
        proj_share,
    )


def solution(mesh):
    fine = Mesh(mesh.devices.reshape(4, 2, 2, 2, 4), ALL)
    cells = P(None, ("z", "yh", "c"), ("yl", "x"), None)
    flat = P(ALL)
    return jax.shard_map(
        step,
        mesh=fine,
        in_specs=(cells, P(), P(), P(), cells),
        out_specs=(cells, cells, flat, flat, flat),
        check_vma=False,
    )
```

```python
import jax
import jax.numpy as jnp
from jax import lax
from jax.experimental import pallas as pl
from jax.experimental.pallas import tpu as pltpu
from jax.sharding import Mesh
from jax.sharding import PartitionSpec as P

ALL = ("z", "yh", "c", "yl", "x")
F32 = jnp.float32
BF16 = jnp.bfloat16
VLIM = 24 * 1024 * 1024
WHOLE = pl.BlockSpec(memory_space=pltpu.VMEM)
STORED = pl.BlockSpec(memory_space=pltpu.HBM)
SCALAR = pl.BlockSpec(memory_space=pltpu.SMEM)


def z_pairs(odd):
    pairs = []
    for gy in range(16):
        for gz in range(8):
            other = ((gz - odd) ^ 1) + odd
            if 0 <= other < 8:
                pairs.append((gy * 8 + gz, gy * 8 + other))
    return pairs


def y_pairs(odd):
    pairs = []
    for gy in range(16):
        for gz in range(8):
            other = ((gy - odd) ^ 1) + odd
            if 0 <= other < 16:
                pairs.append((gy * 8 + gz, other * 8 + gz))
    return pairs


def swap(value, pairs):
    return lax.ppermute(value, ALL, pairs)


def sigmoid(v):
    return 1.0 / (1.0 + jnp.exp(-v))


def slope(v):
    s = sigmoid(v)
    return s * (1.0 + v * (1.0 - s))


def call(body, outs, specs, scratch=(), leaves=()):
    kernel = pl.pallas_call(
        body,
        out_shape=tuple(
            o if i in leaves else pltpu.VMEM(o.shape, o.dtype) for i, o in enumerate(outs)
        ),
        in_specs=specs,
        out_specs=jax.tree.map(lambda _: WHOLE, outs),
        scratch_shapes=list(scratch),
        compiler_params=pltpu.CompilerParams(vmem_limit_bytes=VLIM),
        cost_estimate=pl.CostEstimate(flops=10**9, bytes_accessed=10**7, transcendentals=0),
    )

    def run(*args):
        args = [
            arg if spec is SCALAR else pltpu.with_memory_space_constraint(arg, spec.memory_space)
            for arg, spec in zip(args, specs)
        ]
        return kernel(*args)

    return run


def shape(dims, kind):
    return jax.ShapeDtypeStruct(dims, kind)


def fill_thin(ext, block, left, right, up, down, ready=None):
    left_f = left[...].astype(F32)
    right_f = right[...].astype(F32)
    for x in range(4):
        for y in range(8):
            ext[x, 1 + y, 7:8, :] = left_f[8 * x + y : 8 * x + y + 1]
            ext[x, 1 + y, 16:17, :] = right_f[8 * x + y : 8 * x + y + 1]
    for row, strip in ((0, up), (9, down)):
        s = strip[...].astype(F32)
        for x in range(4):
            ext[x, row, 8:16, :] = s[16 * x : 16 * x + 8]
            ext[x, row, 7:8, :] = s[16 * x + 8 : 16 * x + 9]
            ext[x, row, 16:17, :] = s[16 * x + 9 : 16 * x + 10]
    if ready is not None:
        ready.wait()
    width = block.shape[-1]
    ext[:, 1:9, 8:16, :] = block[...].astype(F32).reshape(4, 8, 8, width)


def conv_rows(step):
    spans = []
    for tap in range(3):
        move = step * (tap - 1)
        start = max(0, -move)
        count = 4 - abs(move)
        if count > 0:
            spans.append((tap, 64 * start, 64 * (start + move), 64 * count))
    return spans


def dot_nn(a, b):
    return lax.dot_general(a, b, (((1,), (0,)), ((), ())), preferred_element_type=F32)


def dot_nt(a, b):
    return lax.dot_general(a, b, (((1,), (1,)), ((), ())), preferred_element_type=F32)


def dot_tn(a, b):
    return lax.dot_general(a, b, (((0,), (0,)), ((), ())), preferred_element_type=F32)


def block_kernel(volume, left, right, up, down, weights, hidden, pre, cols, ext, v, w, sems):
    ready = pltpu.make_async_copy(volume, v, sems.at[3])
    ready.start()
    copies = [pltpu.make_async_copy(weights.at[a], w.at[a], sems.at[a]) for a in range(3)]
    for a in (1, 0, 2):
        copies[a].start()
    fill_thin(ext, v, left, right, up, down, ready)
    for b in range(3):
        for c in range(3):
            k = 3 * b + c
            cols[:, 256 * k : 256 * k + 256] = (
                ext[:, b : b + 8, 7 + c : 15 + c, :].reshape(256, 256).astype(BF16)
            )
    copies[1].wait()
    pre[...] = dot_nn(cols[...], w[1])
    for tap, out_row, in_row, rows in conv_rows(1):
        if tap != 1:
            copies[tap].wait()
            pre[out_row : out_row + rows] += dot_nn(cols[in_row : in_row + rows], w[tap])
    value = pre[...]
    hidden[...] = (value * sigmoid(value)).astype(BF16)


GROUPS = ((0, 3, 0), (4, 1, 3), (7, 1, 4))


def start_weights(source, target, sems, by_row):
    copies = []
    for i, (start, count, at) in enumerate(GROUPS):
        group = []
        for k in range(3):
            taps = source.at[pl.ds(start, count)]
            taps = taps.at[:, k] if by_row else taps.at[:, :, k]
            place = target.at[pl.ds(at, count), :, :, pl.ds(128 * k, 128)]
            group.append(pltpu.make_async_copy(taps, place, sems.at[i, k]))
        copies.append(group)
    for group in reversed(copies):
        for copy in group:
            copy.start()
    return copies


def wait_all(group):
    for copy in group:
        copy.wait()


def line_up(even, own, first, second, line):
    after = 2 * even
    line[1] = own[...]
    line[after] = first[...]
    line[2 - after] = second[...]


def widen(line, lanes, ext):
    width = ext.shape[-1]
    for zi in range(3):
        part = line[zi, :, lanes : lanes + width].astype(F32)
        ext[:, :, 8 * zi : 8 * zi + 8, :] = part.reshape(4, 8, 8, width)


def window(line, ext, lanes, move):
    width = ext.shape[-1]
    if move % 8 == 0:
        return line[1 + move // 8, :, lanes : lanes + width]
    return ext[:, :, 8 + move : 16 + move, :].reshape(256, width).astype(BF16)


RATES = (2, 4, 8)
ROWS_SENT = ((384, 448), (256, 384), (0, 256))


def row_kernel(parity, hidden, z1, z2, weights, pre, sent1, sent2, line, ext, cols, w, total, sems):
    copies = start_weights(weights, w, sems, True)
    line_up(parity[0], hidden, z1, z2, line)
    widen(line, 0, ext)
    for i, rate in enumerate(RATES):
        for c in range(3):
            cols[i, :, 256 * c : 256 * c + 256] = window(line, ext, 0, rate * (c - 1))
    y_even = parity[1] == 1
    for i, rate in reversed(list(enumerate(RATES))):
        wait_all(copies[i])
        out = slice(128 * i, 128 * i + 128)
        lo, hi = ROWS_SENT[i]
        middle = 1 if rate == 2 else 2 + i
        total[...] = dot_nn(cols[i], w[middle].reshape(768, 384)).reshape(4, 8, 8, 384)
        if rate == 2:
            for a, out_row, in_row, rows in conv_rows(2):
                if a != 1:
                    layers = slice(out_row // 64, (out_row + rows) // 64)
                    term = dot_nn(cols[i, in_row : in_row + rows], w[a].reshape(768, 384))
                    total[layers] += term.reshape(rows // 64, 8, 8, 384)
        pre[:, :, :, out] = total[:, :, :, 128:256]
        if rate < 8:
            pre[:, rate:8, :, out] += total[:, 0 : 8 - rate, :, 0:128]
            pre[:, 0 : 8 - rate, :, out] += total[:, rate:8, :, 256:384]
        down = total[:, 8 - rate : 8, :, 0:128].reshape(32 * rate, 128).astype(BF16)
        up = total[:, 0:rate, :, 256:384].reshape(32 * rate, 128).astype(BF16)

        @pl.when(y_even)
        def _():
            sent1[lo:hi] = down
            sent2[lo:hi] = up

        @pl.when(jnp.logical_not(y_even))
        def _():
            sent1[lo:hi] = up
            sent2[lo:hi] = down


def branch_kernel(parity, own, y1, y2, proj, cot, out, joint, gproj, pre):
    pre[...] = own[...]

    def add(before, after):
        for i, rate in enumerate(RATES):
            lo, hi = ROWS_SENT[i]
            lanes = slice(128 * i, 128 * i + 128)
            pre[:, 0:rate, :, lanes] += before[lo:hi].astype(F32).reshape(4, rate, 8, 128)
            pre[:, 8 - rate : 8, :, lanes] += after[lo:hi].astype(F32).reshape(4, rate, 8, 128)

    @pl.when(parity[1] == 1)
    def _():
        add(y2, y1)

    @pl.when(parity[1] == 0)
    def _():
        add(y1, y2)

    value = pre[...].reshape(256, 384)
    joined = (value * sigmoid(value)).astype(BF16)
    out[...] = dot_nn(joined, proj[...]).astype(BF16)
    gproj[...] = dot_tn(joined, cot[...])
    back = dot_nt(cot[...], proj[...])
    joint[...] = (back * slope(value)).astype(BF16)


def spread_kernel(parity, cols, weights, own, sent1, sent2, w, part, up, down, sems):
    copies = start_weights(weights, w, sems, False)
    for b in range(3):
        for i, rate in reversed(list(enumerate(RATES))):
            if b == 0:
                wait_all(copies[i])
            lanes = slice(384 * i, 384 * i + 384)
            middle = 1 if rate == 2 else 2 + i
            part[...] = dot_nt(cols[:, lanes], w[middle, b]).reshape(4, 8, 8, 256)
            if rate == 2:
                for a, in_row, out_row, rows in conv_rows(2):
                    if a != 1:
                        layers = slice(out_row // 64, (out_row + rows) // 64)
                        term = dot_nt(cols[in_row : in_row + rows, lanes], w[a, b])
                        part[layers] += term.reshape(rows // 64, 8, 8, 256)
            if b == 1:
                own[...] += part[...]
            elif b == 0:
                if rate == 8:
                    up[...] = part[...]
                    own[...] = jnp.zeros_like(own)
                else:
                    own[:, 0 : 8 - rate] += part[:, rate:8]
                    up[:, 8 - rate : 8] += part[:, 0:rate]
            else:
                if rate == 8:
                    down[...] = part[...]
                else:
                    own[:, rate:8] += part[:, 0 : 8 - rate]
                    down[:, 0:rate] += part[:, 8 - rate : 8]
    y_even = parity[1] == 1
    up_message = up[...].reshape(256, 256).astype(BF16)
    down_message = down[...].reshape(256, 256).astype(BF16)

    @pl.when(y_even)
    def _():
        sent1[...] = down_message
        sent2[...] = up_message

    @pl.when(jnp.logical_not(y_even))
    def _():
        sent1[...] = up_message
        sent2[...] = down_message


def vanishing(row):
    tap = row // 256
    return tap >= 27 and (tap % 27) // 9 != 1


def share_plan():
    starts, forwards = [], ([], [])
    owners = []
    for c in range(2):
        device = [16 * (h // 8) + 8 * c + h % 8 for h in range(64)]
        full = [h for h in range(64) if not all(vanishing(162 * device[h] + r) for r in range(162))]
        spare = [h for h in range(64) if h not in full]
        slots = [[None, None] for _ in range(64)]
        for h in full:
            slots[h] = [162 * device[h], 162 * device[h] + 54]
            owners.append(device[h])
        for i, h in enumerate(full):
            slot, helper = divmod(i, len(spare))
            slots[spare[helper]][slot] = 162 * device[h] + 108
            forwards[slot].append((device[spare[helper]], device[h]))
        starts.append(slots)
    return starts, forwards, owners


SLOTS, FORWARDS, OWNERS = share_plan()


def aspp_grad_kernel(
    core, parity, hidden, y1, y2, joint, z1, z2, gproj,
    mine, theirs, cols, line, near, ext, left, block, sums, proj_rows,
):
    line_up(parity[0], joint, z1, z2, near)
    for i, rate in enumerate(RATES):
        if rate < 8:
            widen(near, 128 * i, ext)
        for c in range(3):
            at = 384 * i + 128 * c
            cols[:, at : at + 128] = window(near, ext, 128 * i, -rate * (c - 1))
    line_up(parity[1], hidden, y1, y2, line)
    for i, rate in enumerate(RATES):
        cut = 8 * rate
        for b in range(3):
            lanes = slice(256 * b, 256 * b + 256)
            if b == 1 or rate == 8:
                left[:, lanes] = line[b]
                continue
            for x in range(0, 256, 64):
                if b == 0:
                    left[x : x + cut, lanes] = line[0, x + 64 - cut : x + 64]
                    left[x + cut : x + 64, lanes] = line[1, x : x + 64 - cut]
                else:
                    left[x : x + 64 - cut, lanes] = line[1, x + cut : x + 64]
                    left[x + 64 - cut : x + 64, lanes] = line[2, x : x + cut]
        for a, out_row, in_row, rows in conv_rows(2 if i == 0 else 4):
            block[...] = dot_tn(
                left[in_row : in_row + rows, :],
                cols[out_row : out_row + rows, 384 * i : 384 * i + 384],
            )
            for b in range(3):
                for c in range(3):
                    at = 256 * (27 * i + 9 * a + 3 * b + c)
                    sums[at : at + 256] = block[256 * b : 256 * b + 256, 128 * c : 128 * c + 128]
    for unit in OWNERS:
        for row in range(162 * unit // 8 * 8, 162 * unit + 168, 8):
            if vanishing(row):
                sums[row : row + 8] = jnp.zeros((8, 128), F32)
    proj_rows[0:8] = jnp.zeros((8, 128), F32)
    proj_rows[8:392] = gproj[...]
    proj_rows[392:400] = jnp.zeros((8, 128), F32)
    spare = lax.broadcasted_iota(jnp.int32, (8, 128), 0) >= 6

    def pack(target, c):
        for h in range(64):
            for slot in range(2):
                start = SLOTS[c][h][slot]
                row = 2 + 3 * (16 * (h // 8) + 8 * c + h % 8) + 2 * slot
                last = proj_rows[row : row + 8]
                if start is None:
                    target[h, 56 * slot : 56 * slot + 48] = jnp.zeros((48, 128), BF16)
                else:
                    target[h, 56 * slot : 56 * slot + 48] = sums[start : start + 48].astype(BF16)
                    last = jnp.where(spare, last, sums[start + 48 : start + 56])
                target[h, 56 * slot + 48 : 56 * slot + 56] = last.astype(BF16)

    for me in range(2):

        @pl.when(core[0] == me)
        def _():
            pack(mine, me)
            pack(theirs, 1 - me)


def rows_at(ref, base, offset, rows):
    phase = offset % 8
    start = pl.multiple_of(base + (offset - phase), 8)
    length = rows + (8 if phase else 0)
    return ref[pl.ds(start, length), :][phase : phase + rows].astype(BF16)


def block_grad_kernel(core, cols, grad, mine, theirs, sums):
    for tap, out_row, in_row, rows in conv_rows(1):
        sums[2304 * tap : 2304 * tap + 2304] = dot_tn(
            cols[in_row : in_row + rows, :], grad[out_row : out_row + rows, :]
        )
    sums[6912:6928] = jnp.zeros((16, 256), F32)
    me = core[0]

    def step(g, carry):
        for half in range(2):
            for e in range(8):
                chunk = rows_at(sums, g * 864, 54 * (8 * half + e), 56)

                @pl.when(me == half)
                def _():
                    mine[g, e, 0:56] = chunk[:, 0:128]
                    mine[g, e, 56:112] = chunk[:, 128:256]

                @pl.when(me != half)
                def _():
                    theirs[g, e, 0:56] = chunk[:, 0:128]
                    theirs[g, e, 56:112] = chunk[:, 128:256]

        return carry

    lax.fori_loop(0, 8, step, 0)


def finish_kernel(
    owner, got, share, third1, third2, block_share, aspp_share, parts, own, add1, add2, sems
):
    moves = ((got, parts), (share, own), (third1, add1), (third2, add2))
    copies = [pltpu.make_async_copy(a, b, sems.at[i]) for i, (a, b) in enumerate(moves)]
    for copy in copies:
        copy.start()
    for copy in copies[1:]:
        copy.wait()
    keep = owner[0] == 1
    aspp_share[0:54] = jnp.where(keep, own[0:54], 0.0)
    aspp_share[54:108] = jnp.where(keep, own[56:110], 0.0)
    aspp_share[108:162] = jnp.where(keep, add1[...] + add2[...], 0.0)
    copies[0].wait()
    total = parts[0].astype(F32)
    for source in range(1, 64):
        total += parts[source].astype(F32)
    block_share[pl.ds(0, 54, stride=2), :] = total[0:54]
    block_share[pl.ds(1, 54, stride=2), :] = total[56:110]


def volume_grad_kernel(gp, left, right, up, down, w, grad, ext, acc):
    fill_thin(ext, gp, left, right, up, down)
    acc[...] = jnp.zeros_like(acc)
    for b in range(3):
        for c in range(3):
            k = 256 * (3 * b + c)
            piece = ext[:, 2 - b : 10 - b, 9 - c : 17 - c, :].reshape(256, 256).astype(BF16)
            for tap, in_row, out_row, rows in conv_rows(1):
                acc[out_row : out_row + rows] += dot_nt(
                    piece[in_row : in_row + rows], w[tap, k : k + 256, :]
                )
    grad[...] = acc[...].astype(BF16)


def thin_halo(block, z_even, y_even):
    width = block.shape[-1]
    cells = block.reshape(4, 8, 8, width)
    first, last = cells[:, :, 0], cells[:, :, 7]
    z1 = jnp.where(z_even, last, first)
    z2 = jnp.where(z_even, first, last)
    z1, z2 = both_ways(z1, z2, z_pairs)
    left = jnp.where(z_even, z2, z1)
    right = jnp.where(z_even, z1, z2)

    def strip(y):
        return jnp.concatenate(
            [
                cells[:, y],
                left[:, y : y + 1],
                right[:, y : y + 1],
                jnp.zeros((4, 6, width), block.dtype),
            ],
            axis=1,
        )

    top, bottom = strip(0), strip(7)
    y1 = jnp.where(y_even, bottom, top)
    y2 = jnp.where(y_even, top, bottom)
    y1, y2 = both_ways(y1, y2, y_pairs)
    up = jnp.where(y_even, y2, y1)
    down = jnp.where(y_even, y1, y2)
    return (
        left.reshape(32, width),
        right.reshape(32, width),
        up.reshape(64, width),
        down.reshape(64, width),
    )


def both_ways(first, second, pairs):
    first = swap(first, pairs(0))
    second = swap(second, pairs(1))
    return first, second


def to_owners(chunks):
    return lax.all_to_all(chunks, ("z", "yh", "yl", "x"), 0, 0, tiled=True)


def step(volume, block_weight, aspp_weight, proj_weight, cotangent):
    core = lax.axis_index("c")
    z_even = lax.axis_index("x") % 2 == 0
    y_even = core == 0
    parity = jnp.stack([z_even.astype(jnp.int32), y_even.astype(jnp.int32)])
    core = core.astype(jnp.int32).reshape(1)
    core_pairs = y_pairs(0)

    v = volume.reshape(256, 256)
    w = block_weight.reshape(3, 2304, 256)
    wa = aspp_weight.reshape(9, 3, 3, 256, 128)
    cot = cotangent.reshape(256, 128)

    thin = thin_halo(v, z_even, y_even)
    hidden, pre, cols = call(
        block_kernel,
        (shape((256, 256), BF16), shape((256, 256), F32), shape((256, 2304), BF16)),
        [STORED] + [WHOLE] * 4 + [STORED],
        [
            pltpu.VMEM((4, 10, 24, 256), F32),
            pltpu.VMEM((256, 256), BF16),
            pltpu.VMEM((3, 2304, 256), BF16),
            pltpu.SemaphoreType.DMA((4,)),
        ],
    )(v, *thin, w)

    cells = shape((4, 8, 8, 384), F32)
    message = shape((448, 128), BF16)
    weights = [pltpu.VMEM((5, 3, 256, 384), BF16)]
    dma = [pltpu.SemaphoreType.DMA((3, 3))]
    z1, z2 = both_ways(hidden, hidden, z_pairs)
    h1, h2 = both_ways(hidden, hidden, y_pairs)
    own, sent1, sent2 = call(
        row_kernel,
        (cells, message, message),
        [SCALAR] + [WHOLE] * 3 + [STORED],
        [
            pltpu.VMEM((3, 256, 256), BF16),
            pltpu.VMEM((4, 8, 24, 256), F32),
            pltpu.VMEM((3, 256, 768), BF16),
            *weights,
            pltpu.VMEM((4, 8, 8, 384), F32),
            *dma,
        ],
    )(parity, hidden, z1, z2, wa)
    y1, y2 = both_ways(sent1, sent2, y_pairs)
    out, joint, gproj = call(
        branch_kernel,
        (shape((256, 128), BF16), shape((256, 384), BF16), shape((384, 128), F32)),
        [SCALAR] + [WHOLE] * 5,
        [pltpu.VMEM((4, 8, 8, 384), F32)],
        leaves=(0,),
    )(parity, own, y1, y2, proj_weight, cot)

    z1, z2 = both_ways(joint, joint, z_pairs)
    unit = shape((64, 112, 128), BF16)
    aspp_mine, aspp_theirs, grads = call(
        aspp_grad_kernel,
        (unit, unit, shape((256, 1152), BF16)),
        [SCALAR] * 2 + [WHOLE] * 7,
        [
            pltpu.VMEM((3, 256, 256), BF16),
            pltpu.VMEM((3, 256, 384), BF16),
            pltpu.VMEM((4, 8, 24, 128), F32),
            pltpu.VMEM((256, 768), BF16),
            pltpu.VMEM((768, 384), F32),
            pltpu.VMEM((20752, 128), F32),
            pltpu.VMEM((400, 128), F32),
        ],
    )(core, parity, hidden, h1, h2, joint, z1, z2, gproj)
    aspp_other = swap(aspp_theirs, core_pairs)
    own, sent1, sent2 = call(
        spread_kernel,
        (shape((4, 8, 8, 256), F32), shape((256, 256), BF16), shape((256, 256), BF16)),
        [SCALAR, WHOLE, STORED],
        [
            *weights,
            pltpu.VMEM((4, 8, 8, 256), F32),
            pltpu.VMEM((4, 8, 8, 256), F32),
            pltpu.VMEM((4, 8, 8, 256), F32),
            *dma,
        ],
    )(parity, grads, wa)
    y1, y2 = both_ways(sent1, sent2, y_pairs)
    aspp_part = (aspp_mine.astype(F32) + aspp_other.astype(F32)).astype(BF16)
    aspp_got = to_owners(aspp_part)

    grad_hidden = own.reshape(256, 256) + (y1.astype(F32) + y2.astype(F32))
    grad_pre = (grad_hidden * slope(pre)).astype(BF16)

    unit = shape((8, 8, 112, 128), BF16)
    block_mine, block_theirs = call(
        block_grad_kernel,
        (unit, unit),
        [SCALAR] + [WHOLE] * 2,
        [pltpu.VMEM((6928, 256), F32)],
    )(core, cols, grad_pre)
    block_other = swap(block_theirs, core_pairs)

    block_part = (block_mine.astype(F32) + block_other.astype(F32)).astype(BF16)
    block_got = to_owners(block_part.reshape(64, 112, 128))

    thin = thin_halo(grad_pre, z_even, y_even)
    share = jnp.sum(aspp_got.astype(F32), axis=0)
    third1 = swap(share[0:54], FORWARDS[0])
    third2 = swap(share[56:110], FORWARDS[1])
    place_of = lax.axis_index(ALL)
    owner = jnp.any(place_of == jnp.array(OWNERS, jnp.int32)).astype(jnp.int32).reshape(1)
    (grad_volume,) = call(
        volume_grad_kernel,
        (shape((256, 256), BF16),),
        [WHOLE] * 6,
        [pltpu.VMEM((4, 10, 24, 256), F32), pltpu.VMEM((256, 256), F32)],
        leaves=(0,),
    )(grad_pre, *thin, w)
    block_share, aspp_share = call(
        finish_kernel,
        (shape((108, 128), F32), shape((162, 128), F32)),
        [SCALAR] + [STORED] * 4,
        [
            pltpu.VMEM((64, 112, 128), BF16),
            pltpu.VMEM((112, 128), F32),
            pltpu.VMEM((54, 128), F32),
            pltpu.VMEM((54, 128), F32),
            pltpu.SemaphoreType.DMA((4,)),
        ],
        leaves=(0, 1),
    )(owner, block_got, share, third1, third2)
    proj_share = jnp.concatenate([share[54:56], share[110:111]]).reshape(384)
    return (
        out.reshape(4, 8, 8, 128),
        grad_volume.reshape(4, 8, 8, 256),
        block_share.reshape(13824),
        aspp_share.reshape(20736),
        proj_share,
    )


def solution(mesh):
    fine = Mesh(mesh.devices.reshape(4, 2, 2, 2, 4), ALL)
    cells = P(None, ("z", "yh", "c"), ("yl", "x"), None)
    flat = P(ALL)
    return jax.shard_map(
        step,
        mesh=fine,
        in_specs=(cells, P(), P(), P(), cells),
        out_specs=(cells, cells, flat, flat, flat),
        check_vma=False,
    )
```

```python
import jax
import jax.numpy as jnp
from jax import lax
from jax.experimental import pallas as pl
from jax.experimental.pallas import tpu as pltpu
from jax.sharding import Mesh
from jax.sharding import PartitionSpec as P

ALL = ("z", "yh", "c", "yl", "x")
F32 = jnp.float32
BF16 = jnp.bfloat16
VLIM = 24 * 1024 * 1024
WHOLE = pl.BlockSpec(memory_space=pltpu.VMEM)
STORED = pl.BlockSpec(memory_space=pltpu.HBM)
SCALAR = pl.BlockSpec(memory_space=pltpu.SMEM)


def z_pairs(odd):
    pairs = []
    for gy in range(16):
        for gz in range(8):
            other = ((gz - odd) ^ 1) + odd
            if 0 <= other < 8:
                pairs.append((gy * 8 + gz, gy * 8 + other))
    return pairs


def y_pairs(odd):
    pairs = []
    for gy in range(16):
        for gz in range(8):
            other = ((gy - odd) ^ 1) + odd
            if 0 <= other < 16:
                pairs.append((gy * 8 + gz, other * 8 + gz))
    return pairs


def swap(value, pairs):
    return lax.ppermute(value, ALL, pairs)


def sigmoid(v):
    return 1.0 / (1.0 + jnp.exp(-v))


def slope(v):
    s = sigmoid(v)
    return s * (1.0 + v * (1.0 - s))


def call(body, outs, specs, scratch=(), leaves=()):
    kernel = pl.pallas_call(
        body,
        out_shape=tuple(
            o if i in leaves else pltpu.VMEM(o.shape, o.dtype) for i, o in enumerate(outs)
        ),
        in_specs=specs,
        out_specs=jax.tree.map(lambda _: WHOLE, outs),
        scratch_shapes=list(scratch),
        compiler_params=pltpu.CompilerParams(vmem_limit_bytes=VLIM),
        cost_estimate=pl.CostEstimate(flops=10**9, bytes_accessed=10**7, transcendentals=0),
    )

    def run(*args):
        args = [
            arg if spec is SCALAR else pltpu.with_memory_space_constraint(arg, spec.memory_space)
            for arg, spec in zip(args, specs)
        ]
        return kernel(*args)

    return run


def shape(dims, kind):
    return jax.ShapeDtypeStruct(dims, kind)


def fill_thin(ext, block, left, right, up, down, ready=None):
    left_f = left[...].astype(F32)
    right_f = right[...].astype(F32)
    for x in range(4):
        for y in range(8):
            ext[x, 1 + y, 7:8, :] = left_f[8 * x + y : 8 * x + y + 1]
            ext[x, 1 + y, 16:17, :] = right_f[8 * x + y : 8 * x + y + 1]
    for row, strip in ((0, up), (9, down)):
        s = strip[...].astype(F32)
        for x in range(4):
            ext[x, row, 8:16, :] = s[16 * x : 16 * x + 8]
            ext[x, row, 7:8, :] = s[16 * x + 8 : 16 * x + 9]
            ext[x, row, 16:17, :] = s[16 * x + 9 : 16 * x + 10]
    if ready is not None:
        ready.wait()
    width = block.shape[-1]
    ext[:, 1:9, 8:16, :] = block[...].astype(F32).reshape(4, 8, 8, width)


def conv_rows(step):
    spans = []
    for tap in range(3):
        move = step * (tap - 1)
        start = max(0, -move)
        count = 4 - abs(move)
        if count > 0:
            spans.append((tap, 64 * start, 64 * (start + move), 64 * count))
    return spans


def dot_nn(a, b):
    return lax.dot_general(a, b, (((1,), (0,)), ((), ())), preferred_element_type=F32)


def dot_nt(a, b):
    return lax.dot_general(a, b, (((1,), (1,)), ((), ())), preferred_element_type=F32)


def dot_tn(a, b):
    return lax.dot_general(a, b, (((0,), (0,)), ((), ())), preferred_element_type=F32)


def block_kernel(volume, left, right, up, down, w, hidden, pre, cols, ext, v, sem):
    ready = pltpu.make_async_copy(volume, v, sem)
    ready.start()
    fill_thin(ext, v, left, right, up, down, ready)
    for b in range(3):
        for c in range(3):
            k = 3 * b + c
            cols[:, 256 * k : 256 * k + 256] = (
                ext[:, b : b + 8, 7 + c : 15 + c, :].reshape(256, 256).astype(BF16)
            )
    pre[...] = dot_nn(cols[...], w[1])
    for tap, out_row, in_row, rows in conv_rows(1):
        if tap != 1:
            pre[out_row : out_row + rows] += dot_nn(cols[in_row : in_row + rows], w[tap])
    value = pre[...]
    hidden[...] = (value * sigmoid(value)).astype(BF16)


GROUPS = ((0, 3, 0), (4, 1, 3), (7, 1, 4))


def start_weights(source, target, sems, by_row):
    copies = []
    for i, (start, count, at) in enumerate(GROUPS):
        group = []
        for k in range(3):
            taps = source.at[pl.ds(start, count)]
            taps = taps.at[:, k] if by_row else taps.at[:, :, k]
            place = target.at[pl.ds(at, count), :, :, pl.ds(128 * k, 128)]
            group.append(pltpu.make_async_copy(taps, place, sems.at[i, k]))
        copies.append(group)
    for group in reversed(copies):
        for copy in group:
            copy.start()
    return copies


def wait_all(group):
    for copy in group:
        copy.wait()


def fetch_rows(weights, w, sems):
    for group in start_weights(weights, w, sems, True):
        wait_all(group)


def fetch_columns(weights, w, sems):
    for group in start_weights(weights, w, sems, False):
        wait_all(group)


def fetch_block(weights, w, sems):
    copies = [pltpu.make_async_copy(weights.at[a], w.at[a], sems.at[a]) for a in range(3)]
    for copy in copies:
        copy.start()
    wait_all(copies)


def line_up(even, own, first, second, line):
    after = 2 * even
    line[1] = own[...]
    line[after] = first[...]
    line[2 - after] = second[...]


def widen(line, lanes, ext):
    width = ext.shape[-1]
    for zi in range(3):
        part = line[zi, :, lanes : lanes + width].astype(F32)
        ext[:, :, 8 * zi : 8 * zi + 8, :] = part.reshape(4, 8, 8, width)


def window(line, ext, lanes, move):
    width = ext.shape[-1]
    if move % 8 == 0:
        return line[1 + move // 8, :, lanes : lanes + width]
    return ext[:, :, 8 + move : 16 + move, :].reshape(256, width).astype(BF16)


RATES = (2, 4, 8)
ROWS_SENT = ((384, 448), (256, 384), (0, 256))


def row_kernel(parity, hidden, z1, z2, w, pre, sent1, sent2, line, ext, cols, total):
    line_up(parity[0], hidden, z1, z2, line)
    widen(line, 0, ext)
    for i, rate in enumerate(RATES):
        for c in range(3):
            cols[i, :, 256 * c : 256 * c + 256] = window(line, ext, 0, rate * (c - 1))
    y_even = parity[1] == 1
    for i, rate in reversed(list(enumerate(RATES))):
        out = slice(128 * i, 128 * i + 128)
        lo, hi = ROWS_SENT[i]
        middle = 1 if rate == 2 else 2 + i
        total[...] = dot_nn(cols[i], w[middle].reshape(768, 384)).reshape(4, 8, 8, 384)
        if rate == 2:
            for a, out_row, in_row, rows in conv_rows(2):
                if a != 1:
                    layers = slice(out_row // 64, (out_row + rows) // 64)
                    term = dot_nn(cols[i, in_row : in_row + rows], w[a].reshape(768, 384))
                    total[layers] += term.reshape(rows // 64, 8, 8, 384)
        pre[:, :, :, out] = total[:, :, :, 128:256]
        if rate < 8:
            pre[:, rate:8, :, out] += total[:, 0 : 8 - rate, :, 0:128]
            pre[:, 0 : 8 - rate, :, out] += total[:, rate:8, :, 256:384]
        down = total[:, 8 - rate : 8, :, 0:128].reshape(32 * rate, 128).astype(BF16)
        up = total[:, 0:rate, :, 256:384].reshape(32 * rate, 128).astype(BF16)

        @pl.when(y_even)
        def _():
            sent1[lo:hi] = down
            sent2[lo:hi] = up

        @pl.when(jnp.logical_not(y_even))
        def _():
            sent1[lo:hi] = up
            sent2[lo:hi] = down


def branch_kernel(parity, own, y1, y2, proj, cot, out, joint, gproj, pre):
    pre[...] = own[...]

    def add(before, after):
        for i, rate in enumerate(RATES):
            lo, hi = ROWS_SENT[i]
            lanes = slice(128 * i, 128 * i + 128)
            pre[:, 0:rate, :, lanes] += before[lo:hi].astype(F32).reshape(4, rate, 8, 128)
            pre[:, 8 - rate : 8, :, lanes] += after[lo:hi].astype(F32).reshape(4, rate, 8, 128)

    @pl.when(parity[1] == 1)
    def _():
        add(y2, y1)

    @pl.when(parity[1] == 0)
    def _():
        add(y1, y2)

    value = pre[...].reshape(256, 384)
    joined = (value * sigmoid(value)).astype(BF16)
    out[...] = dot_nn(joined, proj[...]).astype(BF16)
    gproj[...] = dot_tn(joined, cot[...])
    back = dot_nt(cot[...], proj[...])
    joint[...] = (back * slope(value)).astype(BF16)


def spread_kernel(parity, cols, w, own, sent1, sent2, part, up, down):
    for b in range(3):
        for i, rate in reversed(list(enumerate(RATES))):
            lanes = slice(384 * i, 384 * i + 384)
            middle = 1 if rate == 2 else 2 + i
            part[...] = dot_nt(cols[:, lanes], w[middle, b]).reshape(4, 8, 8, 256)
            if rate == 2:
                for a, in_row, out_row, rows in conv_rows(2):
                    if a != 1:
                        layers = slice(out_row // 64, (out_row + rows) // 64)
                        term = dot_nt(cols[in_row : in_row + rows, lanes], w[a, b])
                        part[layers] += term.reshape(rows // 64, 8, 8, 256)
            if b == 1:
                own[...] += part[...]
            elif b == 0:
                if rate == 8:
                    up[...] = part[...]
                    own[...] = jnp.zeros_like(own)
                else:
                    own[:, 0 : 8 - rate] += part[:, rate:8]
                    up[:, 8 - rate : 8] += part[:, 0:rate]
            else:
                if rate == 8:
                    down[...] = part[...]
                else:
                    own[:, rate:8] += part[:, 0 : 8 - rate]
                    down[:, 0:rate] += part[:, 8 - rate : 8]
    y_even = parity[1] == 1
    up_message = up[...].reshape(256, 256).astype(BF16)
    down_message = down[...].reshape(256, 256).astype(BF16)

    @pl.when(y_even)
    def _():
        sent1[...] = down_message
        sent2[...] = up_message

    @pl.when(jnp.logical_not(y_even))
    def _():
        sent1[...] = up_message
        sent2[...] = down_message


def vanishing(row):
    tap = row // 256
    return tap >= 27 and (tap % 27) // 9 != 1


def share_plan():
    starts, forwards = [], ([], [])
    owners = []
    for c in range(2):
        device = [16 * (h // 8) + 8 * c + h % 8 for h in range(64)]
        full = [h for h in range(64) if not all(vanishing(162 * device[h] + r) for r in range(162))]
        spare = [h for h in range(64) if h not in full]
        slots = [[None, None] for _ in range(64)]
        for h in full:
            slots[h] = [162 * device[h], 162 * device[h] + 54]
            owners.append(device[h])
        for i, h in enumerate(full):
            slot, helper = divmod(i, len(spare))
            slots[spare[helper]][slot] = 162 * device[h] + 108
            forwards[slot].append((device[spare[helper]], device[h]))
        starts.append(slots)
    return starts, forwards, owners


SLOTS, FORWARDS, OWNERS = share_plan()


def aspp_grad_kernel(
    core, parity, hidden, y1, y2, joint, z1, z2, gproj,
    mine, theirs, cols, line, near, ext, left, block, sums, proj_rows,
):
    line_up(parity[0], joint, z1, z2, near)
    for i, rate in enumerate(RATES):
        if rate < 8:
            widen(near, 128 * i, ext)
        for c in range(3):
            at = 384 * i + 128 * c
            cols[:, at : at + 128] = window(near, ext, 128 * i, -rate * (c - 1))
    line_up(parity[1], hidden, y1, y2, line)
    for i, rate in enumerate(RATES):
        cut = 8 * rate
        for b in range(3):
            lanes = slice(256 * b, 256 * b + 256)
            if b == 1 or rate == 8:
                left[:, lanes] = line[b]
                continue
            for x in range(0, 256, 64):
                if b == 0:
                    left[x : x + cut, lanes] = line[0, x + 64 - cut : x + 64]
                    left[x + cut : x + 64, lanes] = line[1, x : x + 64 - cut]
                else:
                    left[x : x + 64 - cut, lanes] = line[1, x + cut : x + 64]
                    left[x + 64 - cut : x + 64, lanes] = line[2, x : x + cut]
        for a, out_row, in_row, rows in conv_rows(2 if i == 0 else 4):
            block[...] = dot_tn(
                left[in_row : in_row + rows, :],
                cols[out_row : out_row + rows, 384 * i : 384 * i + 384],
            )
            for b in range(3):
                for c in range(3):
                    at = 256 * (27 * i + 9 * a + 3 * b + c)
                    sums[at : at + 256] = block[256 * b : 256 * b + 256, 128 * c : 128 * c + 128]
    for unit in OWNERS:
        for row in range(162 * unit // 8 * 8, 162 * unit + 168, 8):
            if vanishing(row):
                sums[row : row + 8] = jnp.zeros((8, 128), F32)
    proj_rows[0:8] = jnp.zeros((8, 128), F32)
    proj_rows[8:392] = gproj[...]
    proj_rows[392:400] = jnp.zeros((8, 128), F32)
    spare = lax.broadcasted_iota(jnp.int32, (8, 128), 0) >= 6

    def pack(target, c):
        for h in range(64):
            for slot in range(2):
                start = SLOTS[c][h][slot]
                row = 2 + 3 * (16 * (h // 8) + 8 * c + h % 8) + 2 * slot
                last = proj_rows[row : row + 8]
                if start is None:
                    target[h, 56 * slot : 56 * slot + 48] = jnp.zeros((48, 128), BF16)
                else:
                    target[h, 56 * slot : 56 * slot + 48] = sums[start : start + 48].astype(BF16)
                    last = jnp.where(spare, last, sums[start + 48 : start + 56])
                target[h, 56 * slot + 48 : 56 * slot + 56] = last.astype(BF16)

    for me in range(2):

        @pl.when(core[0] == me)
        def _():
            pack(mine, me)
            pack(theirs, 1 - me)


def rows_at(ref, base, offset, rows):
    phase = offset % 8
    start = pl.multiple_of(base + (offset - phase), 8)
    length = rows + (8 if phase else 0)
    return ref[pl.ds(start, length), :][phase : phase + rows].astype(BF16)


def block_grad_kernel(core, cols, grad, mine, theirs, sums):
    for tap, out_row, in_row, rows in conv_rows(1):
        sums[2304 * tap : 2304 * tap + 2304] = dot_tn(
            cols[in_row : in_row + rows, :], grad[out_row : out_row + rows, :]
        )
    sums[6912:6928] = jnp.zeros((16, 256), F32)
    me = core[0]

    def step(g, carry):
        for half in range(2):
            for e in range(8):
                chunk = rows_at(sums, g * 864, 54 * (8 * half + e), 56)

                @pl.when(me == half)
                def _():
                    mine[g, e, 0:56] = chunk[:, 0:128]
                    mine[g, e, 56:112] = chunk[:, 128:256]

                @pl.when(me != half)
                def _():
                    theirs[g, e, 0:56] = chunk[:, 0:128]
                    theirs[g, e, 56:112] = chunk[:, 128:256]

        return carry

    lax.fori_loop(0, 8, step, 0)


def finish_kernel(
    owner, got, share, third1, third2, block_share, aspp_share, parts, own, add1, add2, sems
):
    moves = ((got, parts), (share, own), (third1, add1), (third2, add2))
    copies = [pltpu.make_async_copy(a, b, sems.at[i]) for i, (a, b) in enumerate(moves)]
    for copy in copies:
        copy.start()
    for copy in copies[1:]:
        copy.wait()
    keep = owner[0] == 1
    aspp_share[0:54] = jnp.where(keep, own[0:54], 0.0)
    aspp_share[54:108] = jnp.where(keep, own[56:110], 0.0)
    aspp_share[108:162] = jnp.where(keep, add1[...] + add2[...], 0.0)
    copies[0].wait()
    total = parts[0].astype(F32)
    for source in range(1, 64):
        total += parts[source].astype(F32)
    block_share[pl.ds(0, 54, stride=2), :] = total[0:54]
    block_share[pl.ds(1, 54, stride=2), :] = total[56:110]


def volume_grad_kernel(gp, left, right, up, down, w, grad, ext, acc):
    fill_thin(ext, gp, left, right, up, down)
    acc[...] = jnp.zeros_like(acc)
    for b in range(3):
        for c in range(3):
            k = 256 * (3 * b + c)
            piece = ext[:, 2 - b : 10 - b, 9 - c : 17 - c, :].reshape(256, 256).astype(BF16)
            for tap, in_row, out_row, rows in conv_rows(1):
                acc[out_row : out_row + rows] += dot_nt(
                    piece[in_row : in_row + rows], w[tap, k : k + 256, :]
                )
    grad[...] = acc[...].astype(BF16)


def thin_halo(block, z_even, y_even):
    width = block.shape[-1]
    cells = block.reshape(4, 8, 8, width)
    first, last = cells[:, :, 0], cells[:, :, 7]
    z1 = jnp.where(z_even, last, first)
    z2 = jnp.where(z_even, first, last)
    z1, z2 = both_ways(z1, z2, z_pairs)
    left = jnp.where(z_even, z2, z1)
    right = jnp.where(z_even, z1, z2)

    def strip(y):
        return jnp.concatenate(
            [
                cells[:, y],
                left[:, y : y + 1],
                right[:, y : y + 1],
                jnp.zeros((4, 6, width), block.dtype),
            ],
            axis=1,
        )

    top, bottom = strip(0), strip(7)
    y1 = jnp.where(y_even, bottom, top)
    y2 = jnp.where(y_even, top, bottom)
    y1, y2 = both_ways(y1, y2, y_pairs)
    up = jnp.where(y_even, y2, y1)
    down = jnp.where(y_even, y1, y2)
    return (
        left.reshape(32, width),
        right.reshape(32, width),
        up.reshape(64, width),
        down.reshape(64, width),
    )


def both_ways(first, second, pairs):
    first = swap(first, pairs(0))
    second = swap(second, pairs(1))
    return first, second


def to_owners(chunks):
    return lax.all_to_all(chunks, ("z", "yh", "yl", "x"), 0, 0, tiled=True)


def step(volume, block_weight, aspp_weight, proj_weight, cotangent):
    core = lax.axis_index("c")
    z_even = lax.axis_index("x") % 2 == 0
    y_even = core == 0
    parity = jnp.stack([z_even.astype(jnp.int32), y_even.astype(jnp.int32)])
    core = core.astype(jnp.int32).reshape(1)
    core_pairs = y_pairs(0)

    v = volume.reshape(256, 256)
    w = block_weight.reshape(3, 2304, 256)
    wa = aspp_weight.reshape(9, 3, 3, 256, 128)
    cot = cotangent.reshape(256, 128)

    thin = thin_halo(v, z_even, y_even)
    (w_near,) = call(
        fetch_block,
        (shape((3, 2304, 256), BF16),),
        [STORED],
        [pltpu.SemaphoreType.DMA((3,))],
    )(w)
    hidden, pre, cols = call(
        block_kernel,
        (shape((256, 256), BF16), shape((256, 256), F32), shape((256, 2304), BF16)),
        [STORED] + [WHOLE] * 5,
        [
            pltpu.VMEM((4, 10, 24, 256), F32),
            pltpu.VMEM((256, 256), BF16),
            pltpu.SemaphoreType.DMA,
        ],
    )(v, *thin, w_near)

    cells = shape((4, 8, 8, 384), F32)
    message = shape((448, 128), BF16)
    side_by_side = (shape((5, 3, 256, 384), BF16),)
    dma = [pltpu.SemaphoreType.DMA((3, 3))]
    (w_rows,) = call(fetch_rows, side_by_side, [STORED], dma)(wa)
    (w_columns,) = call(fetch_columns, side_by_side, [STORED], dma)(wa)
    z1, z2 = both_ways(hidden, hidden, z_pairs)
    h1, h2 = both_ways(hidden, hidden, y_pairs)
    own, sent1, sent2 = call(
        row_kernel,
        (cells, message, message),
        [SCALAR] + [WHOLE] * 4,
        [
            pltpu.VMEM((3, 256, 256), BF16),
            pltpu.VMEM((4, 8, 24, 256), F32),
            pltpu.VMEM((3, 256, 768), BF16),
            pltpu.VMEM((4, 8, 8, 384), F32),
        ],
    )(parity, hidden, z1, z2, w_rows)
    y1, y2 = both_ways(sent1, sent2, y_pairs)
    out, joint, gproj = call(
        branch_kernel,
        (shape((256, 128), BF16), shape((256, 384), BF16), shape((384, 128), F32)),
        [SCALAR] + [WHOLE] * 5,
        [pltpu.VMEM((4, 8, 8, 384), F32)],
        leaves=(0,),
    )(parity, own, y1, y2, proj_weight, cot)

    z1, z2 = both_ways(joint, joint, z_pairs)
    unit = shape((64, 112, 128), BF16)
    aspp_mine, aspp_theirs, grads = call(
        aspp_grad_kernel,
        (unit, unit, shape((256, 1152), BF16)),
        [SCALAR] * 2 + [WHOLE] * 7,
        [
            pltpu.VMEM((3, 256, 256), BF16),
            pltpu.VMEM((3, 256, 384), BF16),
            pltpu.VMEM((4, 8, 24, 128), F32),
            pltpu.VMEM((256, 768), BF16),
            pltpu.VMEM((768, 384), F32),
            pltpu.VMEM((20752, 128), F32),
            pltpu.VMEM((400, 128), F32),
        ],
    )(core, parity, hidden, h1, h2, joint, z1, z2, gproj)
    aspp_other = swap(aspp_theirs, core_pairs)
    own, sent1, sent2 = call(
        spread_kernel,
        (shape((4, 8, 8, 256), F32), shape((256, 256), BF16), shape((256, 256), BF16)),
        [SCALAR, WHOLE, WHOLE],
        [
            pltpu.VMEM((4, 8, 8, 256), F32),
            pltpu.VMEM((4, 8, 8, 256), F32),
            pltpu.VMEM((4, 8, 8, 256), F32),
        ],
    )(parity, grads, w_columns)
    y1, y2 = both_ways(sent1, sent2, y_pairs)
    aspp_part = (aspp_mine.astype(F32) + aspp_other.astype(F32)).astype(BF16)
    aspp_got = to_owners(aspp_part)

    grad_hidden = own.reshape(256, 256) + (y1.astype(F32) + y2.astype(F32))
    grad_pre = (grad_hidden * slope(pre)).astype(BF16)

    unit = shape((8, 8, 112, 128), BF16)
    block_mine, block_theirs = call(
        block_grad_kernel,
        (unit, unit),
        [SCALAR] + [WHOLE] * 2,
        [pltpu.VMEM((6928, 256), F32)],
    )(core, cols, grad_pre)
    block_other = swap(block_theirs, core_pairs)

    block_part = (block_mine.astype(F32) + block_other.astype(F32)).astype(BF16)
    block_got = to_owners(block_part.reshape(64, 112, 128))

    thin = thin_halo(grad_pre, z_even, y_even)
    share = jnp.sum(aspp_got.astype(F32), axis=0)
    third1 = swap(share[0:54], FORWARDS[0])
    third2 = swap(share[56:110], FORWARDS[1])
    place_of = lax.axis_index(ALL)
    owner = jnp.any(place_of == jnp.array(OWNERS, jnp.int32)).astype(jnp.int32).reshape(1)
    (grad_volume,) = call(
        volume_grad_kernel,
        (shape((256, 256), BF16),),
        [WHOLE] * 6,
        [pltpu.VMEM((4, 10, 24, 256), F32), pltpu.VMEM((256, 256), F32)],
        leaves=(0,),
    )(grad_pre, *thin, w)
    block_share, aspp_share = call(
        finish_kernel,
        (shape((108, 128), F32), shape((162, 128), F32)),
        [SCALAR] + [STORED] * 4,
        [
            pltpu.VMEM((64, 112, 128), BF16),
            pltpu.VMEM((112, 128), F32),
            pltpu.VMEM((54, 128), F32),
            pltpu.VMEM((54, 128), F32),
            pltpu.SemaphoreType.DMA((4,)),
        ],
        leaves=(0, 1),
    )(owner, block_got, share, third1, third2)
    proj_share = jnp.concatenate([share[54:56], share[110:111]]).reshape(384)
    return (
        out.reshape(4, 8, 8, 128),
        grad_volume.reshape(4, 8, 8, 256),
        block_share.reshape(13824),
        aspp_share.reshape(20736),
        proj_share,
    )


def solution(mesh):
    fine = Mesh(mesh.devices.reshape(4, 2, 2, 2, 4), ALL)
    cells = P(None, ("z", "yh", "c"), ("yl", "x"), None)
    flat = P(ALL)
    return jax.shard_map(
        step,
        mesh=fine,
        in_specs=(cells, P(), P(), P(), cells),
        out_specs=(cells, cells, flat, flat, flat),
        check_vma=False,
    )
```

```python
import jax
import jax.numpy as jnp
from jax import lax
from jax.experimental import pallas as pl
from jax.experimental.pallas import tpu as pltpu
from jax.sharding import Mesh
from jax.sharding import PartitionSpec as P

ALL = ("z", "yh", "c", "yl", "x")
F32 = jnp.float32
BF16 = jnp.bfloat16
VLIM = 24 * 1024 * 1024
WHOLE = pl.BlockSpec(memory_space=pltpu.VMEM)
STORED = pl.BlockSpec(memory_space=pltpu.HBM)
SCALAR = pl.BlockSpec(memory_space=pltpu.SMEM)


def z_pairs(odd):
    pairs = []
    for gy in range(16):
        for gz in range(8):
            other = ((gz - odd) ^ 1) + odd
            if 0 <= other < 8:
                pairs.append((gy * 8 + gz, gy * 8 + other))
    return pairs


def y_pairs(odd):
    pairs = []
    for gy in range(16):
        for gz in range(8):
            other = ((gy - odd) ^ 1) + odd
            if 0 <= other < 16:
                pairs.append((gy * 8 + gz, other * 8 + gz))
    return pairs


def swap(value, pairs):
    return lax.ppermute(value, ALL, pairs)


def sigmoid(v):
    return 1.0 / (1.0 + jnp.exp(-v))


def slope(v):
    s = sigmoid(v)
    return s * (1.0 + v * (1.0 - s))


def call(body, outs, specs, scratch=(), leaves=()):
    kernel = pl.pallas_call(
        body,
        out_shape=tuple(
            o if i in leaves else pltpu.VMEM(o.shape, o.dtype) for i, o in enumerate(outs)
        ),
        in_specs=specs,
        out_specs=jax.tree.map(lambda _: WHOLE, outs),
        scratch_shapes=list(scratch),
        compiler_params=pltpu.CompilerParams(vmem_limit_bytes=VLIM),
        cost_estimate=pl.CostEstimate(flops=10**9, bytes_accessed=10**7, transcendentals=0),
    )

    def run(*args):
        args = [
            arg if spec is SCALAR else pltpu.with_memory_space_constraint(arg, spec.memory_space)
            for arg, spec in zip(args, specs)
        ]
        return kernel(*args)

    return run


def shape(dims, kind):
    return jax.ShapeDtypeStruct(dims, kind)


def fill_thin(ext, block, left, right, up, down, ready=None):
    left_f = left[...].astype(F32)
    right_f = right[...].astype(F32)
    for x in range(4):
        for y in range(8):
            ext[x, 1 + y, 7:8, :] = left_f[8 * x + y : 8 * x + y + 1]
            ext[x, 1 + y, 16:17, :] = right_f[8 * x + y : 8 * x + y + 1]
    for row, strip in ((0, up), (9, down)):
        s = strip[...].astype(F32)
        for x in range(4):
            ext[x, row, 8:16, :] = s[16 * x : 16 * x + 8]
            ext[x, row, 7:8, :] = s[16 * x + 8 : 16 * x + 9]
            ext[x, row, 16:17, :] = s[16 * x + 9 : 16 * x + 10]
    if ready is not None:
        ready.wait()
    width = block.shape[-1]
    ext[:, 1:9, 8:16, :] = block[...].astype(F32).reshape(4, 8, 8, width)


def conv_rows(step):
    spans = []
    for tap in range(3):
        move = step * (tap - 1)
        start = max(0, -move)
        count = 4 - abs(move)
        if count > 0:
            spans.append((tap, 64 * start, 64 * (start + move), 64 * count))
    return spans


def dot_nn(a, b):
    return lax.dot_general(a, b, (((1,), (0,)), ((), ())), preferred_element_type=F32)


def dot_nt(a, b):
    return lax.dot_general(a, b, (((1,), (1,)), ((), ())), preferred_element_type=F32)


def dot_tn(a, b):
    return lax.dot_general(a, b, (((0,), (0,)), ((), ())), preferred_element_type=F32)


def block_kernel(volume, left, right, up, down, w, hidden, pre, cols, ext, v, sem):
    ready = pltpu.make_async_copy(volume, v, sem)
    ready.start()
    fill_thin(ext, v, left, right, up, down, ready)
    for b in range(3):
        for c in range(3):
            k = 3 * b + c
            cols[:, 256 * k : 256 * k + 256] = (
                ext[:, b : b + 8, 7 + c : 15 + c, :].reshape(256, 256).astype(BF16)
            )
    pre[...] = dot_nn(cols[...], w[1])
    for tap, out_row, in_row, rows in conv_rows(1):
        if tap != 1:
            pre[out_row : out_row + rows] += dot_nn(cols[in_row : in_row + rows], w[tap])
    value = pre[...]
    hidden[...] = (value * sigmoid(value)).astype(BF16)


GROUPS = ((0, 3, 0), (4, 1, 3), (7, 1, 4))


def start_weights(source, target, sems, by_row):
    copies = []
    for i, (start, count, at) in enumerate(GROUPS):
        group = []
        for k in range(3):
            taps = source.at[pl.ds(start, count)]
            taps = taps.at[:, k] if by_row else taps.at[:, :, k]
            place = target.at[pl.ds(at, count), :, :, pl.ds(128 * k, 128)]
            group.append(pltpu.make_async_copy(taps, place, sems.at[i, k]))
        copies.append(group)
    for group in reversed(copies):
        for copy in group:
            copy.start()
    return copies


def wait_all(group):
    for copy in group:
        copy.wait()


def fetch_rows(weights, w, sems):
    for group in start_weights(weights, w, sems, True):
        wait_all(group)


def fetch_columns(weights, w, sems):
    for group in start_weights(weights, w, sems, False):
        wait_all(group)


def fetch_block(weights, w, sems):
    copies = [pltpu.make_async_copy(weights.at[a], w.at[a], sems.at[a]) for a in range(3)]
    for copy in copies:
        copy.start()
    wait_all(copies)


def line_up(even, own, first, second, line):
    after = 2 * even
    line[1] = own[...]
    line[after] = first[...]
    line[2 - after] = second[...]


def widen(line, lanes, ext):
    width = ext.shape[-1]
    for zi in range(3):
        part = line[zi, :, lanes : lanes + width].astype(F32)
        ext[:, :, 8 * zi : 8 * zi + 8, :] = part.reshape(4, 8, 8, width)


def window(line, ext, lanes, move):
    width = ext.shape[-1]
    if move % 8 == 0:
        return line[1 + move // 8, :, lanes : lanes + width]
    return ext[:, :, 8 + move : 16 + move, :].reshape(256, width).astype(BF16)


RATES = (2, 4, 8)
ROWS_SENT = ((384, 448), (256, 384), (0, 256))


def row_kernel(parity, hidden, z1, z2, w, pre, sent1, sent2, line, ext, cols, total):
    line_up(parity[0], hidden, z1, z2, line)
    widen(line, 0, ext)
    for i, rate in enumerate(RATES):
        for c in range(3):
            cols[i, :, 256 * c : 256 * c + 256] = window(line, ext, 0, rate * (c - 1))
    y_even = parity[1] == 1
    for i, rate in reversed(list(enumerate(RATES))):
        out = slice(128 * i, 128 * i + 128)
        lo, hi = ROWS_SENT[i]
        middle = 1 if rate == 2 else 2 + i
        total[...] = dot_nn(cols[i], w[middle].reshape(768, 384)).reshape(4, 8, 8, 384)
        if rate == 2:
            for a, out_row, in_row, rows in conv_rows(2):
                if a != 1:
                    layers = slice(out_row // 64, (out_row + rows) // 64)
                    term = dot_nn(cols[i, in_row : in_row + rows], w[a].reshape(768, 384))
                    total[layers] += term.reshape(rows // 64, 8, 8, 384)
        pre[:, :, :, out] = total[:, :, :, 128:256]
        if rate < 8:
            pre[:, rate:8, :, out] += total[:, 0 : 8 - rate, :, 0:128]
            pre[:, 0 : 8 - rate, :, out] += total[:, rate:8, :, 256:384]
        down = total[:, 8 - rate : 8, :, 0:128].reshape(32 * rate, 128).astype(BF16)
        up = total[:, 0:rate, :, 256:384].reshape(32 * rate, 128).astype(BF16)

        @pl.when(y_even)
        def _():
            sent1[lo:hi] = down
            sent2[lo:hi] = up

        @pl.when(jnp.logical_not(y_even))
        def _():
            sent1[lo:hi] = up
            sent2[lo:hi] = down


def branch_kernel(parity, own, y1, y2, proj, cot, out, joint, gproj, edge1, edge2, pre):
    pre[...] = own[...]

    def add(before, after):
        for i, rate in enumerate(RATES):
            lo, hi = ROWS_SENT[i]
            lanes = slice(128 * i, 128 * i + 128)
            pre[:, 0:rate, :, lanes] += before[lo:hi].astype(F32).reshape(4, rate, 8, 128)
            pre[:, 8 - rate : 8, :, lanes] += after[lo:hi].astype(F32).reshape(4, rate, 8, 128)

    @pl.when(parity[1] == 1)
    def _():
        add(y2, y1)

    @pl.when(parity[1] == 0)
    def _():
        add(y1, y2)

    value = pre[...].reshape(256, 384)
    joined = (value * sigmoid(value)).astype(BF16)
    out[...] = dot_nn(joined, proj[...]).astype(BF16)
    gproj[...] = dot_tn(joined, cot[...])
    back = dot_nt(cot[...], proj[...])
    grad = back * slope(value)
    joint[...] = grad.astype(BF16)
    two = grad[:, 0:128].reshape(32, 8, 128)
    four = grad[:, 128:256].reshape(32, 8, 128)
    upper = lax.broadcasted_iota(jnp.int32, (32, 8, 128), 1) < 4
    right = jnp.where(upper, pltpu.roll(four, 4, 1), pltpu.roll(two, 6, 1))
    left = jnp.where(upper, four, pltpu.roll(two, 4, 1))
    right = right.reshape(256, 128).astype(BF16)
    left = left.reshape(256, 128).astype(BF16)
    for edge in (edge1, edge2):
        edge[0:256] = grad[:, 256:384].astype(BF16)

    @pl.when(parity[0] == 1)
    def _():
        edge1[256:512] = right
        edge2[256:512] = left

    @pl.when(parity[0] == 0)
    def _():
        edge1[256:512] = left
        edge2[256:512] = right


def spread_kernel(parity, cols, w, own, sent1, sent2, part, up, down):
    for b in range(3):
        for i, rate in reversed(list(enumerate(RATES))):
            lanes = slice(384 * i, 384 * i + 384)
            middle = 1 if rate == 2 else 2 + i
            part[...] = dot_nt(cols[:, lanes], w[middle, b]).reshape(4, 8, 8, 256)
            if rate == 2:
                for a, in_row, out_row, rows in conv_rows(2):
                    if a != 1:
                        layers = slice(out_row // 64, (out_row + rows) // 64)
                        term = dot_nt(cols[in_row : in_row + rows, lanes], w[a, b])
                        part[layers] += term.reshape(rows // 64, 8, 8, 256)
            if b == 1:
                own[...] += part[...]
            elif b == 0:
                if rate == 8:
                    up[...] = part[...]
                    own[...] = jnp.zeros_like(own)
                else:
                    own[:, 0 : 8 - rate] += part[:, rate:8]
                    up[:, 8 - rate : 8] += part[:, 0:rate]
            else:
                if rate == 8:
                    down[...] = part[...]
                else:
                    own[:, rate:8] += part[:, 0 : 8 - rate]
                    down[:, 0:rate] += part[:, 8 - rate : 8]
    y_even = parity[1] == 1
    up_message = up[...].reshape(256, 256).astype(BF16)
    down_message = down[...].reshape(256, 256).astype(BF16)

    @pl.when(y_even)
    def _():
        sent1[...] = down_message
        sent2[...] = up_message

    @pl.when(jnp.logical_not(y_even))
    def _():
        sent1[...] = up_message
        sent2[...] = down_message


def vanishing(row):
    tap = row // 256
    return tap >= 27 and (tap % 27) // 9 != 1


def share_plan():
    starts, forwards = [], ([], [])
    owners = []
    for c in range(2):
        device = [16 * (h // 8) + 8 * c + h % 8 for h in range(64)]
        full = [h for h in range(64) if not all(vanishing(162 * device[h] + r) for r in range(162))]
        spare = [h for h in range(64) if h not in full]
        slots = [[None, None] for _ in range(64)]
        for h in full:
            slots[h] = [162 * device[h], 162 * device[h] + 54]
            owners.append(device[h])
        for i, h in enumerate(full):
            slot, helper = divmod(i, len(spare))
            slots[spare[helper]][slot] = 162 * device[h] + 108
            forwards[slot].append((device[spare[helper]], device[h]))
        starts.append(slots)
    return starts, forwards, owners


SLOTS, FORWARDS, OWNERS = share_plan()


def aspp_grad_kernel(
    core, parity, hidden, y1, y2, joint, z1, z2, gproj,
    mine, theirs, cols, line, near, ext, left, block, sums, proj_rows,
):
    after = 2 * parity[0]
    near[after] = z1[...]
    near[2 - after] = z2[...]
    before_tile = near[0, 256:512].astype(F32).reshape(32, 8, 128)
    after_tile = near[2, 256:512].astype(F32).reshape(32, 8, 128)
    for i, rate in enumerate(RATES[:2]):
        lower = pltpu.roll(before_tile, rate, 1)
        upper = after_tile if rate == 4 else pltpu.roll(after_tile, 4, 1)
        middle = joint[:, 128 * i : 128 * i + 128].astype(F32)
        for zi, tile in enumerate((lower, middle, upper)):
            ext[:, :, 8 * zi : 8 * zi + 8, :] = tile.reshape(4, 8, 8, 128)
        for c in range(3):
            at = 384 * i + 128 * c
            z0 = 8 - rate * (c - 1)
            cols[:, at : at + 128] = ext[:, :, z0 : z0 + 8, :].reshape(256, 128).astype(BF16)
    cols[:, 768:896] = near[2, 0:256]
    cols[:, 896:1024] = joint[:, 256:384]
    cols[:, 1024:1152] = near[0, 0:256]
    line_up(parity[1], hidden, y1, y2, line)
    for i, rate in enumerate(RATES):
        cut = 8 * rate
        for b in range(3):
            lanes = slice(256 * b, 256 * b + 256)
            if b == 1 or rate == 8:
                left[:, lanes] = line[b]
                continue
            for x in range(0, 256, 64):
                if b == 0:
                    left[x : x + cut, lanes] = line[0, x + 64 - cut : x + 64]
                    left[x + cut : x + 64, lanes] = line[1, x : x + 64 - cut]
                else:
                    left[x : x + 64 - cut, lanes] = line[1, x + cut : x + 64]
                    left[x + 64 - cut : x + 64, lanes] = line[2, x : x + cut]
        for a, out_row, in_row, rows in conv_rows(2 if i == 0 else 4):
            block[...] = dot_tn(
                left[in_row : in_row + rows, :],
                cols[out_row : out_row + rows, 384 * i : 384 * i + 384],
            )
            for b in range(3):
                for c in range(3):
                    at = 256 * (27 * i + 9 * a + 3 * b + c)
                    sums[at : at + 256] = block[256 * b : 256 * b + 256, 128 * c : 128 * c + 128]
    for unit in OWNERS:
        for row in range(162 * unit // 8 * 8, 162 * unit + 168, 8):
            if vanishing(row):
                sums[row : row + 8] = jnp.zeros((8, 128), F32)
    proj_rows[0:8] = jnp.zeros((8, 128), F32)
    proj_rows[8:392] = gproj[...]
    proj_rows[392:400] = jnp.zeros((8, 128), F32)
    spare = lax.broadcasted_iota(jnp.int32, (8, 128), 0) >= 6

    def pack(target, c):
        for h in range(64):
            for slot in range(2):
                start = SLOTS[c][h][slot]
                row = 2 + 3 * (16 * (h // 8) + 8 * c + h % 8) + 2 * slot
                last = proj_rows[row : row + 8]
                if start is None:
                    target[h, 56 * slot : 56 * slot + 48] = jnp.zeros((48, 128), BF16)
                else:
                    target[h, 56 * slot : 56 * slot + 48] = sums[start : start + 48].astype(BF16)
                    last = jnp.where(spare, last, sums[start + 48 : start + 56])
                target[h, 56 * slot + 48 : 56 * slot + 56] = last.astype(BF16)

    for me in range(2):

        @pl.when(core[0] == me)
        def _():
            pack(mine, me)
            pack(theirs, 1 - me)


def rows_at(ref, base, offset, rows):
    phase = offset % 8
    start = pl.multiple_of(base + (offset - phase), 8)
    length = rows + (8 if phase else 0)
    return ref[pl.ds(start, length), :][phase : phase + rows].astype(BF16)


def block_grad_kernel(core, cols, grad, mine, theirs, sums):
    for tap, out_row, in_row, rows in conv_rows(1):
        sums[2304 * tap : 2304 * tap + 2304] = dot_tn(
            cols[in_row : in_row + rows, :], grad[out_row : out_row + rows, :]
        )
    sums[6912:6928] = jnp.zeros((16, 256), F32)
    me = core[0]

    def step(g, carry):
        for half in range(2):
            for e in range(8):
                chunk = rows_at(sums, g * 864, 54 * (8 * half + e), 56)

                @pl.when(me == half)
                def _():
                    mine[g, e, 0:56] = chunk[:, 0:128]
                    mine[g, e, 56:112] = chunk[:, 128:256]

                @pl.when(me != half)
                def _():
                    theirs[g, e, 0:56] = chunk[:, 0:128]
                    theirs[g, e, 56:112] = chunk[:, 128:256]

        return carry

    lax.fori_loop(0, 8, step, 0)


def finish_kernel(
    owner, got, share, third1, third2, block_share, aspp_share, parts, own, add1, add2, sems
):
    quarters = [pl.ds(16 * q, 16) for q in range(4)]
    moves = [(share, own), (third1, add1), (third2, add2)]
    moves += [(got.at[q], parts.at[q]) for q in quarters]
    copies = [pltpu.make_async_copy(a, b, sems.at[i]) for i, (a, b) in enumerate(moves)]
    for copy in copies:
        copy.start()
    wait_all(copies[:3])
    keep = owner[0] == 1
    aspp_share[0:54] = jnp.where(keep, own[0:54], 0.0)
    aspp_share[54:108] = jnp.where(keep, own[56:110], 0.0)
    aspp_share[108:162] = jnp.where(keep, add1[...] + add2[...], 0.0)
    total = jnp.zeros((112, 128), F32)
    for source in range(64):
        if source % 16 == 0:
            copies[3 + source // 16].wait()
        total += parts[source].astype(F32)
    block_share[pl.ds(0, 54, stride=2), :] = total[0:54]
    block_share[pl.ds(1, 54, stride=2), :] = total[56:110]


def volume_grad_kernel(gp, left, right, up, down, w, grad, ext, acc):
    fill_thin(ext, gp, left, right, up, down)
    acc[...] = jnp.zeros_like(acc)
    for b in range(3):
        for c in range(3):
            k = 256 * (3 * b + c)
            piece = ext[:, 2 - b : 10 - b, 9 - c : 17 - c, :].reshape(256, 256).astype(BF16)
            for tap, in_row, out_row, rows in conv_rows(1):
                acc[out_row : out_row + rows] += dot_nt(
                    piece[in_row : in_row + rows], w[tap, k : k + 256, :]
                )
    grad[...] = acc[...].astype(BF16)


def thin_halo(block, z_even, y_even):
    width = block.shape[-1]
    cells = block.reshape(4, 8, 8, width)
    first, last = cells[:, :, 0], cells[:, :, 7]
    z1 = jnp.where(z_even, last, first)
    z2 = jnp.where(z_even, first, last)
    z1, z2 = both_ways(z1, z2, z_pairs)
    left = jnp.where(z_even, z2, z1)
    right = jnp.where(z_even, z1, z2)

    def strip(y):
        return jnp.concatenate(
            [
                cells[:, y],
                left[:, y : y + 1],
                right[:, y : y + 1],
                jnp.zeros((4, 6, width), block.dtype),
            ],
            axis=1,
        )

    top, bottom = strip(0), strip(7)
    y1 = jnp.where(y_even, bottom, top)
    y2 = jnp.where(y_even, top, bottom)
    y1, y2 = both_ways(y1, y2, y_pairs)
    up = jnp.where(y_even, y2, y1)
    down = jnp.where(y_even, y1, y2)
    return (
        left.reshape(32, width),
        right.reshape(32, width),
        up.reshape(64, width),
        down.reshape(64, width),
    )


def both_ways(first, second, pairs):
    first = swap(first, pairs(0))
    second = swap(second, pairs(1))
    return first, second


def to_owners(chunks):
    return lax.all_to_all(chunks, ("z", "yh", "yl", "x"), 0, 0, tiled=True)


def step(volume, block_weight, aspp_weight, proj_weight, cotangent):
    core = lax.axis_index("c")
    z_even = lax.axis_index("x") % 2 == 0
    y_even = core == 0
    parity = jnp.stack([z_even.astype(jnp.int32), y_even.astype(jnp.int32)])
    core = core.astype(jnp.int32).reshape(1)
    core_pairs = y_pairs(0)

    v = volume.reshape(256, 256)
    w = block_weight.reshape(3, 2304, 256)
    wa = aspp_weight.reshape(9, 3, 3, 256, 128)
    cot = cotangent.reshape(256, 128)

    thin = thin_halo(v, z_even, y_even)
    (w_near,) = call(
        fetch_block,
        (shape((3, 2304, 256), BF16),),
        [STORED],
        [pltpu.SemaphoreType.DMA((3,))],
    )(w)
    hidden, pre, cols = call(
        block_kernel,
        (shape((256, 256), BF16), shape((256, 256), F32), shape((256, 2304), BF16)),
        [STORED] + [WHOLE] * 5,
        [
            pltpu.VMEM((4, 10, 24, 256), F32),
            pltpu.VMEM((256, 256), BF16),
            pltpu.SemaphoreType.DMA,
        ],
    )(v, *thin, w_near)

    cells = shape((4, 8, 8, 384), F32)
    message = shape((448, 128), BF16)
    side_by_side = (shape((5, 3, 256, 384), BF16),)
    dma = [pltpu.SemaphoreType.DMA((3, 3))]
    (w_rows,) = call(fetch_rows, side_by_side, [STORED], dma)(wa)
    (w_columns,) = call(fetch_columns, side_by_side, [STORED], dma)(wa)
    z1, z2 = both_ways(hidden, hidden, z_pairs)
    h1, h2 = both_ways(hidden, hidden, y_pairs)
    own, sent1, sent2 = call(
        row_kernel,
        (cells, message, message),
        [SCALAR] + [WHOLE] * 4,
        [
            pltpu.VMEM((3, 256, 256), BF16),
            pltpu.VMEM((4, 8, 24, 256), F32),
            pltpu.VMEM((3, 256, 768), BF16),
            pltpu.VMEM((4, 8, 8, 384), F32),
        ],
    )(parity, hidden, z1, z2, w_rows)
    y1, y2 = both_ways(sent1, sent2, y_pairs)
    out, joint, gproj, edge1, edge2 = call(
        branch_kernel,
        (
            shape((256, 128), BF16),
            shape((256, 384), BF16),
            shape((384, 128), F32),
            shape((512, 128), BF16),
            shape((512, 128), BF16),
        ),
        [SCALAR] + [WHOLE] * 5,
        [pltpu.VMEM((4, 8, 8, 384), F32)],
        leaves=(0,),
    )(parity, own, y1, y2, proj_weight, cot)

    z1, z2 = both_ways(edge1, edge2, z_pairs)
    unit = shape((64, 112, 128), BF16)
    aspp_mine, aspp_theirs, grads = call(
        aspp_grad_kernel,
        (unit, unit, shape((256, 1152), BF16)),
        [SCALAR] * 2 + [WHOLE] * 7,
        [
            pltpu.VMEM((3, 256, 256), BF16),
            pltpu.VMEM((3, 512, 128), BF16),
            pltpu.VMEM((4, 8, 24, 128), F32),
            pltpu.VMEM((256, 768), BF16),
            pltpu.VMEM((768, 384), F32),
            pltpu.VMEM((20752, 128), F32),
            pltpu.VMEM((400, 128), F32),
        ],
    )(core, parity, hidden, h1, h2, joint, z1, z2, gproj)
    aspp_other = swap(aspp_theirs, core_pairs)
    own, sent1, sent2 = call(
        spread_kernel,
        (shape((4, 8, 8, 256), F32), shape((256, 256), BF16), shape((256, 256), BF16)),
        [SCALAR, WHOLE, WHOLE],
        [
            pltpu.VMEM((4, 8, 8, 256), F32),
            pltpu.VMEM((4, 8, 8, 256), F32),
            pltpu.VMEM((4, 8, 8, 256), F32),
        ],
    )(parity, grads, w_columns)
    y1, y2 = both_ways(sent1, sent2, y_pairs)
    aspp_part = (aspp_mine.astype(F32) + aspp_other.astype(F32)).astype(BF16)
    aspp_got = to_owners(aspp_part)

    grad_hidden = own.reshape(256, 256) + (y1.astype(F32) + y2.astype(F32))
    grad_pre = (grad_hidden * slope(pre)).astype(BF16)

    unit = shape((8, 8, 112, 128), BF16)
    block_mine, block_theirs = call(
        block_grad_kernel,
        (unit, unit),
        [SCALAR] + [WHOLE] * 2,
        [pltpu.VMEM((6928, 256), F32)],
    )(core, cols, grad_pre)
    block_other = swap(block_theirs, core_pairs)

    block_part = (block_mine.astype(F32) + block_other.astype(F32)).astype(BF16)
    block_got = to_owners(block_part.reshape(64, 112, 128))

    thin = thin_halo(grad_pre, z_even, y_even)
    share = jnp.sum(aspp_got.astype(F32), axis=0)
    third1 = swap(share[0:54], FORWARDS[0])
    third2 = swap(share[56:110], FORWARDS[1])
    place_of = lax.axis_index(ALL)
    owner = jnp.any(place_of == jnp.array(OWNERS, jnp.int32)).astype(jnp.int32).reshape(1)
    (grad_volume,) = call(
        volume_grad_kernel,
        (shape((256, 256), BF16),),
        [WHOLE] * 6,
        [pltpu.VMEM((4, 10, 24, 256), F32), pltpu.VMEM((256, 256), F32)],
        leaves=(0,),
    )(grad_pre, *thin, w)
    block_share, aspp_share = call(
        finish_kernel,
        (shape((108, 128), F32), shape((162, 128), F32)),
        [SCALAR] + [STORED] * 4,
        [
            pltpu.VMEM((64, 112, 128), BF16),
            pltpu.VMEM((112, 128), F32),
            pltpu.VMEM((54, 128), F32),
            pltpu.VMEM((54, 128), F32),
            pltpu.SemaphoreType.DMA((7,)),
        ],
        leaves=(0, 1),
    )(owner, block_got, share, third1, third2)
    proj_share = jnp.concatenate([share[54:56], share[110:111]]).reshape(384)
    return (
        out.reshape(4, 8, 8, 128),
        grad_volume.reshape(4, 8, 8, 256),
        block_share.reshape(13824),
        aspp_share.reshape(20736),
        proj_share,
    )


def solution(mesh):
    fine = Mesh(mesh.devices.reshape(4, 2, 2, 2, 4), ALL)
    cells = P(None, ("z", "yh", "c"), ("yl", "x"), None)
    flat = P(ALL)
    return jax.shard_map(
        step,
        mesh=fine,
        in_specs=(cells, P(), P(), P(), cells),
        out_specs=(cells, cells, flat, flat, flat),
        check_vma=False,
    )
```
